256 devices in a mesh: gx: 8 (over y, core), gy: 32 (over z, x).
Axes of the slice: x: 4, y: 4, z: 8, core: 2. Of those that a mesh axis runs over, the one named last changes fastest.
Arguments:
- field: float32 [32, 2048, 2048], P(None, 'gy', 'gx'), may hold values from -6 to 6
- row_scale: float32 [2048], replicated, may hold values from 0.5 to 2
- col_scale: float32 [2048], P('gx'), may hold values from 0.5 to 2
- row_rate: float32 [2048], replicated, may hold values from 0.2 to 1
- col_shift: float32 [2048], P('gx'), may hold values from -1 to 1
- col_mix: float32 [2048], P('gx'), may hold values from -1 to 1
Outputs:
- latent: float32 [2, 32, 2048, 2048], P(None, 'gy', None, 'gx')
- loglik: float32 [], replicated
The draws below stay inside these ranges and needn't reach their ends.
All inputs are finite; a program needn't handle non-finite values.
Results may differ from the reference program's by a relative error of at most 0.000075.
Values sent between devices are 32-bit elements; how exact they have to be, the bound alone decides.
A program may use at most 128 MiB of HBM per device.

```python
import math
import jax
import jax.numpy as jnp
import numpy as np

NX = 2048
NY = 2048
ZW = 32
N_GX = 8


def block_scale(own_key, dims, split, low, top_value):
    factor_of, own = 1.0, jax.random.fold_in(own_key, 6)
    for dim, parts in split:
        heights = jnp.exp(jax.random.uniform(jax.random.fold_in(own, dim), (parts,), jnp.float32, low / len(split), top_value / len(split)))
        factor_of = factor_of * jnp.repeat(heights, dims[dim] // parts).reshape([-1 if axis == dim else 1 for axis in range(len(dims))])
    return factor_of


def centred(rng, shape, scale, most, cuts=(), kind=jnp.bfloat16):
    drawn = scale * jax.random.normal(rng, shape, jnp.float32)
    if cuts:
        drawn = drawn * block_scale(rng, shape, cuts, -0.22, 0.18)
    return jnp.clip(drawn, -most, most).astype(kind)


def setup_inputs(seed: int = 0) -> dict:
    key_list = jax.random.split(jax.random.key(seed), 7)
    return {
        "field": centred(key_list[0], (ZW, NY, NX), 1.0, 6.0, ((1, 32), (2, 8)), jnp.float32),
        "row_scale": jnp.clip(jnp.exp(jax.random.uniform(key_list[1], (NY,), jnp.float32, math.log(0.5), math.log(2.0))), 0.5, 2.0),
        "col_scale": jnp.clip(jnp.exp(math.log(2.0) - 1.3862944 * jax.random.uniform(key_list[2], (NX,), jnp.float32) ** block_scale(key_list[2], (NX,), ((0, 8),), -0.2, 0.2)), 0.5, 2.0),
        "row_rate": jnp.clip(jax.random.uniform(key_list[3], (NY,), jnp.float32, 0.2, 1.0), 0.2, 1.0),
        "col_shift": jnp.clip(jax.random.uniform(key_list[4], (NX,), jnp.float32, -1.0, 1.0) * block_scale(key_list[4], (NX,), ((0, 8),), -0.4, 0.0), -1.0, 1.0),
        "col_mix": jnp.clip(jax.random.uniform(key_list[5], (NX,), jnp.float32, -1.0, 1.0) * block_scale(key_list[5], (NX,), ((0, 8),), -0.4, 0.0), -1.0, 1.0),
    }


def column_order(total_cols, groups):
    levels = groups.bit_length() - 1
    width = total_cols // groups
    column = np.arange(total_cols)
    block = column // width
    flipped = block * 0
    for place in range(levels):
        flipped = flipped + (block >> place & 1) * (1 << levels - 1 - place)
    return flipped + groups * (column % width)

def reference(field, row_scale, col_scale, row_rate, col_shift, col_mix):
    spectrum = jnp.fft.fft(jnp.fft.fft(field, axis=2), axis=1)
    spectrum = spectrum[:, :, column_order(NX, N_GX)]
    norm_factor = 1.0 / math.sqrt(NX * NY)
    scale = row_scale[None, :, None] * col_scale[None, None, :]
    latent_u = jnp.real(spectrum) * norm_factor * scale
    latent_v = jnp.imag(spectrum) * norm_factor * scale
    log_scale = row_rate[None, :, None] * jnp.tanh(latent_u + col_shift[None, None, :])
    latent_w = latent_v * jnp.exp(log_scale) + col_mix[None, None, :] * latent_u
    terms = -0.5 * (latent_u * latent_u + latent_w * latent_w) - math.log(2.0 * math.pi) + log_scale + 2.0 * jnp.log(scale)
    loglik = jnp.sum(terms) / (ZW * NY * NX)
    return (jnp.stack([latent_u, latent_w]), loglik)
```

```python
import math

import jax
import jax.numpy as jnp
from jax import lax
from jax.sharding import PartitionSpec as P

precision_top = lax.Precision.HIGHEST


def reverse_bits(value, count):
    result = value * 0
    for place in range(count):
        result = result + (value >> place & 1) * (1 << count - 1 - place)
    return result


def root_table(row_index, freqs, length):
    phase = row_index[:, None] * freqs[None, :] % length
    angle = phase.astype(jnp.float32) * (-2.0 * math.pi / length)
    return (jnp.cos(angle), jnp.sin(angle))


def complex_einsum(form, real_part, imag_part, cos_part, sin_part):
    first = jnp.einsum(form, real_part, cos_part, precision=precision_top)
    second = jnp.einsum(form, real_part, sin_part, precision=precision_top)
    first = first - jnp.einsum(form, imag_part, sin_part, precision=precision_top)
    second = second + jnp.einsum(form, imag_part, cos_part, precision=precision_top)
    return (first, second)


def x_stage(rows, devices):
    count, length = rows.shape
    width = length // devices
    levels = devices.bit_length() - 1
    shaped = rows.reshape(count, devices, width)
    group = jnp.arange(devices, dtype=jnp.int32)
    residue = reverse_bits(group, levels)
    cos_8, sin_8 = root_table(group, residue, devices)
    part_real = jnp.einsum("ygn,gd->dyn", shaped, cos_8, precision=precision_top)
    part_imag = jnp.einsum("ygn,gd->dyn", shaped, sin_8, precision=precision_top)
    local_index = jnp.arange(width, dtype=jnp.int32)
    twist_cos, twist_sin = root_table(residue, local_index, length)
    twist_cos = twist_cos[:, None, :]
    twist_sin = twist_sin[:, None, :]
    turned_real = part_real * twist_cos - part_imag * twist_sin
    turned_imag = part_real * twist_sin + part_imag * twist_cos
    cos_w, sin_w = root_table(local_index, local_index, width)
    return complex_einsum("dyn,nk->dyk", turned_real, turned_imag, cos_w, sin_w)


def y_transform(real_part, imag_part):
    planes, length, width = real_part.shape
    outer = 1 << (length.bit_length() - 1) // 2
    inner = length // outer
    outer_index = jnp.arange(outer, dtype=jnp.int32)
    inner_index = jnp.arange(inner, dtype=jnp.int32)
    cos_one, sin_one = root_table(outer_index, outer_index, outer)
    cos_two, sin_two = root_table(inner_index, inner_index, inner)
    cos_mid, sin_mid = root_table(outer_index, inner_index, length)
    shaped_real = real_part.reshape(planes, outer, inner, width)
    shaped_imag = imag_part.reshape(planes, outer, inner, width)
    step_real, step_imag = complex_einsum(
        "zabc,ak->zkbc", shaped_real, shaped_imag, cos_one, sin_one
    )
    twist_cos = cos_mid[None, :, :, None]
    twist_sin = sin_mid[None, :, :, None]
    turned_real = step_real * twist_cos - step_imag * twist_sin
    turned_imag = step_real * twist_sin + step_imag * twist_cos
    final_real, final_imag = complex_einsum(
        "zkbc,bj->zjkc", turned_real, turned_imag, cos_two, sin_two
    )
    return (final_real.reshape(planes, length, width), final_imag.reshape(planes, length, width))


def per_device(field, row_scale, col_scale, row_rate, col_shift, col_mix):
    devices = lax.axis_size("gx")
    plane = lax.all_to_all(field, "gy", split_axis=0, concat_axis=1, tiled=True)
    plane = plane[0]
    rows = lax.all_to_all(plane, "gx", split_axis=0, concat_axis=1, tiled=True)
    spec_real, spec_imag = x_stage(rows, devices)
    both = jnp.stack([spec_real, spec_imag])
    both = lax.all_to_all(both, "gx", split_axis=1, concat_axis=2, tiled=True)
    spec_real, spec_imag = y_transform(both[0], both[1])
    length = spec_real.shape[1]
    total_cols = spec_real.shape[2] * devices
    norm_factor = 1.0 / math.sqrt(length * total_cols)
    scale = row_scale[None, :, None] * col_scale[None, None, :]
    latent_u = spec_real * norm_factor * scale
    latent_v = spec_imag * norm_factor * scale
    log_scale = row_rate[None, :, None] * jnp.tanh(latent_u + col_shift[None, None, :])
    latent_w = latent_v * jnp.exp(log_scale) + col_mix[None, None, :] * latent_u
    terms = (
        -0.5 * (latent_u * latent_u + latent_w * latent_w)
        - math.log(2.0 * math.pi)
        + log_scale
        + 2.0 * jnp.log(scale)
    )
    total_sum = lax.psum(jnp.sum(terms), ("gx", "gy"))
    mode_count = spec_real.size * devices * lax.axis_size("gy")
    loglik = total_sum / mode_count
    return (jnp.stack([latent_u, latent_w]), loglik)


def solution(mesh):
    return jax.shard_map(
        per_device,
        mesh=mesh,
        in_specs=(P(None, "gy", "gx"), P(), P("gx"), P(), P("gx"), P("gx")),
        out_specs=(P(None, "gy", None, "gx"), P()),
        check_vma=False,
    )
```

```python
import math

import jax
import jax.numpy as jnp
from jax import lax
from jax.experimental import pallas as pl
from jax.experimental.pallas import tpu as pltpu
from jax.sharding import PartitionSpec as P

precision_top = lax.Precision.HIGHEST


def reverse_bits(value, count):
    result = value * 0
    for place in range(count):
        result = result + (value >> place & 1) * (1 << count - 1 - place)
    return result


def root_table(row_index, freqs, length):
    phase = row_index[:, None] * freqs[None, :] % length
    angle = phase.astype(jnp.float32) * (-2.0 * math.pi / length)
    return (jnp.cos(angle), jnp.sin(angle))


def complex_einsum(form, real_part, imag_part, cos_part, sin_part):
    first = jnp.einsum(form, real_part, cos_part, precision=precision_top)
    second = jnp.einsum(form, real_part, sin_part, precision=precision_top)
    first = first - jnp.einsum(form, imag_part, sin_part, precision=precision_top)
    second = second + jnp.einsum(form, imag_part, cos_part, precision=precision_top)
    return (first, second)


def x_stage(rows, devices):
    count, length = rows.shape
    width = length // devices
    levels = devices.bit_length() - 1
    shaped = rows.reshape(count, devices, width)
    group = jnp.arange(devices, dtype=jnp.int32)
    residue = reverse_bits(group, levels)
    cos_8, sin_8 = root_table(group, residue, devices)
    part_real = jnp.einsum("ygn,gd->dyn", shaped, cos_8, precision=precision_top)
    part_imag = jnp.einsum("ygn,gd->dyn", shaped, sin_8, precision=precision_top)
    local_index = jnp.arange(width, dtype=jnp.int32)
    twist_cos, twist_sin = root_table(residue, local_index, length)
    twist_cos = twist_cos[:, None, :]
    twist_sin = twist_sin[:, None, :]
    turned_real = part_real * twist_cos - part_imag * twist_sin
    turned_imag = part_real * twist_sin + part_imag * twist_cos
    cos_w, sin_w = root_table(local_index, local_index, width)
    return complex_einsum("dyn,nk->dyk", turned_real, turned_imag, cos_w, sin_w)


def y_transform(real_part, imag_part):
    planes, length, width = real_part.shape
    outer = 1 << (length.bit_length() - 1) // 2
    inner = length // outer
    outer_index = jnp.arange(outer, dtype=jnp.int32)
    inner_index = jnp.arange(inner, dtype=jnp.int32)
    cos_one, sin_one = root_table(outer_index, outer_index, outer)
    cos_two, sin_two = root_table(inner_index, inner_index, inner)
    cos_mid, sin_mid = root_table(outer_index, inner_index, length)
    shaped_real = real_part.reshape(planes, outer, inner, width)
    shaped_imag = imag_part.reshape(planes, outer, inner, width)
    step_real, step_imag = complex_einsum(
        "zabc,ak->zkbc", shaped_real, shaped_imag, cos_one, sin_one
    )
    twist_cos = cos_mid[None, :, :, None]
    twist_sin = sin_mid[None, :, :, None]
    turned_real = step_real * twist_cos - step_imag * twist_sin
    turned_imag = step_real * twist_sin + step_imag * twist_cos
    final_real, final_imag = complex_einsum(
        "zkbc,bj->zjkc", turned_real, turned_imag, cos_two, sin_two
    )
    return (final_real.reshape(planes, length, width), final_imag.reshape(planes, length, width))


MESH_IDS = pl.DeviceIdType.MESH


def total_kernel(value_ref, out_ref, slots_a, slots_b, send_a, recv_a, send_b, recv_b):
    count_x = lax.axis_size("gx")
    count_y = lax.axis_size("gy")
    me_x = lax.axis_index("gx")
    me_y = lax.axis_index("gy")
    barrier = pltpu.get_barrier_semaphore()
    for step in range(1, count_x):
        pl.semaphore_signal(
            barrier, inc=1, device_id=((me_x + step) % count_x, me_y), device_id_type=MESH_IDS
        )
    for step in range(1, count_y):
        pl.semaphore_signal(
            barrier, inc=1, device_id=(me_x, (me_y + step) % count_y), device_id_type=MESH_IDS
        )
    slots_a[0] = value_ref[...]
    pl.semaphore_wait(barrier, count_x - 1 + count_y - 1)
    sends = []
    for step in range(1, count_x):
        copy = pltpu.make_async_remote_copy(
            src_ref=value_ref,
            dst_ref=slots_a.at[step],
            send_sem=send_a.at[step],
            recv_sem=recv_a.at[step],
            device_id=((me_x + step) % count_x, me_y),
            device_id_type=MESH_IDS,
        )
        copy.start()
        sends.append(copy)
    for copy in sends:
        copy.wait_recv()
    group_sum = slots_a[(me_x - 0) % count_x]
    for source in range(1, count_x):
        group_sum = group_sum + slots_a[(me_x - source + count_x) % count_x]
    slots_b[0] = group_sum
    later = []
    for step in range(1, count_y):
        copy = pltpu.make_async_remote_copy(
            src_ref=slots_b.at[0],
            dst_ref=slots_b.at[step],
            send_sem=send_b.at[step],
            recv_sem=recv_b.at[step],
            device_id=(me_x, (me_y + step) % count_y),
            device_id_type=MESH_IDS,
        )
        copy.start()
        later.append(copy)
    for copy in later:
        copy.wait_recv()
    grand = slots_b[(me_y - 0) % count_y]
    for source in range(1, count_y):
        grand = grand + slots_b[(me_y - source + count_y) % count_y]
    out_ref[...] = grand
    for copy in sends:
        copy.wait_send()
    for copy in later:
        copy.wait_send()


def total_everywhere(value):
    count_x = lax.axis_size("gx")
    count_y = lax.axis_size("gy")
    tile = jnp.broadcast_to(value, (8, 128)).astype(jnp.float32)
    result = pl.pallas_call(
        total_kernel,
        out_shape=jax.ShapeDtypeStruct((8, 128), jnp.float32),
        in_specs=[pl.BlockSpec(memory_space=pltpu.VMEM)],
        out_specs=pl.BlockSpec(memory_space=pltpu.VMEM),
        scratch_shapes=[
            pltpu.VMEM((count_x, 8, 128), jnp.float32),
            pltpu.VMEM((count_y, 8, 128), jnp.float32),
            pltpu.SemaphoreType.DMA((count_x,)),
            pltpu.SemaphoreType.DMA((count_x,)),
            pltpu.SemaphoreType.DMA((count_y,)),
            pltpu.SemaphoreType.DMA((count_y,)),
        ],
        compiler_params=pltpu.CompilerParams(collective_id=0, has_side_effects=True),
    )(tile)
    return result[0, 0]


def per_device(field, row_scale, col_scale, row_rate, col_shift, col_mix):
    devices = lax.axis_size("gx")
    plane = lax.all_to_all(field, "gy", split_axis=0, concat_axis=1, tiled=True)
    plane = plane[0]
    rows = lax.all_to_all(plane, "gx", split_axis=0, concat_axis=1, tiled=True)
    spec_real, spec_imag = x_stage(rows, devices)
    both = jnp.stack([spec_real, spec_imag])
    both = lax.all_to_all(both, "gx", split_axis=1, concat_axis=2, tiled=True)
    spec_real, spec_imag = y_transform(both[0], both[1])
    length = spec_real.shape[1]
    total_cols = spec_real.shape[2] * devices
    norm_factor = 1.0 / math.sqrt(length * total_cols)
    scale = row_scale[None, :, None] * col_scale[None, None, :]
    latent_u = spec_real * norm_factor * scale
    latent_v = spec_imag * norm_factor * scale
    log_scale = row_rate[None, :, None] * jnp.tanh(latent_u + col_shift[None, None, :])
    latent_w = latent_v * jnp.exp(log_scale) + col_mix[None, None, :] * latent_u
    terms = (
        -0.5 * (latent_u * latent_u + latent_w * latent_w)
        - math.log(2.0 * math.pi)
        + log_scale
        + 2.0 * jnp.log(scale)
    )
    total_sum = total_everywhere(jnp.sum(terms))
    mode_count = spec_real.size * devices * lax.axis_size("gy")
    loglik = total_sum / mode_count
    return (jnp.stack([latent_u, latent_w]), loglik)


def solution(mesh):
    return jax.shard_map(
        per_device,
        mesh=mesh,
        in_specs=(P(None, "gy", "gx"), P(), P("gx"), P(), P("gx"), P("gx")),
        out_specs=(P(None, "gy", None, "gx"), P()),
        check_vma=False,
    )
```

```python
import math

import jax
import jax.numpy as jnp
from jax import lax
from jax.experimental import pallas as pl
from jax.experimental.pallas import tpu as pltpu
from jax.sharding import PartitionSpec as P

precision_top = lax.Precision.HIGHEST


def reverse_bits(value, count):
    result = value * 0
    for place in range(count):
        result = result + (value >> place & 1) * (1 << count - 1 - place)
    return result


def root_table(row_index, freqs, length):
    phase = row_index[:, None] * freqs[None, :] % length
    angle = phase.astype(jnp.float32) * (-2.0 * math.pi / length)
    return (jnp.cos(angle), jnp.sin(angle))


def complex_einsum(form, real_part, imag_part, cos_part, sin_part):
    first = jnp.einsum(form, real_part, cos_part, precision=precision_top)
    second = jnp.einsum(form, real_part, sin_part, precision=precision_top)
    first = first - jnp.einsum(form, imag_part, sin_part, precision=precision_top)
    second = second + jnp.einsum(form, imag_part, cos_part, precision=precision_top)
    return (first, second)


def x_stage(rows, devices):
    count, length = rows.shape
    width = length // devices
    levels = devices.bit_length() - 1
    shaped = rows.reshape(count, devices, width)
    group = jnp.arange(devices, dtype=jnp.int32)
    residue = reverse_bits(group, levels)
    cos_8, sin_8 = root_table(group, residue, devices)
    part_real = jnp.einsum("ygn,gd->dyn", shaped, cos_8, precision=precision_top)
    part_imag = jnp.einsum("ygn,gd->dyn", shaped, sin_8, precision=precision_top)
    local_index = jnp.arange(width, dtype=jnp.int32)
    twist_cos, twist_sin = root_table(residue, local_index, length)
    twist_cos = twist_cos[:, None, :]
    twist_sin = twist_sin[:, None, :]
    turned_real = part_real * twist_cos - part_imag * twist_sin
    turned_imag = part_real * twist_sin + part_imag * twist_cos
    cos_w, sin_w = root_table(local_index, local_index, width)
    return complex_einsum("dyn,nk->dyk", turned_real, turned_imag, cos_w, sin_w)


def y_transform(real_part, imag_part):
    chunks, outer, rows, width = real_part.shape
    inner = chunks * rows
    length = outer * inner
    outer_index = jnp.arange(outer, dtype=jnp.int32)
    inner_index = jnp.arange(inner, dtype=jnp.int32)
    cos_one, sin_one = root_table(outer_index, outer_index, outer)
    cos_two, sin_two = root_table(inner_index, inner_index, inner)
    cos_mid, sin_mid = root_table(outer_index, inner_index, length)
    step_real, step_imag = complex_einsum(
        "cabw,ak->kcbw", real_part, imag_part, cos_one, sin_one
    )
    twist_cos = cos_mid.reshape(outer, chunks, rows, 1)
    twist_sin = sin_mid.reshape(outer, chunks, rows, 1)
    turned_real = step_real * twist_cos - step_imag * twist_sin
    turned_imag = step_real * twist_sin + step_imag * twist_cos
    final_real, final_imag = complex_einsum(
        "kcbw,cbj->jkw",
        turned_real,
        turned_imag,
        cos_two.reshape(chunks, rows, inner),
        sin_two.reshape(chunks, rows, inner),
    )
    return (final_real.reshape(1, length, width), final_imag.reshape(1, length, width))


MESH_IDS = pl.DeviceIdType.MESH


def total_kernel(value_ref, out_ref, slots_a, slots_b, send_a, recv_a, send_b, recv_b):
    count_x = lax.axis_size("gx")
    count_y = lax.axis_size("gy")
    me_x = lax.axis_index("gx")
    me_y = lax.axis_index("gy")
    barrier = pltpu.get_barrier_semaphore()
    for step in range(1, count_x):
        pl.semaphore_signal(
            barrier, inc=1, device_id=((me_x + step) % count_x, me_y), device_id_type=MESH_IDS
        )
    for step in range(1, count_y):
        pl.semaphore_signal(
            barrier, inc=1, device_id=(me_x, (me_y + step) % count_y), device_id_type=MESH_IDS
        )
    slots_a[0] = value_ref[...]
    pl.semaphore_wait(barrier, count_x - 1 + count_y - 1)
    sends = []
    for step in range(1, count_x):
        copy = pltpu.make_async_remote_copy(
            src_ref=value_ref,
            dst_ref=slots_a.at[step],
            send_sem=send_a.at[step],
            recv_sem=recv_a.at[step],
            device_id=((me_x + step) % count_x, me_y),
            device_id_type=MESH_IDS,
        )
        copy.start()
        sends.append(copy)
    for copy in sends:
        copy.wait_recv()
    group_sum = slots_a[(me_x - 0) % count_x]
    for source in range(1, count_x):
        group_sum = group_sum + slots_a[(me_x - source + count_x) % count_x]
    slots_b[0] = group_sum
    later = []
    for step in range(1, count_y):
        copy = pltpu.make_async_remote_copy(
            src_ref=slots_b.at[0],
            dst_ref=slots_b.at[step],
            send_sem=send_b.at[step],
            recv_sem=recv_b.at[step],
            device_id=(me_x, (me_y + step) % count_y),
            device_id_type=MESH_IDS,
        )
        copy.start()
        later.append(copy)
    for copy in later:
        copy.wait_recv()
    grand = slots_b[(me_y - 0) % count_y]
    for source in range(1, count_y):
        grand = grand + slots_b[(me_y - source + count_y) % count_y]
    out_ref[...] = grand
    for copy in sends:
        copy.wait_send()
    for copy in later:
        copy.wait_send()


def total_everywhere(value):
    count_x = lax.axis_size("gx")
    count_y = lax.axis_size("gy")
    tile = jnp.broadcast_to(value, (8, 128)).astype(jnp.float32)
    result = pl.pallas_call(
        total_kernel,
        out_shape=jax.ShapeDtypeStruct((8, 128), jnp.float32),
        in_specs=[pl.BlockSpec(memory_space=pltpu.VMEM)],
        out_specs=pl.BlockSpec(memory_space=pltpu.VMEM),
        scratch_shapes=[
            pltpu.VMEM((count_x, 8, 128), jnp.float32),
            pltpu.VMEM((count_y, 8, 128), jnp.float32),
            pltpu.SemaphoreType.DMA((count_x,)),
            pltpu.SemaphoreType.DMA((count_x,)),
            pltpu.SemaphoreType.DMA((count_y,)),
            pltpu.SemaphoreType.DMA((count_y,)),
        ],
        compiler_params=pltpu.CompilerParams(collective_id=0, has_side_effects=True),
    )(tile)
    return result[0, 0]


def per_device(field, row_scale, col_scale, row_rate, col_shift, col_mix):
    devices = lax.axis_size("gx")
    chunks = 4
    rows = field.shape[1] // chunks
    pieces = []
    for chunk in range(chunks):
        part = field[:, chunk * rows:(chunk + 1) * rows, :]
        plane = lax.all_to_all(part, "gy", split_axis=0, concat_axis=1, tiled=True)[0]
        block = lax.all_to_all(plane, "gx", split_axis=0, concat_axis=1, tiled=True)
        spec_real, spec_imag = x_stage(block, devices)
        both = jnp.stack([spec_real, spec_imag])
        both = lax.all_to_all(both, "gx", split_axis=1, concat_axis=2, tiled=True)
        pieces.append(both.reshape(2, plane.shape[0] // rows, rows, -1))
    gathered = jnp.stack(pieces, axis=1)
    spec_real, spec_imag = y_transform(gathered[0], gathered[1])
    length = spec_real.shape[1]
    total_cols = spec_real.shape[2] * devices
    norm_factor = 1.0 / math.sqrt(length * total_cols)
    scale = row_scale[None, :, None] * col_scale[None, None, :]
    latent_u = spec_real * norm_factor * scale
    latent_v = spec_imag * norm_factor * scale
    log_scale = row_rate[None, :, None] * jnp.tanh(latent_u + col_shift[None, None, :])
    latent_w = latent_v * jnp.exp(log_scale) + col_mix[None, None, :] * latent_u
    terms = (
        -0.5 * (latent_u * latent_u + latent_w * latent_w)
        - math.log(2.0 * math.pi)
        + log_scale
        + 2.0 * jnp.log(scale)
    )
    total_sum = total_everywhere(jnp.sum(terms))
    mode_count = spec_real.size * devices * lax.axis_size("gy")
    loglik = total_sum / mode_count
    return (jnp.stack([latent_u, latent_w]), loglik)


def solution(mesh):
    return jax.shard_map(
        per_device,
        mesh=mesh,
        in_specs=(P(None, "gy", "gx"), P(), P("gx"), P(), P("gx"), P("gx")),
        out_specs=(P(None, "gy", None, "gx"), P()),
        check_vma=False,
    )
```

```python
import functools
import math

import jax
import jax.numpy as jnp
from jax import lax
from jax.experimental import pallas as pl
from jax.experimental.pallas import tpu as pltpu
from jax.sharding import PartitionSpec as P

precision_top = lax.Precision.HIGHEST


def reverse_bits(value, count):
    result = value * 0
    for place in range(count):
        result = result + (value >> place & 1) * (1 << count - 1 - place)
    return result


def root_table(row_index, freqs, length):
    phase = row_index[:, None] * freqs[None, :] % length
    angle = phase.astype(jnp.float32) * (-2.0 * math.pi / length)
    return (jnp.cos(angle), jnp.sin(angle))


def complex_einsum(form, real_part, imag_part, cos_part, sin_part):
    first = jnp.einsum(form, real_part, cos_part, precision=precision_top)
    second = jnp.einsum(form, real_part, sin_part, precision=precision_top)
    first = first - jnp.einsum(form, imag_part, sin_part, precision=precision_top)
    second = second + jnp.einsum(form, imag_part, cos_part, precision=precision_top)
    return (first, second)


def x_stage(rows, devices):
    count, length = rows.shape
    width = length // devices
    levels = devices.bit_length() - 1
    shaped = rows.reshape(count, devices, width)
    group = jnp.arange(devices, dtype=jnp.int32)
    residue = reverse_bits(group, levels)
    cos_8, sin_8 = root_table(group, residue, devices)
    part_real = jnp.einsum("ygn,gd->dyn", shaped, cos_8, precision=precision_top)
    part_imag = jnp.einsum("ygn,gd->dyn", shaped, sin_8, precision=precision_top)
    local_index = jnp.arange(width, dtype=jnp.int32)
    twist_cos, twist_sin = root_table(residue, local_index, length)
    twist_cos = twist_cos[:, None, :]
    twist_sin = twist_sin[:, None, :]
    turned_real = part_real * twist_cos - part_imag * twist_sin
    turned_imag = part_real * twist_sin + part_imag * twist_cos
    cos_w, sin_w = root_table(local_index, local_index, width)
    return complex_einsum("dyn,nk->dyk", turned_real, turned_imag, cos_w, sin_w)


def y_transform(real_part, imag_part):
    planes, length, width = real_part.shape
    outer = 1 << (length.bit_length() - 1) // 2
    inner = length // outer
    outer_index = jnp.arange(outer, dtype=jnp.int32)
    inner_index = jnp.arange(inner, dtype=jnp.int32)
    cos_one, sin_one = root_table(outer_index, outer_index, outer)
    cos_two, sin_two = root_table(inner_index, inner_index, inner)
    cos_mid, sin_mid = root_table(outer_index, inner_index, length)
    shaped_real = real_part.reshape(planes, outer, inner, width)
    shaped_imag = imag_part.reshape(planes, outer, inner, width)
    step_real, step_imag = complex_einsum(
        "zabc,ak->zkbc", shaped_real, shaped_imag, cos_one, sin_one
    )
    twist_cos = cos_mid[None, :, :, None]
    twist_sin = sin_mid[None, :, :, None]
    turned_real = step_real * twist_cos - step_imag * twist_sin
    turned_imag = step_real * twist_sin + step_imag * twist_cos
    final_real, final_imag = complex_einsum(
        "zkbc,bj->zjkc", turned_real, turned_imag, cos_two, sin_two
    )
    return (final_real.reshape(planes, length, width), final_imag.reshape(planes, length, width))


def y_kernel(norm_factor, cos_a_ref, sin_a_ref, twist_cos_ref, twist_sin_ref,
             cos_b_ref, sin_b_ref, row_scale_ref, row_rate_ref, col_scale_ref, col_shift_ref,
             col_mix_ref, real_hbm, imag_hbm, out_hbm, sum_ref,
             held, step_real, step_imag, staged, in_sems, out_sems):
    size_a, size_b, width = real_hbm.shape
    half = width // 2
    loads = []
    for part, source in enumerate((real_hbm, imag_hbm)):
        for index in range(size_b):
            copy = pltpu.make_async_copy(
                source.at[:, index, :], held.at[part, index], in_sems.at[part, index]
            )
            copy.start()
            loads.append(copy)

    def dot(left, right):
        return jnp.dot(left, right, precision=precision_top, preferred_element_type=jnp.float32)

    cos_a = cos_a_ref[...]
    sin_a = sin_a_ref[...]
    for index in range(size_b):
        loads[index].wait()
        loads[size_b + index].wait()
        part_real = held[0, index]
        part_imag = held[1, index]
        out_real = dot(cos_a, part_real) - dot(sin_a, part_imag)
        out_imag = dot(cos_a, part_imag) + dot(sin_a, part_real)
        rows = pl.ds(index * size_a, size_a)
        twist_cos = twist_cos_ref[rows, :]
        twist_sin = twist_sin_ref[rows, :]
        turned_real = out_real * twist_cos - out_imag * twist_sin
        turned_imag = out_real * twist_sin + out_imag * twist_cos
        for side in range(2):
            lanes = slice(side * half, (side + 1) * half)
            step_real[side, rows, :] = turned_real[:, lanes]
            step_imag[side, rows, :] = turned_imag[:, lanes]

    col_scale = col_scale_ref[...]
    col_shift = col_shift_ref[...]
    col_mix = col_mix_ref[...]
    cos_b = cos_b_ref[...]
    sin_b = sin_b_ref[...]

    def second(index, total):
        picked = pl.ds(index, size_b, stride=size_a)
        part_real = jnp.concatenate([step_real[0, picked, :], step_real[1, picked, :]], axis=1)
        part_imag = jnp.concatenate([step_imag[0, picked, :], step_imag[1, picked, :]], axis=1)
        spec_real = dot(cos_b, part_real) - dot(sin_b, part_imag)
        spec_imag = dot(cos_b, part_imag) + dot(sin_b, part_real)
        rows = pl.ds(pl.multiple_of(index * size_b, size_b), size_b)
        scale = row_scale_ref[rows, :] * col_scale
        latent_u = spec_real * norm_factor * scale
        latent_v = spec_imag * norm_factor * scale
        log_scale = row_rate_ref[rows, :] * jnp.tanh(latent_u + col_shift)
        latent_w = latent_v * jnp.exp(log_scale) + col_mix * latent_u
        terms = (
            -0.5 * (latent_u * latent_u + latent_w * latent_w)
            - math.log(2.0 * math.pi)
            + log_scale
            + 2.0 * jnp.log(scale)
        )
        staged[0, index] = latent_u
        staged[1, index] = latent_w
        for part in range(2):
            pltpu.make_async_copy(
                staged.at[part, index], out_hbm.at[part, :, index, :], out_sems.at[part, index]
            ).start()
        return total + terms

    total = lax.fori_loop(0, size_a, second, jnp.zeros((size_b, width), jnp.float32))
    sum_ref[...] = jnp.broadcast_to(jnp.sum(total), sum_ref.shape)

    def finish(index, carry):
        for part in range(2):
            pltpu.make_async_copy(
                staged.at[part, index], out_hbm.at[part, :, index, :], out_sems.at[part, index]
            ).wait()
        return carry

    lax.fori_loop(0, size_a, finish, 0)


def y_stage(real_part, imag_part, row_scale, col_scale, row_rate, col_shift, col_mix, norm_factor):
    length, width = real_part.shape
    size_b = 1 << (length.bit_length() - 1) // 2
    size_a = length // size_b
    index_a = jnp.arange(size_a, dtype=jnp.int32)
    index_b = jnp.arange(size_b, dtype=jnp.int32)
    cos_a, sin_a = root_table(index_a, index_a, size_a)
    cos_b, sin_b = root_table(index_b, index_b, size_b)
    twist_cos, twist_sin = root_table(index_b, index_a, length)
    twist_cos = twist_cos.reshape(length, 1)
    twist_sin = twist_sin.reshape(length, 1)
    row_scale_t = row_scale.reshape(size_b, size_a).T.reshape(length, 1)
    row_rate_t = row_rate.reshape(size_b, size_a).T.reshape(length, 1)
    vmem = pl.BlockSpec(memory_space=pltpu.VMEM)
    anywhere = pl.BlockSpec(memory_space=pl.ANY)
    latent, sums = pl.pallas_call(
        functools.partial(y_kernel, norm_factor),
        out_shape=(
            jax.ShapeDtypeStruct((2, size_b, size_a, width), jnp.float32),
            jax.ShapeDtypeStruct((8, 128), jnp.float32),
        ),
        in_specs=[vmem] * 11 + [anywhere] * 2,
        out_specs=(anywhere, vmem),
        scratch_shapes=[
            pltpu.VMEM((2, size_b, size_a, width), jnp.float32),
            pltpu.VMEM((2, length, width // 2), jnp.float32),
            pltpu.VMEM((2, length, width // 2), jnp.float32),
            pltpu.VMEM((2, size_a, size_b, width), jnp.float32),
            pltpu.SemaphoreType.DMA((2, size_b)),
            pltpu.SemaphoreType.DMA((2, size_a)),
        ],
        compiler_params=pltpu.CompilerParams(vmem_limit_bytes=60 * 1024 * 1024),
    )(
        cos_a, sin_a, twist_cos, twist_sin, cos_b, sin_b,
        row_scale_t, row_rate_t, col_scale.reshape(1, width), col_shift.reshape(1, width),
        col_mix.reshape(1, width),
        real_part.reshape(size_a, size_b, width), imag_part.reshape(size_a, size_b, width),
    )
    return latent.reshape(2, length, width), sums[0, 0]

MESH_IDS = pl.DeviceIdType.MESH


def total_kernel(value_ref, out_ref, slots_a, slots_b, send_a, recv_a, send_b, recv_b):
    count_x = lax.axis_size("gx")
    count_y = lax.axis_size("gy")
    me_x = lax.axis_index("gx")
    me_y = lax.axis_index("gy")
    barrier = pltpu.get_barrier_semaphore()
    for step in range(1, count_x):
        pl.semaphore_signal(
            barrier, inc=1, device_id=((me_x + step) % count_x, me_y), device_id_type=MESH_IDS
        )
    for step in range(1, count_y):
        pl.semaphore_signal(
            barrier, inc=1, device_id=(me_x, (me_y + step) % count_y), device_id_type=MESH_IDS
        )
    slots_a[0] = value_ref[...]
    pl.semaphore_wait(barrier, count_x - 1 + count_y - 1)
    sends = []
    for step in range(1, count_x):
        copy = pltpu.make_async_remote_copy(
            src_ref=value_ref,
            dst_ref=slots_a.at[step],
            send_sem=send_a.at[step],
            recv_sem=recv_a.at[step],
            device_id=((me_x + step) % count_x, me_y),
            device_id_type=MESH_IDS,
        )
        copy.start()
        sends.append(copy)
    for copy in sends:
        copy.wait_recv()
    group_sum = slots_a[(me_x - 0) % count_x]
    for source in range(1, count_x):
        group_sum = group_sum + slots_a[(me_x - source + count_x) % count_x]
    slots_b[0] = group_sum
    later = []
    for step in range(1, count_y):
        copy = pltpu.make_async_remote_copy(
            src_ref=slots_b.at[0],
            dst_ref=slots_b.at[step],
            send_sem=send_b.at[step],
            recv_sem=recv_b.at[step],
            device_id=(me_x, (me_y + step) % count_y),
            device_id_type=MESH_IDS,
        )
        copy.start()
        later.append(copy)
    for copy in later:
        copy.wait_recv()
    grand = slots_b[(me_y - 0) % count_y]
    for source in range(1, count_y):
        grand = grand + slots_b[(me_y - source + count_y) % count_y]
    out_ref[...] = grand
    for copy in sends:
        copy.wait_send()
    for copy in later:
        copy.wait_send()


def total_everywhere(value):
    count_x = lax.axis_size("gx")
    count_y = lax.axis_size("gy")
    tile = jnp.broadcast_to(value, (8, 128)).astype(jnp.float32)
    result = pl.pallas_call(
        total_kernel,
        out_shape=jax.ShapeDtypeStruct((8, 128), jnp.float32),
        in_specs=[pl.BlockSpec(memory_space=pltpu.VMEM)],
        out_specs=pl.BlockSpec(memory_space=pltpu.VMEM),
        scratch_shapes=[
            pltpu.VMEM((count_x, 8, 128), jnp.float32),
            pltpu.VMEM((count_y, 8, 128), jnp.float32),
            pltpu.SemaphoreType.DMA((count_x,)),
            pltpu.SemaphoreType.DMA((count_x,)),
            pltpu.SemaphoreType.DMA((count_y,)),
            pltpu.SemaphoreType.DMA((count_y,)),
        ],
        compiler_params=pltpu.CompilerParams(collective_id=0, has_side_effects=True),
    )(tile)
    return result[0, 0]


def per_device(field, row_scale, col_scale, row_rate, col_shift, col_mix):
    devices = lax.axis_size("gx")
    plane = lax.all_to_all(field, "gy", split_axis=0, concat_axis=1, tiled=True)
    plane = plane[0]
    rows = lax.all_to_all(plane, "gx", split_axis=0, concat_axis=1, tiled=True)
    spec_real, spec_imag = x_stage(rows, devices)
    both = jnp.stack([spec_real, spec_imag])
    both = lax.all_to_all(both, "gx", split_axis=1, concat_axis=2, tiled=True)
    length = both.shape[2]
    total_cols = both.shape[3] * devices
    norm_factor = 1.0 / math.sqrt(length * total_cols)
    latent, part_sum = y_stage(
        both[0, 0], both[1, 0], row_scale, col_scale, row_rate, col_shift, col_mix, norm_factor
    )
    total_sum = total_everywhere(part_sum)
    mode_count = length * total_cols * lax.axis_size("gy")
    loglik = total_sum / mode_count
    return (latent[:, None], loglik)


def solution(mesh):
    return jax.shard_map(
        per_device,
        mesh=mesh,
        in_specs=(P(None, "gy", "gx"), P(), P("gx"), P(), P("gx"), P("gx")),
        out_specs=(P(None, "gy", None, "gx"), P()),
        check_vma=False,
    )
```

```python
import functools
import math

import jax
import jax.numpy as jnp
from jax import lax
from jax.experimental import pallas as pl
from jax.experimental.pallas import tpu as pltpu
from jax.sharding import PartitionSpec as P

precision_top = lax.Precision.HIGHEST


def reverse_bits(value, count):
    result = value * 0
    for place in range(count):
        result = result + (value >> place & 1) * (1 << count - 1 - place)
    return result


def root_table(row_index, freqs, length):
    phase = row_index[:, None] * freqs[None, :] % length
    angle = phase.astype(jnp.float32) * (-2.0 * math.pi / length)
    return (jnp.cos(angle), jnp.sin(angle))


def complex_einsum(form, real_part, imag_part, cos_part, sin_part):
    first = jnp.einsum(form, real_part, cos_part, precision=precision_top)
    second = jnp.einsum(form, real_part, sin_part, precision=precision_top)
    first = first - jnp.einsum(form, imag_part, sin_part, precision=precision_top)
    second = second + jnp.einsum(form, imag_part, cos_part, precision=precision_top)
    return (first, second)


def x_stage(rows, devices):
    count, length = rows.shape
    width = length // devices
    levels = devices.bit_length() - 1
    shaped = rows.reshape(count, devices, width)
    group = jnp.arange(devices, dtype=jnp.int32)
    residue = reverse_bits(group, levels)
    cos_8, sin_8 = root_table(group, residue, devices)
    part_real = jnp.einsum("ygn,gd->dyn", shaped, cos_8, precision=precision_top)
    part_imag = jnp.einsum("ygn,gd->dyn", shaped, sin_8, precision=precision_top)
    local_index = jnp.arange(width, dtype=jnp.int32)
    twist_cos, twist_sin = root_table(residue, local_index, length)
    twist_cos = twist_cos[:, None, :]
    twist_sin = twist_sin[:, None, :]
    turned_real = part_real * twist_cos - part_imag * twist_sin
    turned_imag = part_real * twist_sin + part_imag * twist_cos
    cos_w, sin_w = root_table(local_index, local_index, width)
    return complex_einsum("dyn,nk->dyk", turned_real, turned_imag, cos_w, sin_w)


def y_transform(real_part, imag_part):
    planes, length, width = real_part.shape
    outer = 1 << (length.bit_length() - 1) // 2
    inner = length // outer
    outer_index = jnp.arange(outer, dtype=jnp.int32)
    inner_index = jnp.arange(inner, dtype=jnp.int32)
    cos_one, sin_one = root_table(outer_index, outer_index, outer)
    cos_two, sin_two = root_table(inner_index, inner_index, inner)
    cos_mid, sin_mid = root_table(outer_index, inner_index, length)
    shaped_real = real_part.reshape(planes, outer, inner, width)
    shaped_imag = imag_part.reshape(planes, outer, inner, width)
    step_real, step_imag = complex_einsum(
        "zabc,ak->zkbc", shaped_real, shaped_imag, cos_one, sin_one
    )
    twist_cos = cos_mid[None, :, :, None]
    twist_sin = sin_mid[None, :, :, None]
    turned_real = step_real * twist_cos - step_imag * twist_sin
    turned_imag = step_real * twist_sin + step_imag * twist_cos
    final_real, final_imag = complex_einsum(
        "zkbc,bj->zjkc", turned_real, turned_imag, cos_two, sin_two
    )
    return (final_real.reshape(planes, length, width), final_imag.reshape(planes, length, width))


def y_kernel(norm_factor, cos_a_ref, sin_a_ref, twist_cos_ref, twist_sin_ref,
             cos_b_ref, sin_b_ref, row_scale_ref, row_rate_ref, col_scale_ref, col_shift_ref,
             col_mix_ref, real_hbm, imag_hbm, out_hbm, sum_ref,
             held, step_real, step_imag, staged, in_sems, out_sems):
    high, low, blocks, rows, width = real_hbm.shape
    size_b = low * rows
    size_a = high * blocks
    half = width // 2
    loads = []
    for part, source in enumerate((real_hbm, imag_hbm)):
        for index in range(size_b):
            copy = pltpu.make_async_copy(
                source.at[:, index // rows, :, index % rows, :],
                held.at[part, index],
                in_sems.at[part, index],
            )
            copy.start()
            loads.append(copy)

    def dot(left, right):
        return jnp.dot(left, right, precision=precision_top, preferred_element_type=jnp.float32)

    cos_a = cos_a_ref[...]
    sin_a = sin_a_ref[...]
    for index in range(size_b):
        loads[index].wait()
        loads[size_b + index].wait()
        part_real = held[0, index].reshape(size_a, width)
        part_imag = held[1, index].reshape(size_a, width)
        out_real = dot(cos_a, part_real) - dot(sin_a, part_imag)
        out_imag = dot(cos_a, part_imag) + dot(sin_a, part_real)
        rows = pl.ds(index * size_a, size_a)
        twist_cos = twist_cos_ref[rows, :]
        twist_sin = twist_sin_ref[rows, :]
        turned_real = out_real * twist_cos - out_imag * twist_sin
        turned_imag = out_real * twist_sin + out_imag * twist_cos
        for side in range(2):
            lanes = slice(side * half, (side + 1) * half)
            step_real[side, rows, :] = turned_real[:, lanes]
            step_imag[side, rows, :] = turned_imag[:, lanes]

    col_scale = col_scale_ref[...]
    col_shift = col_shift_ref[...]
    col_mix = col_mix_ref[...]
    cos_b = cos_b_ref[...]
    sin_b = sin_b_ref[...]

    def second(index, total):
        picked = pl.ds(index, size_b, stride=size_a)
        part_real = jnp.concatenate([step_real[0, picked, :], step_real[1, picked, :]], axis=1)
        part_imag = jnp.concatenate([step_imag[0, picked, :], step_imag[1, picked, :]], axis=1)
        spec_real = dot(cos_b, part_real) - dot(sin_b, part_imag)
        spec_imag = dot(cos_b, part_imag) + dot(sin_b, part_real)
        rows = pl.ds(pl.multiple_of(index * size_b, size_b), size_b)
        scale = row_scale_ref[rows, :] * col_scale
        latent_u = spec_real * norm_factor * scale
        latent_v = spec_imag * norm_factor * scale
        log_scale = row_rate_ref[rows, :] * jnp.tanh(latent_u + col_shift)
        latent_w = latent_v * jnp.exp(log_scale) + col_mix * latent_u
        terms = (
            -0.5 * (latent_u * latent_u + latent_w * latent_w)
            - math.log(2.0 * math.pi)
            + log_scale
            + 2.0 * jnp.log(scale)
        )
        staged[0, index] = latent_u
        staged[1, index] = latent_w
        for part in range(2):
            pltpu.make_async_copy(
                staged.at[part, index], out_hbm.at[part, :, index, :], out_sems.at[part, index]
            ).start()
        return total + terms

    total = lax.fori_loop(0, size_a, second, jnp.zeros((size_b, width), jnp.float32))
    sum_ref[...] = jnp.broadcast_to(jnp.sum(total), sum_ref.shape)

    def finish(index, carry):
        for part in range(2):
            pltpu.make_async_copy(
                staged.at[part, index], out_hbm.at[part, :, index, :], out_sems.at[part, index]
            ).wait()
        return carry

    lax.fori_loop(0, size_a, finish, 0)


def y_stage(spectrum, row_scale, col_scale, row_rate, col_shift, col_mix, norm_factor, devices, height):
    _, length, width = spectrum.shape
    size_b = 1 << (length.bit_length() - 1) // 2
    size_a = length // size_b
    blocks = length // height
    rows = height // devices
    low = size_b // rows
    high = devices // low
    index_a = jnp.arange(size_a, dtype=jnp.int32)
    index_b = jnp.arange(size_b, dtype=jnp.int32)
    order_a = (index_a % blocks) * high + index_a // blocks
    cos_a, sin_a = root_table(index_a, order_a, size_a)
    cos_b, sin_b = root_table(index_b, index_b, size_b)
    twist_cos, twist_sin = root_table(index_b, index_a, length)
    twist_cos = twist_cos.reshape(length, 1)
    twist_sin = twist_sin.reshape(length, 1)
    row_scale_t = row_scale.reshape(size_b, size_a).T.reshape(length, 1)
    row_rate_t = row_rate.reshape(size_b, size_a).T.reshape(length, 1)
    vmem = pl.BlockSpec(memory_space=pltpu.VMEM)
    anywhere = pl.BlockSpec(memory_space=pl.ANY)
    shaped = spectrum.reshape(2, high, low, blocks, rows, width)
    latent, sums = pl.pallas_call(
        functools.partial(y_kernel, norm_factor),
        out_shape=(
            jax.ShapeDtypeStruct((2, size_b, size_a, width), jnp.float32),
            jax.ShapeDtypeStruct((8, 128), jnp.float32),
        ),
        in_specs=[vmem] * 11 + [anywhere] * 2,
        out_specs=(anywhere, vmem),
        scratch_shapes=[
            pltpu.VMEM((2, size_b, high, blocks, width), jnp.float32),
            pltpu.VMEM((2, length, width // 2), jnp.float32),
            pltpu.VMEM((2, length, width // 2), jnp.float32),
            pltpu.VMEM((2, size_a, size_b, width), jnp.float32),
            pltpu.SemaphoreType.DMA((2, size_b)),
            pltpu.SemaphoreType.DMA((2, size_a)),
        ],
        compiler_params=pltpu.CompilerParams(vmem_limit_bytes=60 * 1024 * 1024),
    )(
        cos_a, sin_a, twist_cos, twist_sin, cos_b, sin_b,
        row_scale_t, row_rate_t, col_scale.reshape(1, width), col_shift.reshape(1, width),
        col_mix.reshape(1, width), shaped[0], shaped[1],
    )
    return latent.reshape(2, length, width), sums[0, 0]

MESH_IDS = pl.DeviceIdType.MESH


def total_kernel(value_ref, out_ref, slots_a, slots_b, send_a, recv_a, send_b, recv_b):
    count_x = lax.axis_size("gx")
    count_y = lax.axis_size("gy")
    me_x = lax.axis_index("gx")
    me_y = lax.axis_index("gy")
    barrier = pltpu.get_barrier_semaphore()
    for step in range(1, count_x):
        pl.semaphore_signal(
            barrier, inc=1, device_id=((me_x + step) % count_x, me_y), device_id_type=MESH_IDS
        )
    for step in range(1, count_y):
        pl.semaphore_signal(
            barrier, inc=1, device_id=(me_x, (me_y + step) % count_y), device_id_type=MESH_IDS
        )
    slots_a[0] = value_ref[...]
    pl.semaphore_wait(barrier, count_x - 1 + count_y - 1)
    sends = []
    for step in range(1, count_x):
        copy = pltpu.make_async_remote_copy(
            src_ref=value_ref,
            dst_ref=slots_a.at[step],
            send_sem=send_a.at[step],
            recv_sem=recv_a.at[step],
            device_id=((me_x + step) % count_x, me_y),
            device_id_type=MESH_IDS,
        )
        copy.start()
        sends.append(copy)
    for copy in sends:
        copy.wait_recv()
    group_sum = slots_a[(me_x - 0) % count_x]
    for source in range(1, count_x):
        group_sum = group_sum + slots_a[(me_x - source + count_x) % count_x]
    slots_b[0] = group_sum
    later = []
    for step in range(1, count_y):
        copy = pltpu.make_async_remote_copy(
            src_ref=slots_b.at[0],
            dst_ref=slots_b.at[step],
            send_sem=send_b.at[step],
            recv_sem=recv_b.at[step],
            device_id=(me_x, (me_y + step) % count_y),
            device_id_type=MESH_IDS,
        )
        copy.start()
        later.append(copy)
    for copy in later:
        copy.wait_recv()
    grand = slots_b[(me_y - 0) % count_y]
    for source in range(1, count_y):
        grand = grand + slots_b[(me_y - source + count_y) % count_y]
    out_ref[...] = grand
    for copy in sends:
        copy.wait_send()
    for copy in later:
        copy.wait_send()


def total_everywhere(value):
    count_x = lax.axis_size("gx")
    count_y = lax.axis_size("gy")
    tile = jnp.broadcast_to(value, (8, 128)).astype(jnp.float32)
    result = pl.pallas_call(
        total_kernel,
        out_shape=jax.ShapeDtypeStruct((8, 128), jnp.float32),
        in_specs=[pl.BlockSpec(memory_space=pltpu.VMEM)],
        out_specs=pl.BlockSpec(memory_space=pltpu.VMEM),
        scratch_shapes=[
            pltpu.VMEM((count_x, 8, 128), jnp.float32),
            pltpu.VMEM((count_y, 8, 128), jnp.float32),
            pltpu.SemaphoreType.DMA((count_x,)),
            pltpu.SemaphoreType.DMA((count_x,)),
            pltpu.SemaphoreType.DMA((count_y,)),
            pltpu.SemaphoreType.DMA((count_y,)),
        ],
        compiler_params=pltpu.CompilerParams(collective_id=0, has_side_effects=True),
    )(tile)
    return result[0, 0]


def per_device(field, row_scale, col_scale, row_rate, col_shift, col_mix):
    devices = lax.axis_size("gx")
    planes, height, width = field.shape
    rows = height // devices
    outgoing = field.reshape(planes, devices, rows, width).transpose(1, 0, 2, 3)
    outgoing = outgoing.reshape(devices * planes, rows, width)
    incoming = lax.all_to_all(outgoing, ("gx", "gy"), split_axis=0, concat_axis=0, tiled=True)
    incoming = incoming.reshape(devices, planes, rows, width).transpose(1, 2, 0, 3)
    block = incoming.reshape(planes * rows, devices * width)
    spec_real, spec_imag = x_stage(block, devices)
    both = jnp.stack([spec_real, spec_imag])
    both = lax.all_to_all(both, "gx", split_axis=1, concat_axis=2, tiled=True)
    length = both.shape[2]
    total_cols = both.shape[3] * devices
    norm_factor = 1.0 / math.sqrt(length * total_cols)
    latent, part_sum = y_stage(
        both[:, 0], row_scale, col_scale, row_rate, col_shift, col_mix, norm_factor, devices, height
    )
    total_sum = total_everywhere(part_sum)
    mode_count = length * total_cols * lax.axis_size("gy")
    loglik = total_sum / mode_count
    return (latent[:, None], loglik)


def solution(mesh):
    return jax.shard_map(
        per_device,
        mesh=mesh,
        in_specs=(P(None, "gy", "gx"), P(), P("gx"), P(), P("gx"), P("gx")),
        out_specs=(P(None, "gy", None, "gx"), P()),
        check_vma=False,
    )
```

```python
import functools
import math

import jax
import jax.numpy as jnp
from jax import lax
from jax.experimental import pallas as pl
from jax.experimental.pallas import tpu as pltpu
from jax.sharding import PartitionSpec as P

precision_top = lax.Precision.HIGHEST


def reverse_bits(value, count):
    result = value * 0
    for place in range(count):
        result = result + (value >> place & 1) * (1 << count - 1 - place)
    return result


def root_table(row_index, freqs, length):
    phase = row_index[:, None] * freqs[None, :] % length
    angle = phase.astype(jnp.float32) * (-2.0 * math.pi / length)
    return (jnp.cos(angle), jnp.sin(angle))


def complex_einsum(form, real_part, imag_part, cos_part, sin_part):
    first = jnp.einsum(form, real_part, cos_part, precision=precision_top)
    second = jnp.einsum(form, real_part, sin_part, precision=precision_top)
    first = first - jnp.einsum(form, imag_part, sin_part, precision=precision_top)
    second = second + jnp.einsum(form, imag_part, cos_part, precision=precision_top)
    return (first, second)


def x_stage(rows, devices):
    count, length = rows.shape
    width = length // devices
    levels = devices.bit_length() - 1
    shaped = rows.reshape(count, devices, width)
    group = jnp.arange(devices, dtype=jnp.int32)
    residue = reverse_bits(group, levels)
    cos_8, sin_8 = root_table(group, residue, devices)
    part_real = jnp.einsum("ygn,gd->dyn", shaped, cos_8, precision=precision_top)
    part_imag = jnp.einsum("ygn,gd->dyn", shaped, sin_8, precision=precision_top)
    local_index = jnp.arange(width, dtype=jnp.int32)
    twist_cos, twist_sin = root_table(residue, local_index, length)
    twist_cos = twist_cos[:, None, :]
    twist_sin = twist_sin[:, None, :]
    turned_real = part_real * twist_cos - part_imag * twist_sin
    turned_imag = part_real * twist_sin + part_imag * twist_cos
    cos_w, sin_w = root_table(local_index, local_index, width)
    return complex_einsum("dyn,nk->dyk", turned_real, turned_imag, cos_w, sin_w)


def y_transform(real_part, imag_part):
    planes, length, width = real_part.shape
    outer = 1 << (length.bit_length() - 1) // 2
    inner = length // outer
    outer_index = jnp.arange(outer, dtype=jnp.int32)
    inner_index = jnp.arange(inner, dtype=jnp.int32)
    cos_one, sin_one = root_table(outer_index, outer_index, outer)
    cos_two, sin_two = root_table(inner_index, inner_index, inner)
    cos_mid, sin_mid = root_table(outer_index, inner_index, length)
    shaped_real = real_part.reshape(planes, outer, inner, width)
    shaped_imag = imag_part.reshape(planes, outer, inner, width)
    step_real, step_imag = complex_einsum(
        "zabc,ak->zkbc", shaped_real, shaped_imag, cos_one, sin_one
    )
    twist_cos = cos_mid[None, :, :, None]
    twist_sin = sin_mid[None, :, :, None]
    turned_real = step_real * twist_cos - step_imag * twist_sin
    turned_imag = step_real * twist_sin + step_imag * twist_cos
    final_real, final_imag = complex_einsum(
        "zkbc,bj->zjkc", turned_real, turned_imag, cos_two, sin_two
    )
    return (final_real.reshape(planes, length, width), final_imag.reshape(planes, length, width))


def y_kernel(norm_factor, cos_a_ref, sin_a_ref, twist_cos_ref, twist_sin_ref,
             cos_b_ref, sin_b_ref, row_scale_ref, row_rate_ref, col_scale_ref, col_shift_ref,
             col_mix_ref, spectrum_hbm, out_hbm, sum_ref,
             held, step_real, step_imag, staged, in_sems, out_sems):
    _, high, low, blocks, rows, width = spectrum_hbm.shape
    size_b = low * rows
    size_a = high * blocks
    half = width // 2
    loads = []
    for part in range(2):
        for index in range(size_b):
            copy = pltpu.make_async_copy(
                spectrum_hbm.at[part, :, index // rows, :, index % rows, :],
                held.at[part, index],
                in_sems.at[part, index],
            )
            copy.start()
            loads.append(copy)

    def dot(left, right):
        return jnp.dot(left, right, precision=precision_top, preferred_element_type=jnp.float32)

    both_a = jnp.concatenate([cos_a_ref[...], sin_a_ref[...]], axis=0)

    def first(index, carry):
        for part in range(2):
            pltpu.make_async_copy(
                spectrum_hbm.at[part, :, index // rows, :, index % rows, :],
                held.at[part, index],
                in_sems.at[part, index],
            ).wait()
        part_real = held[0, index].reshape(size_a, width)
        part_imag = held[1, index].reshape(size_a, width)
        from_real = dot(both_a, part_real)
        from_imag = dot(both_a, part_imag)
        out_real = from_real[:size_a] - from_imag[size_a:]
        out_imag = from_imag[:size_a] + from_real[size_a:]
        rows_here = pl.ds(pl.multiple_of(index * size_a, size_a), size_a)
        twist_cos = twist_cos_ref[rows_here, :]
        twist_sin = twist_sin_ref[rows_here, :]
        turned_real = out_real * twist_cos - out_imag * twist_sin
        turned_imag = out_real * twist_sin + out_imag * twist_cos
        for side in range(2):
            lanes = slice(side * half, (side + 1) * half)
            step_real[side, rows_here, :] = turned_real[:, lanes]
            step_imag[side, rows_here, :] = turned_imag[:, lanes]
        return carry

    lax.fori_loop(0, size_b, first, 0)

    col_scale = col_scale_ref[...]
    col_shift = col_shift_ref[...]
    col_mix = col_mix_ref[...]
    both_b = jnp.concatenate([cos_b_ref[...], sin_b_ref[...]], axis=0)

    def second(index, total):
        picked = pl.ds(index, size_b, stride=size_a)
        part_real = jnp.concatenate([step_real[0, picked, :], step_real[1, picked, :]], axis=1)
        part_imag = jnp.concatenate([step_imag[0, picked, :], step_imag[1, picked, :]], axis=1)
        from_real = dot(both_b, part_real)
        from_imag = dot(both_b, part_imag)
        spec_real = from_real[:size_b] - from_imag[size_b:]
        spec_imag = from_imag[:size_b] + from_real[size_b:]
        rows = pl.ds(pl.multiple_of(index * size_b, size_b), size_b)
        scale = row_scale_ref[rows, :] * col_scale
        latent_u = spec_real * norm_factor * scale
        latent_v = spec_imag * norm_factor * scale
        log_scale = row_rate_ref[rows, :] * jnp.tanh(latent_u + col_shift)
        latent_w = latent_v * jnp.exp(log_scale) + col_mix * latent_u
        terms = (
            -0.5 * (latent_u * latent_u + latent_w * latent_w)
            - math.log(2.0 * math.pi)
            + log_scale
            + 2.0 * jnp.log(scale)
        )
        staged[0, index] = latent_u
        staged[1, index] = latent_w
        for part in range(2):
            pltpu.make_async_copy(
                staged.at[part, index], out_hbm.at[part, :, index, :], out_sems.at[part, index]
            ).start()
        return total + terms

    total = lax.fori_loop(0, size_a, second, jnp.zeros((size_b, width), jnp.float32))
    sum_ref[...] = jnp.broadcast_to(jnp.sum(total), sum_ref.shape)

    def finish(index, carry):
        for part in range(2):
            pltpu.make_async_copy(
                staged.at[part, index], out_hbm.at[part, :, index, :], out_sems.at[part, index]
            ).wait()
        return carry

    lax.fori_loop(0, size_a, finish, 0)


def y_stage(spectrum, row_scale, col_scale, row_rate, col_shift, col_mix, norm_factor, devices, height):
    _, length, width = spectrum.shape
    size_b = 1 << (length.bit_length() - 1) // 2
    size_a = length // size_b
    blocks = length // height
    rows = height // devices
    low = size_b // rows
    high = devices // low
    index_a = jnp.arange(size_a, dtype=jnp.int32)
    index_b = jnp.arange(size_b, dtype=jnp.int32)
    order_a = (index_a % blocks) * high + index_a // blocks
    cos_a, sin_a = root_table(index_a, order_a, size_a)
    cos_b, sin_b = root_table(index_b, index_b, size_b)
    twist_cos, twist_sin = root_table(index_b, index_a, length)
    twist_cos = twist_cos.reshape(length, 1)
    twist_sin = twist_sin.reshape(length, 1)
    row_scale_t = row_scale.reshape(size_b, size_a).T.reshape(length, 1)
    row_rate_t = row_rate.reshape(size_b, size_a).T.reshape(length, 1)
    vmem = pl.BlockSpec(memory_space=pltpu.VMEM)
    anywhere = pl.BlockSpec(memory_space=pl.ANY)
    shaped = spectrum.reshape(2, high, low, blocks, rows, width)
    latent, sums = pl.pallas_call(
        functools.partial(y_kernel, norm_factor),
        out_shape=(
            jax.ShapeDtypeStruct((2, size_b, size_a, width), jnp.float32),
            jax.ShapeDtypeStruct((8, 128), jnp.float32),
        ),
        in_specs=[vmem] * 11 + [anywhere],
        out_specs=(anywhere, vmem),
        scratch_shapes=[
            pltpu.VMEM((2, size_b, high, blocks, width), jnp.float32),
            pltpu.VMEM((2, length, width // 2), jnp.float32),
            pltpu.VMEM((2, length, width // 2), jnp.float32),
            pltpu.VMEM((2, size_a, size_b, width), jnp.float32),
            pltpu.SemaphoreType.DMA((2, size_b)),
            pltpu.SemaphoreType.DMA((2, size_a)),
        ],
        compiler_params=pltpu.CompilerParams(vmem_limit_bytes=60 * 1024 * 1024),
    )(
        cos_a, sin_a, twist_cos, twist_sin, cos_b, sin_b,
        row_scale_t, row_rate_t, col_scale.reshape(1, width), col_shift.reshape(1, width),
        col_mix.reshape(1, width), shaped,
    )
    return latent.reshape(2, length, width), sums[0, 0]

MESH_IDS = pl.DeviceIdType.MESH


def total_kernel(value_ref, out_ref, slots_a, slots_b, send_a, recv_a, send_b, recv_b):
    count_x = lax.axis_size("gx")
    count_y = lax.axis_size("gy")
    me_x = lax.axis_index("gx")
    me_y = lax.axis_index("gy")
    barrier = pltpu.get_barrier_semaphore()
    for step in range(1, count_x):
        pl.semaphore_signal(
            barrier, inc=1, device_id=((me_x + step) % count_x, me_y), device_id_type=MESH_IDS
        )
    for step in range(1, count_y):
        pl.semaphore_signal(
            barrier, inc=1, device_id=(me_x, (me_y + step) % count_y), device_id_type=MESH_IDS
        )
    slots_a[0] = value_ref[...]
    pl.semaphore_wait(barrier, count_x - 1 + count_y - 1)
    sends = []
    for step in range(1, count_x):
        copy = pltpu.make_async_remote_copy(
            src_ref=value_ref,
            dst_ref=slots_a.at[step],
            send_sem=send_a.at[step],
            recv_sem=recv_a.at[step],
            device_id=((me_x + step) % count_x, me_y),
            device_id_type=MESH_IDS,
        )
        copy.start()
        sends.append(copy)
    for copy in sends:
        copy.wait_recv()
    group_sum = slots_a[(me_x - 0) % count_x]
    for source in range(1, count_x):
        group_sum = group_sum + slots_a[(me_x - source + count_x) % count_x]
    slots_b[0] = group_sum
    later = []
    for step in range(1, count_y):
        copy = pltpu.make_async_remote_copy(
            src_ref=slots_b.at[0],
            dst_ref=slots_b.at[step],
            send_sem=send_b.at[step],
            recv_sem=recv_b.at[step],
            device_id=(me_x, (me_y + step) % count_y),
            device_id_type=MESH_IDS,
        )
        copy.start()
        later.append(copy)
    for copy in later:
        copy.wait_recv()
    grand = slots_b[(me_y - 0) % count_y]
    for source in range(1, count_y):
        grand = grand + slots_b[(me_y - source + count_y) % count_y]
    out_ref[...] = grand
    for copy in sends:
        copy.wait_send()
    for copy in later:
        copy.wait_send()


def total_everywhere(value):
    count_x = lax.axis_size("gx")
    count_y = lax.axis_size("gy")
    tile = jnp.broadcast_to(value, (8, 128)).astype(jnp.float32)
    result = pl.pallas_call(
        total_kernel,
        out_shape=jax.ShapeDtypeStruct((8, 128), jnp.float32),
        in_specs=[pl.BlockSpec(memory_space=pltpu.VMEM)],
        out_specs=pl.BlockSpec(memory_space=pltpu.VMEM),
        scratch_shapes=[
            pltpu.VMEM((count_x, 8, 128), jnp.float32),
            pltpu.VMEM((count_y, 8, 128), jnp.float32),
            pltpu.SemaphoreType.DMA((count_x,)),
            pltpu.SemaphoreType.DMA((count_x,)),
            pltpu.SemaphoreType.DMA((count_y,)),
            pltpu.SemaphoreType.DMA((count_y,)),
        ],
        compiler_params=pltpu.CompilerParams(collective_id=0, has_side_effects=True),
    )(tile)
    return result[0, 0]


def per_device(field, row_scale, col_scale, row_rate, col_shift, col_mix):
    devices = lax.axis_size("gx")
    planes, height, width = field.shape
    rows = height // devices
    outgoing = field.reshape(planes, devices, rows, width).transpose(1, 0, 2, 3)
    outgoing = outgoing.reshape(devices * planes, rows, width)
    incoming = lax.all_to_all(outgoing, ("gx", "gy"), split_axis=0, concat_axis=0, tiled=True)
    incoming = incoming.reshape(devices, planes, rows, width).transpose(1, 2, 0, 3)
    block = incoming.reshape(planes * rows, devices * width)
    spec_real, spec_imag = x_stage(block, devices)
    both = jnp.stack([spec_real, spec_imag])
    both = lax.all_to_all(both, "gx", split_axis=1, concat_axis=2, tiled=True)
    length = both.shape[2]
    total_cols = both.shape[3] * devices
    norm_factor = 1.0 / math.sqrt(length * total_cols)
    latent, part_sum = y_stage(
        both[:, 0], row_scale, col_scale, row_rate, col_shift, col_mix, norm_factor, devices, height
    )
    total_sum = total_everywhere(part_sum)
    mode_count = length * total_cols * lax.axis_size("gy")
    loglik = total_sum / mode_count
    return (latent[:, None], loglik)


def solution(mesh):
    return jax.shard_map(
        per_device,
        mesh=mesh,
        in_specs=(P(None, "gy", "gx"), P(), P("gx"), P(), P("gx"), P("gx")),
        out_specs=(P(None, "gy", None, "gx"), P()),
        check_vma=False,
    )
```

```python
import functools
import math

import jax
import jax.numpy as jnp
from jax import lax
from jax.experimental import pallas as pl
from jax.experimental.pallas import tpu as pltpu
from jax.sharding import PartitionSpec as P

precision_top = lax.Precision.HIGHEST


def reverse_bits(value, count):
    result = value * 0
    for place in range(count):
        result = result + (value >> place & 1) * (1 << count - 1 - place)
    return result


def root_table(row_index, freqs, length):
    phase = row_index[:, None] * freqs[None, :] % length
    angle = phase.astype(jnp.float32) * (-2.0 * math.pi / length)
    return (jnp.cos(angle), jnp.sin(angle))


def complex_einsum(form, real_part, imag_part, cos_part, sin_part):
    first = jnp.einsum(form, real_part, cos_part, precision=precision_top)
    second = jnp.einsum(form, real_part, sin_part, precision=precision_top)
    first = first - jnp.einsum(form, imag_part, sin_part, precision=precision_top)
    second = second + jnp.einsum(form, imag_part, cos_part, precision=precision_top)
    return (first, second)


def x_stage(pieces):
    blocks, devices, rows, width = pieces.shape
    length = devices * width
    levels = devices.bit_length() - 1
    group = jnp.arange(devices, dtype=jnp.int32)
    residue = reverse_bits(group, levels)
    cos_8, sin_8 = root_table(group, residue, devices)
    part_real = jnp.einsum("bgtn,gd->dbtn", pieces, cos_8, precision=precision_top)
    part_imag = jnp.einsum("bgtn,gd->dbtn", pieces, sin_8, precision=precision_top)
    part_real = part_real.reshape(devices, blocks * rows, width)
    part_imag = part_imag.reshape(devices, blocks * rows, width)
    local_index = jnp.arange(width, dtype=jnp.int32)
    twist_cos, twist_sin = root_table(residue, local_index, length)
    twist_cos = twist_cos[:, None, :]
    twist_sin = twist_sin[:, None, :]
    turned_real = part_real * twist_cos - part_imag * twist_sin
    turned_imag = part_real * twist_sin + part_imag * twist_cos
    cos_w, sin_w = root_table(local_index, local_index, width)
    spec_real, spec_imag = complex_einsum("dyn,nk->dyk", turned_real, turned_imag, cos_w, sin_w)
    return jnp.stack([spec_real, spec_imag], axis=1)


def y_transform(real_part, imag_part):
    planes, length, width = real_part.shape
    outer = 1 << (length.bit_length() - 1) // 2
    inner = length // outer
    outer_index = jnp.arange(outer, dtype=jnp.int32)
    inner_index = jnp.arange(inner, dtype=jnp.int32)
    cos_one, sin_one = root_table(outer_index, outer_index, outer)
    cos_two, sin_two = root_table(inner_index, inner_index, inner)
    cos_mid, sin_mid = root_table(outer_index, inner_index, length)
    shaped_real = real_part.reshape(planes, outer, inner, width)
    shaped_imag = imag_part.reshape(planes, outer, inner, width)
    step_real, step_imag = complex_einsum(
        "zabc,ak->zkbc", shaped_real, shaped_imag, cos_one, sin_one
    )
    twist_cos = cos_mid[None, :, :, None]
    twist_sin = sin_mid[None, :, :, None]
    turned_real = step_real * twist_cos - step_imag * twist_sin
    turned_imag = step_real * twist_sin + step_imag * twist_cos
    final_real, final_imag = complex_einsum(
        "zkbc,bj->zjkc", turned_real, turned_imag, cos_two, sin_two
    )
    return (final_real.reshape(planes, length, width), final_imag.reshape(planes, length, width))


def y_kernel(norm_factor, cos_a_ref, sin_a_ref, twist_cos_ref, twist_sin_ref,
             cos_b_ref, sin_b_ref, row_scale_ref, row_rate_ref, col_scale_ref, col_shift_ref,
             col_mix_ref, spectrum_hbm, out_hbm, sum_ref,
             held, step_real, step_imag, staged, in_sems, out_sems):
    high, low, _, blocks, rows, width = spectrum_hbm.shape
    size_b = low * rows
    size_a = high * blocks
    half = width // 2
    loads = []
    for part in range(2):
        for index in range(size_b):
            copy = pltpu.make_async_copy(
                spectrum_hbm.at[:, index // rows, part, :, index % rows, :],
                held.at[part, index],
                in_sems.at[part, index],
            )
            copy.start()
            loads.append(copy)

    def dot(left, right):
        return jnp.dot(left, right, precision=precision_top, preferred_element_type=jnp.float32)

    both_a = jnp.concatenate([cos_a_ref[...], sin_a_ref[...]], axis=0)

    def first(index, carry):
        for part in range(2):
            pltpu.make_async_copy(
                spectrum_hbm.at[:, index // rows, part, :, index % rows, :],
                held.at[part, index],
                in_sems.at[part, index],
            ).wait()
        part_real = held[0, index].reshape(size_a, width)
        part_imag = held[1, index].reshape(size_a, width)
        from_real = dot(both_a, part_real)
        from_imag = dot(both_a, part_imag)
        out_real = from_real[:size_a] - from_imag[size_a:]
        out_imag = from_imag[:size_a] + from_real[size_a:]
        rows_here = pl.ds(pl.multiple_of(index * size_a, size_a), size_a)
        twist_cos = twist_cos_ref[rows_here, :]
        twist_sin = twist_sin_ref[rows_here, :]
        turned_real = out_real * twist_cos - out_imag * twist_sin
        turned_imag = out_real * twist_sin + out_imag * twist_cos
        for side in range(2):
            lanes = slice(side * half, (side + 1) * half)
            step_real[side, rows_here, :] = turned_real[:, lanes]
            step_imag[side, rows_here, :] = turned_imag[:, lanes]
        return carry

    lax.fori_loop(0, size_b, first, 0)

    col_scale = col_scale_ref[...]
    col_shift = col_shift_ref[...]
    col_mix = col_mix_ref[...]
    both_b = jnp.concatenate([cos_b_ref[...], sin_b_ref[...]], axis=0)

    def second(index, total):
        picked = pl.ds(index, size_b, stride=size_a)
        part_real = jnp.concatenate([step_real[0, picked, :], step_real[1, picked, :]], axis=1)
        part_imag = jnp.concatenate([step_imag[0, picked, :], step_imag[1, picked, :]], axis=1)
        from_real = dot(both_b, part_real)
        from_imag = dot(both_b, part_imag)
        spec_real = from_real[:size_b] - from_imag[size_b:]
        spec_imag = from_imag[:size_b] + from_real[size_b:]
        rows = pl.ds(pl.multiple_of(index * size_b, size_b), size_b)
        scale = row_scale_ref[rows, :] * col_scale
        latent_u = spec_real * norm_factor * scale
        latent_v = spec_imag * norm_factor * scale
        log_scale = row_rate_ref[rows, :] * jnp.tanh(latent_u + col_shift)
        latent_w = latent_v * jnp.exp(log_scale) + col_mix * latent_u
        terms = (
            -0.5 * (latent_u * latent_u + latent_w * latent_w)
            - math.log(2.0 * math.pi)
            + log_scale
            + 2.0 * jnp.log(scale)
        )
        staged[0, index] = latent_u
        staged[1, index] = latent_w
        for part in range(2):
            pltpu.make_async_copy(
                staged.at[part, index], out_hbm.at[part, :, index, :], out_sems.at[part, index]
            ).start()
        return total + terms

    total = lax.fori_loop(0, size_a, second, jnp.zeros((size_b, width), jnp.float32))
    sum_ref[...] = jnp.broadcast_to(jnp.sum(total), sum_ref.shape)

    def finish(index, carry):
        for part in range(2):
            pltpu.make_async_copy(
                staged.at[part, index], out_hbm.at[part, :, index, :], out_sems.at[part, index]
            ).wait()
        return carry

    lax.fori_loop(0, size_a, finish, 0)


def y_stage(spectrum, row_scale, col_scale, row_rate, col_shift, col_mix, norm_factor, devices, height):
    _, _, count, width = spectrum.shape
    length = devices * count
    size_b = 1 << (length.bit_length() - 1) // 2
    size_a = length // size_b
    blocks = length // height
    rows = height // devices
    low = size_b // rows
    high = devices // low
    index_a = jnp.arange(size_a, dtype=jnp.int32)
    index_b = jnp.arange(size_b, dtype=jnp.int32)
    order_a = (index_a % blocks) * high + index_a // blocks
    cos_a, sin_a = root_table(index_a, order_a, size_a)
    cos_b, sin_b = root_table(index_b, index_b, size_b)
    twist_cos, twist_sin = root_table(index_b, index_a, length)
    twist_cos = twist_cos.reshape(length, 1)
    twist_sin = twist_sin.reshape(length, 1)
    row_scale_t = row_scale.reshape(size_b, size_a).T.reshape(length, 1)
    row_rate_t = row_rate.reshape(size_b, size_a).T.reshape(length, 1)
    vmem = pl.BlockSpec(memory_space=pltpu.VMEM)
    anywhere = pl.BlockSpec(memory_space=pl.ANY)
    shaped = spectrum.reshape(high, low, 2, blocks, rows, width)
    latent, sums = pl.pallas_call(
        functools.partial(y_kernel, norm_factor),
        out_shape=(
            jax.ShapeDtypeStruct((2, size_b, size_a, width), jnp.float32),
            jax.ShapeDtypeStruct((8, 128), jnp.float32),
        ),
        in_specs=[vmem] * 11 + [anywhere],
        out_specs=(anywhere, vmem),
        scratch_shapes=[
            pltpu.VMEM((2, size_b, high, blocks, width), jnp.float32),
            pltpu.VMEM((2, length, width // 2), jnp.float32),
            pltpu.VMEM((2, length, width // 2), jnp.float32),
            pltpu.VMEM((2, size_a, size_b, width), jnp.float32),
            pltpu.SemaphoreType.DMA((2, size_b)),
            pltpu.SemaphoreType.DMA((2, size_a)),
        ],
        compiler_params=pltpu.CompilerParams(vmem_limit_bytes=60 * 1024 * 1024),
    )(
        cos_a, sin_a, twist_cos, twist_sin, cos_b, sin_b,
        row_scale_t, row_rate_t, col_scale.reshape(1, width), col_shift.reshape(1, width),
        col_mix.reshape(1, width), shaped,
    )
    return latent.reshape(2, length, width), sums[0, 0]

MESH_IDS = pl.DeviceIdType.MESH


def total_kernel(value_ref, out_ref, slots_a, slots_b, send_a, recv_a, send_b, recv_b):
    count_x = lax.axis_size("gx")
    count_y = lax.axis_size("gy")
    me_x = lax.axis_index("gx")
    me_y = lax.axis_index("gy")
    barrier = pltpu.get_barrier_semaphore()
    for step in range(1, count_x):
        pl.semaphore_signal(
            barrier, inc=1, device_id=((me_x + step) % count_x, me_y), device_id_type=MESH_IDS
        )
    for step in range(1, count_y):
        pl.semaphore_signal(
            barrier, inc=1, device_id=(me_x, (me_y + step) % count_y), device_id_type=MESH_IDS
        )
    slots_a[0] = value_ref[...]
    pl.semaphore_wait(barrier, count_x - 1 + count_y - 1)
    sends = []
    for step in range(1, count_x):
        copy = pltpu.make_async_remote_copy(
            src_ref=value_ref,
            dst_ref=slots_a.at[step],
            send_sem=send_a.at[step],
            recv_sem=recv_a.at[step],
            device_id=((me_x + step) % count_x, me_y),
            device_id_type=MESH_IDS,
        )
        copy.start()
        sends.append(copy)
    for copy in sends:
        copy.wait_recv()
    group_sum = slots_a[(me_x - 0) % count_x]
    for source in range(1, count_x):
        group_sum = group_sum + slots_a[(me_x - source + count_x) % count_x]
    slots_b[0] = group_sum
    later = []
    for step in range(1, count_y):
        copy = pltpu.make_async_remote_copy(
            src_ref=slots_b.at[0],
            dst_ref=slots_b.at[step],
            send_sem=send_b.at[step],
            recv_sem=recv_b.at[step],
            device_id=(me_x, (me_y + step) % count_y),
            device_id_type=MESH_IDS,
        )
        copy.start()
        later.append(copy)
    for copy in later:
        copy.wait_recv()
    grand = slots_b[(me_y - 0) % count_y]
    for source in range(1, count_y):
        grand = grand + slots_b[(me_y - source + count_y) % count_y]
    out_ref[...] = grand
    for copy in sends:
        copy.wait_send()
    for copy in later:
        copy.wait_send()


def total_everywhere(value):
    count_x = lax.axis_size("gx")
    count_y = lax.axis_size("gy")
    tile = jnp.broadcast_to(value, (8, 128)).astype(jnp.float32)
    result = pl.pallas_call(
        total_kernel,
        out_shape=jax.ShapeDtypeStruct((8, 128), jnp.float32),
        in_specs=[pl.BlockSpec(memory_space=pltpu.VMEM)],
        out_specs=pl.BlockSpec(memory_space=pltpu.VMEM),
        scratch_shapes=[
            pltpu.VMEM((count_x, 8, 128), jnp.float32),
            pltpu.VMEM((count_y, 8, 128), jnp.float32),
            pltpu.SemaphoreType.DMA((count_x,)),
            pltpu.SemaphoreType.DMA((count_x,)),
            pltpu.SemaphoreType.DMA((count_y,)),
            pltpu.SemaphoreType.DMA((count_y,)),
        ],
        compiler_params=pltpu.CompilerParams(collective_id=0, has_side_effects=True),
    )(tile)
    return result[0, 0]


def per_device(field, row_scale, col_scale, row_rate, col_shift, col_mix):
    devices = lax.axis_size("gx")
    planes, height, width = field.shape
    rows = height // devices
    outgoing = field.reshape(planes * devices, rows, width)
    incoming = lax.all_to_all(outgoing, ("gy", "gx"), split_axis=0, concat_axis=0, tiled=True)
    incoming = incoming.reshape(planes, devices, rows, width)
    both = x_stage(incoming)
    both = lax.all_to_all(both, "gx", split_axis=0, concat_axis=0, tiled=True)
    length = both.shape[0] * both.shape[2]
    total_cols = both.shape[3] * devices
    norm_factor = 1.0 / math.sqrt(length * total_cols)
    latent, part_sum = y_stage(
        both, row_scale, col_scale, row_rate, col_shift, col_mix, norm_factor, devices, height
    )
    total_sum = total_everywhere(part_sum)
    mode_count = length * total_cols * lax.axis_size("gy")
    loglik = total_sum / mode_count
    return (latent[:, None], loglik)


def solution(mesh):
    return jax.shard_map(
        per_device,
        mesh=mesh,
        in_specs=(P(None, "gy", "gx"), P(), P("gx"), P(), P("gx"), P("gx")),
        out_specs=(P(None, "gy", None, "gx"), P()),
        check_vma=False,
    )
```

```python
import functools
import math

import jax
import jax.numpy as jnp
from jax import lax
from jax.experimental import pallas as pl
from jax.experimental.pallas import tpu as pltpu
from jax.sharding import PartitionSpec as P

precision_top = lax.Precision.HIGHEST


def reverse_bits(value, count):
    result = value * 0
    for place in range(count):
        result = result + (value >> place & 1) * (1 << count - 1 - place)
    return result


def root_table(row_index, freqs, length):
    phase = row_index[:, None] * freqs[None, :] % length
    angle = phase.astype(jnp.float32) * (-2.0 * math.pi / length)
    return (jnp.cos(angle), jnp.sin(angle))


def complex_einsum(form, real_part, imag_part, cos_part, sin_part):
    first = jnp.einsum(form, real_part, cos_part, precision=precision_top)
    second = jnp.einsum(form, real_part, sin_part, precision=precision_top)
    first = first - jnp.einsum(form, imag_part, sin_part, precision=precision_top)
    second = second + jnp.einsum(form, imag_part, cos_part, precision=precision_top)
    return (first, second)


def x_stage(pieces):
    blocks, devices, rows, width = pieces.shape
    length = devices * width
    levels = devices.bit_length() - 1
    group = jnp.arange(devices, dtype=jnp.int32)
    residue = reverse_bits(group, levels)
    cos_8, sin_8 = root_table(group, residue, devices)
    part_real = jnp.einsum("bgtn,gd->dbtn", pieces, cos_8, precision=precision_top)
    part_imag = jnp.einsum("bgtn,gd->dbtn", pieces, sin_8, precision=precision_top)
    part_real = part_real.reshape(devices, blocks * rows, width)
    part_imag = part_imag.reshape(devices, blocks * rows, width)
    local_index = jnp.arange(width, dtype=jnp.int32)
    twist_cos, twist_sin = root_table(residue, local_index, length)
    twist_cos = twist_cos[:, None, :]
    twist_sin = twist_sin[:, None, :]
    turned_real = part_real * twist_cos - part_imag * twist_sin
    turned_imag = part_real * twist_sin + part_imag * twist_cos
    cos_w, sin_w = root_table(local_index, local_index, width)
    spec_real, spec_imag = complex_einsum("dyn,nk->dyk", turned_real, turned_imag, cos_w, sin_w)
    return jnp.stack([spec_real, spec_imag], axis=1)


def y_transform(real_part, imag_part):
    planes, length, width = real_part.shape
    outer = 1 << (length.bit_length() - 1) // 2
    inner = length // outer
    outer_index = jnp.arange(outer, dtype=jnp.int32)
    inner_index = jnp.arange(inner, dtype=jnp.int32)
    cos_one, sin_one = root_table(outer_index, outer_index, outer)
    cos_two, sin_two = root_table(inner_index, inner_index, inner)
    cos_mid, sin_mid = root_table(outer_index, inner_index, length)
    shaped_real = real_part.reshape(planes, outer, inner, width)
    shaped_imag = imag_part.reshape(planes, outer, inner, width)
    step_real, step_imag = complex_einsum(
        "zabc,ak->zkbc", shaped_real, shaped_imag, cos_one, sin_one
    )
    twist_cos = cos_mid[None, :, :, None]
    twist_sin = sin_mid[None, :, :, None]
    turned_real = step_real * twist_cos - step_imag * twist_sin
    turned_imag = step_real * twist_sin + step_imag * twist_cos
    final_real, final_imag = complex_einsum(
        "zkbc,bj->zjkc", turned_real, turned_imag, cos_two, sin_two
    )
    return (final_real.reshape(planes, length, width), final_imag.reshape(planes, length, width))


def y_kernel(norm_factor, cos_a_ref, sin_a_ref, twist_cos_ref, twist_sin_ref,
             cos_b_ref, sin_b_ref, row_scale_ref, row_rate_ref, col_scale_ref, col_shift_ref,
             col_mix_ref, spectrum_hbm, out_hbm, sum_ref,
             held, step_real, step_imag, staged, in_sems, out_sems):
    high, low, _, blocks, rows, width = spectrum_hbm.shape
    size_b = low * rows
    size_a = high * blocks
    half = width // 2
    loads = []
    for part in range(2):
        for index in range(size_b):
            copy = pltpu.make_async_copy(
                spectrum_hbm.at[:, index // rows, part, :, index % rows, :],
                held.at[part, index],
                in_sems.at[part, index],
            )
            copy.start()
            loads.append(copy)

    def dot(left, right):
        return jnp.dot(left, right, precision=precision_top, preferred_element_type=jnp.float32)

    both_a = jnp.concatenate([cos_a_ref[...], sin_a_ref[...]], axis=0)

    def first(index, carry):
        for part in range(2):
            pltpu.make_async_copy(
                spectrum_hbm.at[:, index // rows, part, :, index % rows, :],
                held.at[part, index],
                in_sems.at[part, index],
            ).wait()
        part_real = held[0, index].reshape(size_a, width)
        part_imag = held[1, index].reshape(size_a, width)
        from_real = dot(both_a, part_real)
        from_imag = dot(both_a, part_imag)
        out_real = from_real[:size_a] - from_imag[size_a:]
        out_imag = from_imag[:size_a] + from_real[size_a:]
        rows_here = pl.ds(pl.multiple_of(index * size_a, size_a), size_a)
        twist_cos = twist_cos_ref[rows_here, :]
        twist_sin = twist_sin_ref[rows_here, :]
        turned_real = out_real * twist_cos - out_imag * twist_sin
        turned_imag = out_real * twist_sin + out_imag * twist_cos
        for side in range(2):
            lanes = slice(side * half, (side + 1) * half)
            step_real[side, rows_here, :] = turned_real[:, lanes]
            step_imag[side, rows_here, :] = turned_imag[:, lanes]
        return carry

    lax.fori_loop(0, size_b, first, 0)

    col_scale = col_scale_ref[...]
    col_shift = col_shift_ref[...]
    col_mix = col_mix_ref[...]
    both_b = jnp.concatenate([cos_b_ref[...], sin_b_ref[...]], axis=0)

    def second(index, total):
        picked = pl.ds(index, size_b, stride=size_a)
        part_real = jnp.concatenate([step_real[0, picked, :], step_real[1, picked, :]], axis=1)
        part_imag = jnp.concatenate([step_imag[0, picked, :], step_imag[1, picked, :]], axis=1)
        from_real = dot(both_b, part_real)
        from_imag = dot(both_b, part_imag)
        spec_real = from_real[:size_b] - from_imag[size_b:]
        spec_imag = from_imag[:size_b] + from_real[size_b:]
        rows = pl.ds(pl.multiple_of(index * size_b, size_b), size_b)
        scale = row_scale_ref[rows, :] * col_scale
        latent_u = spec_real * norm_factor * scale
        latent_v = spec_imag * norm_factor * scale
        log_scale = row_rate_ref[rows, :] * jnp.tanh(latent_u + col_shift)
        latent_w = latent_v * jnp.exp(log_scale) + col_mix * latent_u
        terms = (
            -0.5 * (latent_u * latent_u + latent_w * latent_w)
            - math.log(2.0 * math.pi)
            + log_scale
            + 2.0 * jnp.log(scale)
        )
        staged[0, index] = latent_u
        staged[1, index] = latent_w
        for part in range(2):
            pltpu.make_async_copy(
                staged.at[part, index], out_hbm.at[part, :, index, :], out_sems.at[part, index]
            ).start()
        return total + terms

    total = lax.fori_loop(0, size_a, second, jnp.zeros((size_b, width), jnp.float32))
    sum_ref[...] = jnp.broadcast_to(jnp.sum(total), sum_ref.shape)

    def finish(index, carry):
        for part in range(2):
            pltpu.make_async_copy(
                staged.at[part, index], out_hbm.at[part, :, index, :], out_sems.at[part, index]
            ).wait()
        return carry

    lax.fori_loop(0, size_a, finish, 0)


def y_stage(spectrum, row_scale, col_scale, row_rate, col_shift, col_mix, norm_factor, devices, height):
    _, _, count, width = spectrum.shape
    length = devices * count
    size_b = 1 << (length.bit_length() - 1) // 2
    size_a = length // size_b
    blocks = length // height
    rows = height // devices
    low = size_b // rows
    high = devices // low
    index_a = jnp.arange(size_a, dtype=jnp.int32)
    index_b = jnp.arange(size_b, dtype=jnp.int32)
    order_a = (index_a % blocks) * high + index_a // blocks
    cos_a, sin_a = root_table(index_a, order_a, size_a)
    cos_b, sin_b = root_table(index_b, index_b, size_b)
    twist_cos, twist_sin = root_table(index_b, index_a, length)
    twist_cos = twist_cos.reshape(length, 1)
    twist_sin = twist_sin.reshape(length, 1)
    row_scale_t = row_scale.reshape(size_b, size_a).T.reshape(length, 1)
    row_rate_t = row_rate.reshape(size_b, size_a).T.reshape(length, 1)
    vmem = pl.BlockSpec(memory_space=pltpu.VMEM)
    anywhere = pl.BlockSpec(memory_space=pl.ANY)
    shaped = spectrum.reshape(high, low, 2, blocks, rows, width)
    latent, sums = pl.pallas_call(
        functools.partial(y_kernel, norm_factor),
        out_shape=(
            jax.ShapeDtypeStruct((2, size_b, size_a, width), jnp.float32),
            jax.ShapeDtypeStruct((8, 128), jnp.float32),
        ),
        in_specs=[vmem] * 11 + [anywhere],
        out_specs=(anywhere, vmem),
        scratch_shapes=[
            pltpu.VMEM((2, size_b, high, blocks, width), jnp.float32),
            pltpu.VMEM((2, length, width // 2), jnp.float32),
            pltpu.VMEM((2, length, width // 2), jnp.float32),
            pltpu.VMEM((2, size_a, size_b, width), jnp.float32),
            pltpu.SemaphoreType.DMA((2, size_b)),
            pltpu.SemaphoreType.DMA((2, size_a)),
        ],
        compiler_params=pltpu.CompilerParams(vmem_limit_bytes=60 * 1024 * 1024),
    )(
        cos_a, sin_a, twist_cos, twist_sin, cos_b, sin_b,
        row_scale_t, row_rate_t, col_scale.reshape(1, width), col_shift.reshape(1, width),
        col_mix.reshape(1, width), shaped,
    )
    return latent.reshape(2, length, width), sums

MESH_IDS = pl.DeviceIdType.MESH


def total_kernel(value_ref, out_ref, slots_a, slots_b, send_a, recv_a, send_b, recv_b):
    count_x = lax.axis_size("gx")
    count_y = lax.axis_size("gy")
    me_x = lax.axis_index("gx")
    me_y = lax.axis_index("gy")
    barrier = pltpu.get_barrier_semaphore()
    for step in range(1, count_x):
        pl.semaphore_signal(
            barrier, inc=1, device_id=((me_x + step) % count_x, me_y), device_id_type=MESH_IDS
        )
    for step in range(1, count_y):
        pl.semaphore_signal(
            barrier, inc=1, device_id=(me_x, (me_y + step) % count_y), device_id_type=MESH_IDS
        )
    slots_a[0] = value_ref[...]
    pl.semaphore_wait(barrier, count_x - 1 + count_y - 1)
    sends = []
    for step in range(1, count_x):
        copy = pltpu.make_async_remote_copy(
            src_ref=value_ref,
            dst_ref=slots_a.at[step],
            send_sem=send_a.at[step],
            recv_sem=recv_a.at[step],
            device_id=((me_x + step) % count_x, me_y),
            device_id_type=MESH_IDS,
        )
        copy.start()
        sends.append(copy)
    for copy in sends:
        copy.wait_recv()
    group_sum = slots_a[(me_x - 0) % count_x]
    for source in range(1, count_x):
        group_sum = group_sum + slots_a[(me_x - source + count_x) % count_x]
    slots_b[0] = group_sum
    later = []
    for step in range(1, count_y):
        copy = pltpu.make_async_remote_copy(
            src_ref=slots_b.at[0],
            dst_ref=slots_b.at[step],
            send_sem=send_b.at[step],
            recv_sem=recv_b.at[step],
            device_id=(me_x, (me_y + step) % count_y),
            device_id_type=MESH_IDS,
        )
        copy.start()
        later.append(copy)
    for copy in later:
        copy.wait_recv()
    grand = slots_b[(me_y - 0) % count_y]
    for source in range(1, count_y):
        grand = grand + slots_b[(me_y - source + count_y) % count_y]
    out_ref[...] = grand
    for copy in sends:
        copy.wait_send()
    for copy in later:
        copy.wait_send()


def total_everywhere(tile):
    count_x = lax.axis_size("gx")
    count_y = lax.axis_size("gy")
    result = pl.pallas_call(
        total_kernel,
        out_shape=jax.ShapeDtypeStruct((8, 128), jnp.float32),
        in_specs=[pl.BlockSpec(memory_space=pltpu.VMEM)],
        out_specs=pl.BlockSpec(memory_space=pltpu.VMEM),
        scratch_shapes=[
            pltpu.VMEM((count_x, 8, 128), jnp.float32),
            pltpu.VMEM((count_y, 8, 128), jnp.float32),
            pltpu.SemaphoreType.DMA((count_x,)),
            pltpu.SemaphoreType.DMA((count_x,)),
            pltpu.SemaphoreType.DMA((count_y,)),
            pltpu.SemaphoreType.DMA((count_y,)),
        ],
        compiler_params=pltpu.CompilerParams(collective_id=0, has_side_effects=True),
    )(tile)
    return result[0, 0]


def per_device(field, row_scale, col_scale, row_rate, col_shift, col_mix):
    devices = lax.axis_size("gx")
    planes, height, width = field.shape
    rows = height // devices
    outgoing = field.reshape(planes * devices, rows, width)
    incoming = lax.all_to_all(outgoing, ("gy", "gx"), split_axis=0, concat_axis=0, tiled=True)
    incoming = incoming.reshape(planes, devices, rows, width)
    both = x_stage(incoming)
    both = lax.all_to_all(both, "gx", split_axis=0, concat_axis=0, tiled=True)
    length = both.shape[0] * both.shape[2]
    total_cols = both.shape[3] * devices
    norm_factor = 1.0 / math.sqrt(length * total_cols)
    latent, part_sum = y_stage(
        both, row_scale, col_scale, row_rate, col_shift, col_mix, norm_factor, devices, height
    )
    total_sum = total_everywhere(part_sum)
    mode_count = length * total_cols * lax.axis_size("gy")
    loglik = total_sum / mode_count
    return (latent[:, None], loglik)


def solution(mesh):
    return jax.shard_map(
        per_device,
        mesh=mesh,
        in_specs=(P(None, "gy", "gx"), P(), P("gx"), P(), P("gx"), P("gx")),
        out_specs=(P(None, "gy", None, "gx"), P()),
        check_vma=False,
    )
```

```python
import functools
import math

import jax
import jax.numpy as jnp
from jax import lax
from jax.experimental import pallas as pl
from jax.experimental.pallas import tpu as pltpu
from jax.sharding import PartitionSpec as P

precision_top = lax.Precision.HIGHEST
precision_mid = lax.Precision.HIGH


def reverse_bits(value, count):
    result = value * 0
    for place in range(count):
        result = result + (value >> place & 1) * (1 << count - 1 - place)
    return result


def root_table(row_index, freqs, length):
    phase = row_index[:, None] * freqs[None, :] % length
    angle = phase.astype(jnp.float32) * (-2.0 * math.pi / length)
    return (jnp.cos(angle), jnp.sin(angle))


def complex_einsum(form, real_part, imag_part, cos_part, sin_part, precision=precision_top):
    first = jnp.einsum(form, real_part, cos_part, precision=precision)
    second = jnp.einsum(form, real_part, sin_part, precision=precision)
    first = first - jnp.einsum(form, imag_part, sin_part, precision=precision)
    second = second + jnp.einsum(form, imag_part, cos_part, precision=precision)
    return (first, second)


def x_stage(pieces):
    blocks, devices, rows, width = pieces.shape
    length = devices * width
    levels = devices.bit_length() - 1
    group = jnp.arange(devices, dtype=jnp.int32)
    residue = reverse_bits(group, levels)
    cos_8, sin_8 = root_table(group, residue, devices)
    part_real = jnp.einsum("bgtn,gd->dbtn", pieces, cos_8, precision=precision_top)
    part_imag = jnp.einsum("bgtn,gd->dbtn", pieces, sin_8, precision=precision_top)
    part_real = part_real.reshape(devices, blocks * rows, width)
    part_imag = part_imag.reshape(devices, blocks * rows, width)
    local_index = jnp.arange(width, dtype=jnp.int32)
    twist_cos, twist_sin = root_table(residue, local_index, length)
    twist_cos = twist_cos[:, None, :]
    twist_sin = twist_sin[:, None, :]
    turned_real = part_real * twist_cos - part_imag * twist_sin
    turned_imag = part_real * twist_sin + part_imag * twist_cos
    cos_w, sin_w = root_table(local_index, local_index, width)
    spec_real, spec_imag = complex_einsum(
        "dyn,nk->dyk", turned_real, turned_imag, cos_w, sin_w, precision_mid
    )
    return jnp.stack([spec_real, spec_imag], axis=1)


def y_transform(real_part, imag_part):
    planes, length, width = real_part.shape
    outer = 1 << (length.bit_length() - 1) // 2
    inner = length // outer
    outer_index = jnp.arange(outer, dtype=jnp.int32)
    inner_index = jnp.arange(inner, dtype=jnp.int32)
    cos_one, sin_one = root_table(outer_index, outer_index, outer)
    cos_two, sin_two = root_table(inner_index, inner_index, inner)
    cos_mid, sin_mid = root_table(outer_index, inner_index, length)
    shaped_real = real_part.reshape(planes, outer, inner, width)
    shaped_imag = imag_part.reshape(planes, outer, inner, width)
    step_real, step_imag = complex_einsum(
        "zabc,ak->zkbc", shaped_real, shaped_imag, cos_one, sin_one
    )
    twist_cos = cos_mid[None, :, :, None]
    twist_sin = sin_mid[None, :, :, None]
    turned_real = step_real * twist_cos - step_imag * twist_sin
    turned_imag = step_real * twist_sin + step_imag * twist_cos
    final_real, final_imag = complex_einsum(
        "zkbc,bj->zjkc", turned_real, turned_imag, cos_two, sin_two
    )
    return (final_real.reshape(planes, length, width), final_imag.reshape(planes, length, width))


def y_kernel(norm_factor, cos_a_ref, sin_a_ref, twist_cos_ref, twist_sin_ref,
             cos_b_ref, sin_b_ref, row_scale_ref, row_rate_ref, col_scale_ref, col_shift_ref,
             col_mix_ref, spectrum_hbm, out_hbm, sum_ref,
             held, step_real, step_imag, staged, in_sems, out_sems):
    high, low, _, blocks, rows, width = spectrum_hbm.shape
    size_b = low * rows
    size_a = high * blocks
    half = width // 2
    loads = []
    for part in range(2):
        for index in range(size_b):
            copy = pltpu.make_async_copy(
                spectrum_hbm.at[:, index // rows, part, :, index % rows, :],
                held.at[part, index],
                in_sems.at[part, index],
            )
            copy.start()
            loads.append(copy)

    def dot(left, right):
        return jnp.dot(left, right, precision=precision_mid, preferred_element_type=jnp.float32)

    both_a = jnp.concatenate([cos_a_ref[...], sin_a_ref[...]], axis=0)

    def first(index, carry):
        for part in range(2):
            pltpu.make_async_copy(
                spectrum_hbm.at[:, index // rows, part, :, index % rows, :],
                held.at[part, index],
                in_sems.at[part, index],
            ).wait()
        part_real = held[0, index].reshape(size_a, width)
        part_imag = held[1, index].reshape(size_a, width)
        from_real = dot(both_a, part_real)
        from_imag = dot(both_a, part_imag)
        out_real = from_real[:size_a] - from_imag[size_a:]
        out_imag = from_imag[:size_a] + from_real[size_a:]
        rows_here = pl.ds(pl.multiple_of(index * size_a, size_a), size_a)
        twist_cos = twist_cos_ref[rows_here, :]
        twist_sin = twist_sin_ref[rows_here, :]
        turned_real = out_real * twist_cos - out_imag * twist_sin
        turned_imag = out_real * twist_sin + out_imag * twist_cos
        for side in range(2):
            lanes = slice(side * half, (side + 1) * half)
            step_real[side, rows_here, :] = turned_real[:, lanes]
            step_imag[side, rows_here, :] = turned_imag[:, lanes]
        return carry

    lax.fori_loop(0, size_b, first, 0)

    col_scale = col_scale_ref[...]
    col_shift = col_shift_ref[...]
    col_mix = col_mix_ref[...]
    both_b = jnp.concatenate([cos_b_ref[...], sin_b_ref[...]], axis=0)

    def second(index, total):
        picked = pl.ds(index, size_b, stride=size_a)
        part_real = jnp.concatenate([step_real[0, picked, :], step_real[1, picked, :]], axis=1)
        part_imag = jnp.concatenate([step_imag[0, picked, :], step_imag[1, picked, :]], axis=1)
        from_real = dot(both_b, part_real)
        from_imag = dot(both_b, part_imag)
        spec_real = from_real[:size_b] - from_imag[size_b:]
        spec_imag = from_imag[:size_b] + from_real[size_b:]
        rows = pl.ds(pl.multiple_of(index * size_b, size_b), size_b)
        scale = row_scale_ref[rows, :] * col_scale
        latent_u = spec_real * norm_factor * scale
        latent_v = spec_imag * norm_factor * scale
        log_scale = row_rate_ref[rows, :] * jnp.tanh(latent_u + col_shift)
        latent_w = latent_v * jnp.exp(log_scale) + col_mix * latent_u
        terms = (
            -0.5 * (latent_u * latent_u + latent_w * latent_w)
            - math.log(2.0 * math.pi)
            + log_scale
            + 2.0 * jnp.log(scale)
        )
        staged[0, index] = latent_u
        staged[1, index] = latent_w
        for part in range(2):
            pltpu.make_async_copy(
                staged.at[part, index], out_hbm.at[part, :, index, :], out_sems.at[part, index]
            ).start()
        return total + terms

    total = lax.fori_loop(0, size_a, second, jnp.zeros((size_b, width), jnp.float32))
    sum_ref[...] = jnp.broadcast_to(jnp.sum(total), sum_ref.shape)

    def finish(index, carry):
        for part in range(2):
            pltpu.make_async_copy(
                staged.at[part, index], out_hbm.at[part, :, index, :], out_sems.at[part, index]
            ).wait()
        return carry

    lax.fori_loop(0, size_a, finish, 0)


def y_stage(spectrum, row_scale, col_scale, row_rate, col_shift, col_mix, norm_factor, devices, height):
    _, _, count, width = spectrum.shape
    length = devices * count
    size_b = 1 << (length.bit_length() - 1) // 2
    size_a = length // size_b
    blocks = length // height
    rows = height // devices
    low = size_b // rows
    high = devices // low
    index_a = jnp.arange(size_a, dtype=jnp.int32)
    index_b = jnp.arange(size_b, dtype=jnp.int32)
    order_a = (index_a % blocks) * high + index_a // blocks
    cos_a, sin_a = root_table(index_a, order_a, size_a)
    cos_b, sin_b = root_table(index_b, index_b, size_b)
    twist_cos, twist_sin = root_table(index_b, index_a, length)
    twist_cos = twist_cos.reshape(length, 1)
    twist_sin = twist_sin.reshape(length, 1)
    row_scale_t = row_scale.reshape(size_b, size_a).T.reshape(length, 1)
    row_rate_t = row_rate.reshape(size_b, size_a).T.reshape(length, 1)
    vmem = pl.BlockSpec(memory_space=pltpu.VMEM)
    anywhere = pl.BlockSpec(memory_space=pl.ANY)
    shaped = spectrum.reshape(high, low, 2, blocks, rows, width)
    latent, sums = pl.pallas_call(
        functools.partial(y_kernel, norm_factor),
        out_shape=(
            jax.ShapeDtypeStruct((2, size_b, size_a, width), jnp.float32),
            jax.ShapeDtypeStruct((8, 128), jnp.float32),
        ),
        in_specs=[vmem] * 11 + [anywhere],
        out_specs=(anywhere, vmem),
        scratch_shapes=[
            pltpu.VMEM((2, size_b, high, blocks, width), jnp.float32),
            pltpu.VMEM((2, length, width // 2), jnp.float32),
            pltpu.VMEM((2, length, width // 2), jnp.float32),
            pltpu.VMEM((2, size_a, size_b, width), jnp.float32),
            pltpu.SemaphoreType.DMA((2, size_b)),
            pltpu.SemaphoreType.DMA((2, size_a)),
        ],
        compiler_params=pltpu.CompilerParams(vmem_limit_bytes=60 * 1024 * 1024),
    )(
        cos_a, sin_a, twist_cos, twist_sin, cos_b, sin_b,
        row_scale_t, row_rate_t, col_scale.reshape(1, width), col_shift.reshape(1, width),
        col_mix.reshape(1, width), shaped,
    )
    return latent.reshape(2, length, width), sums

MESH_IDS = pl.DeviceIdType.MESH


def total_kernel(value_ref, out_ref, slots_a, slots_b, send_a, recv_a, send_b, recv_b):
    count_x = lax.axis_size("gx")
    count_y = lax.axis_size("gy")
    me_x = lax.axis_index("gx")
    me_y = lax.axis_index("gy")
    barrier = pltpu.get_barrier_semaphore()
    for step in range(1, count_x):
        pl.semaphore_signal(
            barrier, inc=1, device_id=((me_x + step) % count_x, me_y), device_id_type=MESH_IDS
        )
    for step in range(1, count_y):
        pl.semaphore_signal(
            barrier, inc=1, device_id=(me_x, (me_y + step) % count_y), device_id_type=MESH_IDS
        )
    slots_a[0] = value_ref[...]
    pl.semaphore_wait(barrier, count_x - 1 + count_y - 1)
    sends = []
    for step in range(1, count_x):
        copy = pltpu.make_async_remote_copy(
            src_ref=value_ref,
            dst_ref=slots_a.at[step],
            send_sem=send_a.at[step],
            recv_sem=recv_a.at[step],
            device_id=((me_x + step) % count_x, me_y),
            device_id_type=MESH_IDS,
        )
        copy.start()
        sends.append(copy)
    for copy in sends:
        copy.wait_recv()
    group_sum = slots_a[(me_x - 0) % count_x]
    for source in range(1, count_x):
        group_sum = group_sum + slots_a[(me_x - source + count_x) % count_x]
    slots_b[0] = group_sum
    later = []
    for step in range(1, count_y):
        copy = pltpu.make_async_remote_copy(
            src_ref=slots_b.at[0],
            dst_ref=slots_b.at[step],
            send_sem=send_b.at[step],
            recv_sem=recv_b.at[step],
            device_id=(me_x, (me_y + step) % count_y),
            device_id_type=MESH_IDS,
        )
        copy.start()
        later.append(copy)
    for copy in later:
        copy.wait_recv()
    grand = slots_b[(me_y - 0) % count_y]
    for source in range(1, count_y):
        grand = grand + slots_b[(me_y - source + count_y) % count_y]
    out_ref[...] = grand
    for copy in sends:
        copy.wait_send()
    for copy in later:
        copy.wait_send()


def total_everywhere(tile):
    count_x = lax.axis_size("gx")
    count_y = lax.axis_size("gy")
    result = pl.pallas_call(
        total_kernel,
        out_shape=jax.ShapeDtypeStruct((8, 128), jnp.float32),
        in_specs=[pl.BlockSpec(memory_space=pltpu.VMEM)],
        out_specs=pl.BlockSpec(memory_space=pltpu.VMEM),
        scratch_shapes=[
            pltpu.VMEM((count_x, 8, 128), jnp.float32),
            pltpu.VMEM((count_y, 8, 128), jnp.float32),
            pltpu.SemaphoreType.DMA((count_x,)),
            pltpu.SemaphoreType.DMA((count_x,)),
            pltpu.SemaphoreType.DMA((count_y,)),
            pltpu.SemaphoreType.DMA((count_y,)),
        ],
        compiler_params=pltpu.CompilerParams(collective_id=0, has_side_effects=True),
    )(tile)
    return result[0, 0]


def per_device(field, row_scale, col_scale, row_rate, col_shift, col_mix):
    devices = lax.axis_size("gx")
    planes, height, width = field.shape
    rows = height // devices
    outgoing = field.reshape(planes * devices, rows, width)
    incoming = lax.all_to_all(outgoing, ("gy", "gx"), split_axis=0, concat_axis=0, tiled=True)
    incoming = incoming.reshape(planes, devices, rows, width)
    both = x_stage(incoming)
    both = lax.all_to_all(both, "gx", split_axis=0, concat_axis=0, tiled=True)
    length = both.shape[0] * both.shape[2]
    total_cols = both.shape[3] * devices
    norm_factor = 1.0 / math.sqrt(length * total_cols)
    latent, part_sum = y_stage(
        both, row_scale, col_scale, row_rate, col_shift, col_mix, norm_factor, devices, height
    )
    total_sum = total_everywhere(part_sum)
    mode_count = length * total_cols * lax.axis_size("gy")
    loglik = total_sum / mode_count
    return (latent[:, None], loglik)


def solution(mesh):
    return jax.shard_map(
        per_device,
        mesh=mesh,
        in_specs=(P(None, "gy", "gx"), P(), P("gx"), P(), P("gx"), P("gx")),
        out_specs=(P(None, "gy", None, "gx"), P()),
        check_vma=False,
    )
```

```python
import functools
import math

import jax
import jax.numpy as jnp
from jax import lax
from jax.experimental import pallas as pl
from jax.experimental.pallas import tpu as pltpu
from jax.sharding import PartitionSpec as P

precision_top = lax.Precision.HIGHEST
precision_mid = lax.Precision.HIGH


def reverse_bits(value, count):
    result = value * 0
    for place in range(count):
        result = result + (value >> place & 1) * (1 << count - 1 - place)
    return result


def root_table(row_index, freqs, length):
    phase = row_index[:, None] * freqs[None, :] % length
    angle = phase.astype(jnp.float32) * (-2.0 * math.pi / length)
    return (jnp.cos(angle), jnp.sin(angle))


def complex_einsum(form, real_part, imag_part, cos_part, sin_part, precision=precision_top):
    first = jnp.einsum(form, real_part, cos_part, precision=precision)
    second = jnp.einsum(form, real_part, sin_part, precision=precision)
    first = first - jnp.einsum(form, imag_part, sin_part, precision=precision)
    second = second + jnp.einsum(form, imag_part, cos_part, precision=precision)
    return (first, second)


def x_stage(pieces):
    blocks, devices, rows, width = pieces.shape
    length = devices * width
    levels = devices.bit_length() - 1
    group = jnp.arange(devices, dtype=jnp.int32)
    residue = reverse_bits(group, levels)
    cos_8, sin_8 = root_table(group, residue, devices)
    part_real = jnp.einsum("bgtn,gd->dbtn", pieces, cos_8, precision=precision_top)
    part_imag = jnp.einsum("bgtn,gd->dbtn", pieces, sin_8, precision=precision_top)
    part_real = part_real.reshape(devices, blocks * rows, width)
    part_imag = part_imag.reshape(devices, blocks * rows, width)
    local_index = jnp.arange(width, dtype=jnp.int32)
    freqs = residue[:, None] + devices * local_index[None, :]
    phase = local_index[None, :, None] * freqs[:, None, :] % length
    angle = phase.astype(jnp.float32) * (-2.0 * math.pi / length)
    cos_t = jnp.cos(angle)
    sin_t = jnp.sin(angle)
    from_real = jnp.concatenate([cos_t, sin_t], axis=2)
    from_imag = jnp.concatenate([-sin_t, cos_t], axis=2)
    spectrum = jnp.einsum("dyn,dnk->dyk", part_real, from_real, precision=precision_mid)
    spectrum = spectrum + jnp.einsum("dyn,dnk->dyk", part_imag, from_imag, precision=precision_mid)
    return spectrum


def y_transform(real_part, imag_part):
    planes, length, width = real_part.shape
    outer = 1 << (length.bit_length() - 1) // 2
    inner = length // outer
    outer_index = jnp.arange(outer, dtype=jnp.int32)
    inner_index = jnp.arange(inner, dtype=jnp.int32)
    cos_one, sin_one = root_table(outer_index, outer_index, outer)
    cos_two, sin_two = root_table(inner_index, inner_index, inner)
    cos_mid, sin_mid = root_table(outer_index, inner_index, length)
    shaped_real = real_part.reshape(planes, outer, inner, width)
    shaped_imag = imag_part.reshape(planes, outer, inner, width)
    step_real, step_imag = complex_einsum(
        "zabc,ak->zkbc", shaped_real, shaped_imag, cos_one, sin_one
    )
    twist_cos = cos_mid[None, :, :, None]
    twist_sin = sin_mid[None, :, :, None]
    turned_real = step_real * twist_cos - step_imag * twist_sin
    turned_imag = step_real * twist_sin + step_imag * twist_cos
    final_real, final_imag = complex_einsum(
        "zkbc,bj->zjkc", turned_real, turned_imag, cos_two, sin_two
    )
    return (final_real.reshape(planes, length, width), final_imag.reshape(planes, length, width))


def y_kernel(norm_factor, cos_a_ref, sin_a_ref, twist_cos_ref, twist_sin_ref,
             cos_b_ref, sin_b_ref, row_scale_ref, row_rate_ref, col_scale_ref, col_shift_ref,
             col_mix_ref, spectrum_hbm, out_hbm, sum_ref,
             held, step_real, step_imag, staged, in_sems, out_sems):
    high, low, blocks, rows, both_width = spectrum_hbm.shape
    width = both_width // 2
    size_b = low * rows
    size_a = high * blocks
    half = width // 2
    loads = []
    for part in range(2):
        for index in range(size_b):
            copy = pltpu.make_async_copy(
                spectrum_hbm.at[:, index // rows, :, index % rows, pl.ds(part * width, width)],
                held.at[part, index],
                in_sems.at[part, index],
            )
            copy.start()
            loads.append(copy)

    def dot(left, right):
        return jnp.dot(left, right, precision=precision_mid, preferred_element_type=jnp.float32)

    both_a = jnp.concatenate([cos_a_ref[...], sin_a_ref[...]], axis=0)

    def first(index, carry):
        for part in range(2):
            pltpu.make_async_copy(
                spectrum_hbm.at[:, index // rows, :, index % rows, pl.ds(part * width, width)],
                held.at[part, index],
                in_sems.at[part, index],
            ).wait()
        part_real = held[0, index].reshape(size_a, width)
        part_imag = held[1, index].reshape(size_a, width)
        from_real = dot(both_a, part_real)
        from_imag = dot(both_a, part_imag)
        out_real = from_real[:size_a] - from_imag[size_a:]
        out_imag = from_imag[:size_a] + from_real[size_a:]
        rows_here = pl.ds(pl.multiple_of(index * size_a, size_a), size_a)
        twist_cos = twist_cos_ref[rows_here, :]
        twist_sin = twist_sin_ref[rows_here, :]
        turned_real = out_real * twist_cos - out_imag * twist_sin
        turned_imag = out_real * twist_sin + out_imag * twist_cos
        for side in range(2):
            lanes = slice(side * half, (side + 1) * half)
            step_real[side, rows_here, :] = turned_real[:, lanes]
            step_imag[side, rows_here, :] = turned_imag[:, lanes]
        return carry

    lax.fori_loop(0, size_b, first, 0)

    col_scale = col_scale_ref[...]
    col_shift = col_shift_ref[...]
    col_mix = col_mix_ref[...]
    both_b = jnp.concatenate([cos_b_ref[...], sin_b_ref[...]], axis=0)

    def second(index, total):
        picked = pl.ds(index, size_b, stride=size_a)
        part_real = jnp.concatenate([step_real[0, picked, :], step_real[1, picked, :]], axis=1)
        part_imag = jnp.concatenate([step_imag[0, picked, :], step_imag[1, picked, :]], axis=1)
        from_real = dot(both_b, part_real)
        from_imag = dot(both_b, part_imag)
        spec_real = from_real[:size_b] - from_imag[size_b:]
        spec_imag = from_imag[:size_b] + from_real[size_b:]
        rows = pl.ds(pl.multiple_of(index * size_b, size_b), size_b)
        scale = row_scale_ref[rows, :] * col_scale
        latent_u = spec_real * norm_factor * scale
        latent_v = spec_imag * norm_factor * scale
        log_scale = row_rate_ref[rows, :] * jnp.tanh(latent_u + col_shift)
        latent_w = latent_v * jnp.exp(log_scale) + col_mix * latent_u
        terms = (
            -0.5 * (latent_u * latent_u + latent_w * latent_w)
            - math.log(2.0 * math.pi)
            + log_scale
            + 2.0 * jnp.log(scale)
        )
        staged[0, index] = latent_u
        staged[1, index] = latent_w
        for part in range(2):
            pltpu.make_async_copy(
                staged.at[part, index], out_hbm.at[part, :, index, :], out_sems.at[part, index]
            ).start()
        return total + terms

    total = lax.fori_loop(0, size_a, second, jnp.zeros((size_b, width), jnp.float32))
    sum_ref[...] = jnp.broadcast_to(jnp.sum(total), sum_ref.shape)

    def finish(index, carry):
        for part in range(2):
            pltpu.make_async_copy(
                staged.at[part, index], out_hbm.at[part, :, index, :], out_sems.at[part, index]
            ).wait()
        return carry

    lax.fori_loop(0, size_a, finish, 0)


def y_stage(spectrum, row_scale, col_scale, row_rate, col_shift, col_mix, norm_factor, devices, height):
    _, count, both_width = spectrum.shape
    width = both_width // 2
    length = devices * count
    size_b = 1 << (length.bit_length() - 1) // 2
    size_a = length // size_b
    blocks = length // height
    rows = height // devices
    low = size_b // rows
    high = devices // low
    index_a = jnp.arange(size_a, dtype=jnp.int32)
    index_b = jnp.arange(size_b, dtype=jnp.int32)
    order_a = (index_a % blocks) * high + index_a // blocks
    cos_a, sin_a = root_table(index_a, order_a, size_a)
    cos_b, sin_b = root_table(index_b, index_b, size_b)
    twist_cos, twist_sin = root_table(index_b, index_a, length)
    twist_cos = twist_cos.reshape(length, 1)
    twist_sin = twist_sin.reshape(length, 1)
    row_scale_t = row_scale.reshape(size_b, size_a).T.reshape(length, 1)
    row_rate_t = row_rate.reshape(size_b, size_a).T.reshape(length, 1)
    vmem = pl.BlockSpec(memory_space=pltpu.VMEM)
    anywhere = pl.BlockSpec(memory_space=pl.ANY)
    shaped = spectrum.reshape(high, low, blocks, rows, both_width)
    latent, sums = pl.pallas_call(
        functools.partial(y_kernel, norm_factor),
        out_shape=(
            jax.ShapeDtypeStruct((2, size_b, size_a, width), jnp.float32),
            jax.ShapeDtypeStruct((8, 128), jnp.float32),
        ),
        in_specs=[vmem] * 11 + [anywhere],
        out_specs=(anywhere, vmem),
        scratch_shapes=[
            pltpu.VMEM((2, size_b, high, blocks, width), jnp.float32),
            pltpu.VMEM((2, length, width // 2), jnp.float32),
            pltpu.VMEM((2, length, width // 2), jnp.float32),
            pltpu.VMEM((2, size_a, size_b, width), jnp.float32),
            pltpu.SemaphoreType.DMA((2, size_b)),
            pltpu.SemaphoreType.DMA((2, size_a)),
        ],
        compiler_params=pltpu.CompilerParams(vmem_limit_bytes=60 * 1024 * 1024),
    )(
        cos_a, sin_a, twist_cos, twist_sin, cos_b, sin_b,
        row_scale_t, row_rate_t, col_scale.reshape(1, width), col_shift.reshape(1, width),
        col_mix.reshape(1, width), shaped,
    )
    return latent.reshape(2, length, width), sums

MESH_IDS = pl.DeviceIdType.MESH


def total_kernel(value_ref, out_ref, slots_a, slots_b, send_a, recv_a, send_b, recv_b):
    count_x = lax.axis_size("gx")
    count_y = lax.axis_size("gy")
    me_x = lax.axis_index("gx")
    me_y = lax.axis_index("gy")
    barrier = pltpu.get_barrier_semaphore()
    for step in range(1, count_x):
        pl.semaphore_signal(
            barrier, inc=1, device_id=((me_x + step) % count_x, me_y), device_id_type=MESH_IDS
        )
    for step in range(1, count_y):
        pl.semaphore_signal(
            barrier, inc=1, device_id=(me_x, (me_y + step) % count_y), device_id_type=MESH_IDS
        )
    slots_a[0] = value_ref[...]
    pl.semaphore_wait(barrier, count_x - 1 + count_y - 1)
    sends = []
    for step in range(1, count_x):
        copy = pltpu.make_async_remote_copy(
            src_ref=value_ref,
            dst_ref=slots_a.at[step],
            send_sem=send_a.at[step],
            recv_sem=recv_a.at[step],
            device_id=((me_x + step) % count_x, me_y),
            device_id_type=MESH_IDS,
        )
        copy.start()
        sends.append(copy)
    for copy in sends:
        copy.wait_recv()
    group_sum = slots_a[(me_x - 0) % count_x]
    for source in range(1, count_x):
        group_sum = group_sum + slots_a[(me_x - source + count_x) % count_x]
    slots_b[0] = group_sum
    later = []
    for step in range(1, count_y):
        copy = pltpu.make_async_remote_copy(
            src_ref=slots_b.at[0],
            dst_ref=slots_b.at[step],
            send_sem=send_b.at[step],
            recv_sem=recv_b.at[step],
            device_id=(me_x, (me_y + step) % count_y),
            device_id_type=MESH_IDS,
        )
        copy.start()
        later.append(copy)
    for copy in later:
        copy.wait_recv()
    grand = slots_b[(me_y - 0) % count_y]
    for source in range(1, count_y):
        grand = grand + slots_b[(me_y - source + count_y) % count_y]
    out_ref[...] = grand
    for copy in sends:
        copy.wait_send()
    for copy in later:
        copy.wait_send()


def total_everywhere(tile):
    count_x = lax.axis_size("gx")
    count_y = lax.axis_size("gy")
    result = pl.pallas_call(
        total_kernel,
        out_shape=jax.ShapeDtypeStruct((8, 128), jnp.float32),
        in_specs=[pl.BlockSpec(memory_space=pltpu.VMEM)],
        out_specs=pl.BlockSpec(memory_space=pltpu.VMEM),
        scratch_shapes=[
            pltpu.VMEM((count_x, 8, 128), jnp.float32),
            pltpu.VMEM((count_y, 8, 128), jnp.float32),
            pltpu.SemaphoreType.DMA((count_x,)),
            pltpu.SemaphoreType.DMA((count_x,)),
            pltpu.SemaphoreType.DMA((count_y,)),
            pltpu.SemaphoreType.DMA((count_y,)),
        ],
        compiler_params=pltpu.CompilerParams(collective_id=0, has_side_effects=True),
    )(tile)
    return result[0, 0]


def per_device(field, row_scale, col_scale, row_rate, col_shift, col_mix):
    devices = lax.axis_size("gx")
    planes, height, width = field.shape
    rows = height // devices
    outgoing = field.reshape(planes * devices, rows, width)
    incoming = lax.all_to_all(outgoing, ("gy", "gx"), split_axis=0, concat_axis=0, tiled=True)
    incoming = incoming.reshape(planes, devices, rows, width)
    both = x_stage(incoming)
    both = lax.all_to_all(both, "gx", split_axis=0, concat_axis=0, tiled=True)
    length = both.shape[0] * both.shape[1]
    total_cols = both.shape[2] // 2 * devices
    norm_factor = 1.0 / math.sqrt(length * total_cols)
    latent, part_sum = y_stage(
        both, row_scale, col_scale, row_rate, col_shift, col_mix, norm_factor, devices, height
    )
    total_sum = total_everywhere(part_sum)
    mode_count = length * total_cols * lax.axis_size("gy")
    loglik = total_sum / mode_count
    return (latent[:, None], loglik)


def solution(mesh):
    return jax.shard_map(
        per_device,
        mesh=mesh,
        in_specs=(P(None, "gy", "gx"), P(), P("gx"), P(), P("gx"), P("gx")),
        out_specs=(P(None, "gy", None, "gx"), P()),
        check_vma=False,
    )
```

```python
import functools
import math

import jax
import jax.numpy as jnp
from jax import lax
from jax.experimental import pallas as pl
from jax.experimental.pallas import tpu as pltpu
from jax.sharding import PartitionSpec as P

precision_top = lax.Precision.HIGHEST
precision_mid = lax.Precision.HIGH


def reverse_bits(value, count):
    result = value * 0
    for place in range(count):
        result = result + (value >> place & 1) * (1 << count - 1 - place)
    return result


def root_table(row_index, freqs, length):
    phase = row_index[:, None] * freqs[None, :] % length
    angle = phase.astype(jnp.float32) * (-2.0 * math.pi / length)
    return (jnp.cos(angle), jnp.sin(angle))


def complex_einsum(form, real_part, imag_part, cos_part, sin_part, precision=precision_top):
    first = jnp.einsum(form, real_part, cos_part, precision=precision)
    second = jnp.einsum(form, real_part, sin_part, precision=precision)
    first = first - jnp.einsum(form, imag_part, sin_part, precision=precision)
    second = second + jnp.einsum(form, imag_part, cos_part, precision=precision)
    return (first, second)


def x_stage(pieces):
    blocks, devices, rows, width = pieces.shape
    length = devices * width
    levels = devices.bit_length() - 1
    group = jnp.arange(devices, dtype=jnp.int32)
    residue = reverse_bits(group, levels)
    slices = [pieces[:, g].reshape(blocks * rows, width) for g in range(devices)]
    real_slots = []
    imag_slots = []
    for slot in range(devices):
        turn = sum(((slot >> place) & 1) << (levels - 1 - place) for place in range(levels))
        real_terms = []
        imag_terms = []
        for g in range(devices):
            phase = g * turn % devices
            angle = -2.0 * math.pi * phase / devices
            cos_value = 0.0 if phase * 4 % devices == 0 and phase * 4 // devices % 2 == 1 else math.cos(angle)
            sin_value = 0.0 if phase * 2 % devices == 0 else math.sin(angle)
            if cos_value != 0.0:
                real_terms.append(slices[g] * cos_value)
            if sin_value != 0.0:
                imag_terms.append(slices[g] * sin_value)
        real_slots.append(sum(real_terms[1:], real_terms[0]))
        imag_slots.append(
            sum(imag_terms[1:], imag_terms[0]) if imag_terms else jnp.zeros_like(slices[0])
        )
    part_real = jnp.stack(real_slots)
    part_imag = jnp.stack(imag_slots)
    local_index = jnp.arange(width, dtype=jnp.int32)
    freqs = residue[:, None] + devices * local_index[None, :]
    phase = local_index[None, :, None] * freqs[:, None, :] % length
    angle = phase.astype(jnp.float32) * (-2.0 * math.pi / length)
    cos_t = jnp.cos(angle)
    sin_t = jnp.sin(angle)
    from_real = jnp.concatenate([cos_t, sin_t], axis=2)
    from_imag = jnp.concatenate([-sin_t, cos_t], axis=2)
    spectrum = jnp.einsum("dyn,dnk->dyk", part_real, from_real, precision=precision_mid)
    spectrum = spectrum + jnp.einsum("dyn,dnk->dyk", part_imag, from_imag, precision=precision_mid)
    return spectrum


def y_transform(real_part, imag_part):
    planes, length, width = real_part.shape
    outer = 1 << (length.bit_length() - 1) // 2
    inner = length // outer
    outer_index = jnp.arange(outer, dtype=jnp.int32)
    inner_index = jnp.arange(inner, dtype=jnp.int32)
    cos_one, sin_one = root_table(outer_index, outer_index, outer)
    cos_two, sin_two = root_table(inner_index, inner_index, inner)
    cos_mid, sin_mid = root_table(outer_index, inner_index, length)
    shaped_real = real_part.reshape(planes, outer, inner, width)
    shaped_imag = imag_part.reshape(planes, outer, inner, width)
    step_real, step_imag = complex_einsum(
        "zabc,ak->zkbc", shaped_real, shaped_imag, cos_one, sin_one
    )
    twist_cos = cos_mid[None, :, :, None]
    twist_sin = sin_mid[None, :, :, None]
    turned_real = step_real * twist_cos - step_imag * twist_sin
    turned_imag = step_real * twist_sin + step_imag * twist_cos
    final_real, final_imag = complex_einsum(
        "zkbc,bj->zjkc", turned_real, turned_imag, cos_two, sin_two
    )
    return (final_real.reshape(planes, length, width), final_imag.reshape(planes, length, width))


def y_kernel(norm_factor, cos_a_ref, sin_a_ref, twist_cos_ref, twist_sin_ref,
             cos_b_ref, sin_b_ref, row_scale_ref, row_rate_ref, col_scale_ref, col_shift_ref,
             col_mix_ref, spectrum_hbm, out_hbm, sum_ref,
             held, step_real, step_imag, staged, in_sems, out_sems):
    high, low, blocks, rows, both_width = spectrum_hbm.shape
    width = both_width // 2
    size_b = low * rows
    size_a = high * blocks
    half = width // 2
    loads = []
    for part in range(2):
        for index in range(size_b):
            copy = pltpu.make_async_copy(
                spectrum_hbm.at[:, index // rows, :, index % rows, pl.ds(part * width, width)],
                held.at[part, index],
                in_sems.at[part, index],
            )
            copy.start()
            loads.append(copy)

    def dot(left, right):
        return jnp.dot(left, right, precision=precision_mid, preferred_element_type=jnp.float32)

    both_a = jnp.concatenate([cos_a_ref[...], sin_a_ref[...]], axis=0)

    def first(index, carry):
        for part in range(2):
            pltpu.make_async_copy(
                spectrum_hbm.at[:, index // rows, :, index % rows, pl.ds(part * width, width)],
                held.at[part, index],
                in_sems.at[part, index],
            ).wait()
        part_real = held[0, index].reshape(size_a, width)
        part_imag = held[1, index].reshape(size_a, width)
        from_real = dot(both_a, part_real)
        from_imag = dot(both_a, part_imag)
        out_real = from_real[:size_a] - from_imag[size_a:]
        out_imag = from_imag[:size_a] + from_real[size_a:]
        rows_here = pl.ds(pl.multiple_of(index * size_a, size_a), size_a)
        twist_cos = twist_cos_ref[rows_here, :]
        twist_sin = twist_sin_ref[rows_here, :]
        turned_real = out_real * twist_cos - out_imag * twist_sin
        turned_imag = out_real * twist_sin + out_imag * twist_cos
        for side in range(2):
            lanes = slice(side * half, (side + 1) * half)
            step_real[side, rows_here, :] = turned_real[:, lanes]
            step_imag[side, rows_here, :] = turned_imag[:, lanes]
        return carry

    lax.fori_loop(0, size_b, first, 0)

    col_scale = col_scale_ref[...]
    col_shift = col_shift_ref[...]
    col_mix = col_mix_ref[...]
    both_b = jnp.concatenate([cos_b_ref[...], sin_b_ref[...]], axis=0)

    def second(index, total):
        picked = pl.ds(index, size_b, stride=size_a)
        part_real = jnp.concatenate([step_real[0, picked, :], step_real[1, picked, :]], axis=1)
        part_imag = jnp.concatenate([step_imag[0, picked, :], step_imag[1, picked, :]], axis=1)
        from_real = dot(both_b, part_real)
        from_imag = dot(both_b, part_imag)
        spec_real = from_real[:size_b] - from_imag[size_b:]
        spec_imag = from_imag[:size_b] + from_real[size_b:]
        rows = pl.ds(pl.multiple_of(index * size_b, size_b), size_b)
        scale = row_scale_ref[rows, :] * col_scale
        latent_u = spec_real * norm_factor * scale
        latent_v = spec_imag * norm_factor * scale
        log_scale = row_rate_ref[rows, :] * jnp.tanh(latent_u + col_shift)
        latent_w = latent_v * jnp.exp(log_scale) + col_mix * latent_u
        terms = (
            -0.5 * (latent_u * latent_u + latent_w * latent_w)
            - math.log(2.0 * math.pi)
            + log_scale
            + 2.0 * jnp.log(scale)
        )
        staged[0, index] = latent_u
        staged[1, index] = latent_w
        for part in range(2):
            pltpu.make_async_copy(
                staged.at[part, index], out_hbm.at[part, :, index, :], out_sems.at[part, index]
            ).start()
        return total + terms

    total = lax.fori_loop(0, size_a, second, jnp.zeros((size_b, width), jnp.float32))
    sum_ref[...] = jnp.broadcast_to(jnp.sum(total), sum_ref.shape)

    def finish(index, carry):
        for part in range(2):
            pltpu.make_async_copy(
                staged.at[part, index], out_hbm.at[part, :, index, :], out_sems.at[part, index]
            ).wait()
        return carry

    lax.fori_loop(0, size_a, finish, 0)


def y_stage(spectrum, row_scale, col_scale, row_rate, col_shift, col_mix, norm_factor, devices, height):
    _, count, both_width = spectrum.shape
    width = both_width // 2
    length = devices * count
    size_b = 1 << (length.bit_length() - 1) // 2
    size_a = length // size_b
    blocks = length // height
    rows = height // devices
    low = size_b // rows
    high = devices // low
    index_a = jnp.arange(size_a, dtype=jnp.int32)
    index_b = jnp.arange(size_b, dtype=jnp.int32)
    order_a = (index_a % blocks) * high + index_a // blocks
    cos_a, sin_a = root_table(index_a, order_a, size_a)
    cos_b, sin_b = root_table(index_b, index_b, size_b)
    twist_cos, twist_sin = root_table(index_b, index_a, length)
    twist_cos = twist_cos.reshape(length, 1)
    twist_sin = twist_sin.reshape(length, 1)
    row_scale_t = row_scale.reshape(size_b, size_a).T.reshape(length, 1)
    row_rate_t = row_rate.reshape(size_b, size_a).T.reshape(length, 1)
    vmem = pl.BlockSpec(memory_space=pltpu.VMEM)
    anywhere = pl.BlockSpec(memory_space=pl.ANY)
    shaped = spectrum.reshape(high, low, blocks, rows, both_width)
    latent, sums = pl.pallas_call(
        functools.partial(y_kernel, norm_factor),
        out_shape=(
            jax.ShapeDtypeStruct((2, size_b, size_a, width), jnp.float32),
            jax.ShapeDtypeStruct((8, 128), jnp.float32),
        ),
        in_specs=[vmem] * 11 + [anywhere],
        out_specs=(anywhere, vmem),
        scratch_shapes=[
            pltpu.VMEM((2, size_b, high, blocks, width), jnp.float32),
            pltpu.VMEM((2, length, width // 2), jnp.float32),
            pltpu.VMEM((2, length, width // 2), jnp.float32),
            pltpu.VMEM((2, size_a, size_b, width), jnp.float32),
            pltpu.SemaphoreType.DMA((2, size_b)),
            pltpu.SemaphoreType.DMA((2, size_a)),
        ],
        compiler_params=pltpu.CompilerParams(vmem_limit_bytes=60 * 1024 * 1024),
    )(
        cos_a, sin_a, twist_cos, twist_sin, cos_b, sin_b,
        row_scale_t, row_rate_t, col_scale.reshape(1, width), col_shift.reshape(1, width),
        col_mix.reshape(1, width), shaped,
    )
    return latent.reshape(2, length, width), sums

MESH_IDS = pl.DeviceIdType.MESH


def total_kernel(value_ref, out_ref, slots_a, slots_b, send_a, recv_a, send_b, recv_b):
    count_x = lax.axis_size("gx")
    count_y = lax.axis_size("gy")
    me_x = lax.axis_index("gx")
    me_y = lax.axis_index("gy")
    barrier = pltpu.get_barrier_semaphore()
    for step in range(1, count_x):
        pl.semaphore_signal(
            barrier, inc=1, device_id=((me_x + step) % count_x, me_y), device_id_type=MESH_IDS
        )
    for step in range(1, count_y):
        pl.semaphore_signal(
            barrier, inc=1, device_id=(me_x, (me_y + step) % count_y), device_id_type=MESH_IDS
        )
    slots_a[0] = value_ref[...]
    pl.semaphore_wait(barrier, count_x - 1 + count_y - 1)
    sends = []
    for step in range(1, count_x):
        copy = pltpu.make_async_remote_copy(
            src_ref=value_ref,
            dst_ref=slots_a.at[step],
            send_sem=send_a.at[step],
            recv_sem=recv_a.at[step],
            device_id=((me_x + step) % count_x, me_y),
            device_id_type=MESH_IDS,
        )
        copy.start()
        sends.append(copy)
    for copy in sends:
        copy.wait_recv()
    group_sum = slots_a[(me_x - 0) % count_x]
    for source in range(1, count_x):
        group_sum = group_sum + slots_a[(me_x - source + count_x) % count_x]
    slots_b[0] = group_sum
    later = []
    for step in range(1, count_y):
        copy = pltpu.make_async_remote_copy(
            src_ref=slots_b.at[0],
            dst_ref=slots_b.at[step],
            send_sem=send_b.at[step],
            recv_sem=recv_b.at[step],
            device_id=(me_x, (me_y + step) % count_y),
            device_id_type=MESH_IDS,
        )
        copy.start()
        later.append(copy)
    for copy in later:
        copy.wait_recv()
    grand = slots_b[(me_y - 0) % count_y]
    for source in range(1, count_y):
        grand = grand + slots_b[(me_y - source + count_y) % count_y]
    out_ref[...] = grand
    for copy in sends:
        copy.wait_send()
    for copy in later:
        copy.wait_send()


def total_everywhere(tile):
    count_x = lax.axis_size("gx")
    count_y = lax.axis_size("gy")
    result = pl.pallas_call(
        total_kernel,
        out_shape=jax.ShapeDtypeStruct((8, 128), jnp.float32),
        in_specs=[pl.BlockSpec(memory_space=pltpu.VMEM)],
        out_specs=pl.BlockSpec(memory_space=pltpu.VMEM),
        scratch_shapes=[
            pltpu.VMEM((count_x, 8, 128), jnp.float32),
            pltpu.VMEM((count_y, 8, 128), jnp.float32),
            pltpu.SemaphoreType.DMA((count_x,)),
            pltpu.SemaphoreType.DMA((count_x,)),
            pltpu.SemaphoreType.DMA((count_y,)),
            pltpu.SemaphoreType.DMA((count_y,)),
        ],
        compiler_params=pltpu.CompilerParams(collective_id=0, has_side_effects=True),
    )(tile)
    return result[0, 0]


def per_device(field, row_scale, col_scale, row_rate, col_shift, col_mix):
    devices = lax.axis_size("gx")
    planes, height, width = field.shape
    rows = height // devices
    outgoing = field.reshape(planes * devices, rows, width)
    incoming = lax.all_to_all(outgoing, ("gy", "gx"), split_axis=0, concat_axis=0, tiled=True)
    incoming = incoming.reshape(planes, devices, rows, width)
    both = x_stage(incoming)
    both = lax.all_to_all(both, "gx", split_axis=0, concat_axis=0, tiled=True)
    length = both.shape[0] * both.shape[1]
    total_cols = both.shape[2] // 2 * devices
    norm_factor = 1.0 / math.sqrt(length * total_cols)
    latent, part_sum = y_stage(
        both, row_scale, col_scale, row_rate, col_shift, col_mix, norm_factor, devices, height
    )
    total_sum = total_everywhere(part_sum)
    mode_count = length * total_cols * lax.axis_size("gy")
    loglik = total_sum / mode_count
    return (latent[:, None], loglik)


def solution(mesh):
    return jax.shard_map(
        per_device,
        mesh=mesh,
        in_specs=(P(None, "gy", "gx"), P(), P("gx"), P(), P("gx"), P("gx")),
        out_specs=(P(None, "gy", None, "gx"), P()),
        check_vma=False,
    )
```

```python
import functools
import math

import jax
import jax.numpy as jnp
from jax import lax
from jax.experimental import pallas as pl
from jax.experimental.pallas import tpu as pltpu
from jax.sharding import PartitionSpec as P

precision_top = lax.Precision.HIGHEST
precision_mid = lax.Precision.HIGH


def reverse_bits(value, count):
    result = value * 0
    for place in range(count):
        result = result + (value >> place & 1) * (1 << count - 1 - place)
    return result


def root_table(row_index, freqs, length):
    phase = row_index[:, None] * freqs[None, :] % length
    angle = phase.astype(jnp.float32) * (-2.0 * math.pi / length)
    return (jnp.cos(angle), jnp.sin(angle))


def complex_einsum(form, real_part, imag_part, cos_part, sin_part, precision=precision_top):
    first = jnp.einsum(form, real_part, cos_part, precision=precision)
    second = jnp.einsum(form, real_part, sin_part, precision=precision)
    first = first - jnp.einsum(form, imag_part, sin_part, precision=precision)
    second = second + jnp.einsum(form, imag_part, cos_part, precision=precision)
    return (first, second)


def x_stage(pieces):
    blocks, devices, rows, width = pieces.shape
    length = devices * width
    levels = devices.bit_length() - 1
    group = jnp.arange(devices, dtype=jnp.int32)
    residue = reverse_bits(group, levels)
    slices = [pieces[:, g].reshape(blocks * rows, width) for g in range(devices)]
    real_slots = []
    imag_slots = []
    for slot in range(devices):
        turn = sum(((slot >> place) & 1) << (levels - 1 - place) for place in range(levels))
        real_terms = []
        imag_terms = []
        for g in range(devices):
            phase = g * turn % devices
            angle = -2.0 * math.pi * phase / devices
            cos_value = 0.0 if phase * 4 % devices == 0 and phase * 4 // devices % 2 == 1 else math.cos(angle)
            sin_value = 0.0 if phase * 2 % devices == 0 else math.sin(angle)
            if cos_value != 0.0:
                real_terms.append(slices[g] * cos_value)
            if sin_value != 0.0:
                imag_terms.append(slices[g] * sin_value)
        real_slots.append(sum(real_terms[1:], real_terms[0]))
        imag_slots.append(
            sum(imag_terms[1:], imag_terms[0]) if imag_terms else jnp.zeros_like(slices[0])
        )
    part_real = jnp.stack(real_slots)
    part_imag = jnp.stack(imag_slots)
    local_index = jnp.arange(width, dtype=jnp.int32)
    freqs = residue[:, None] + devices * local_index[None, :]
    phase = local_index[None, :, None] * freqs[:, None, :] % length
    angle = phase.astype(jnp.float32) * (-2.0 * math.pi / length)
    cos_t = jnp.cos(angle)
    sin_t = jnp.sin(angle)
    from_real = jnp.concatenate([cos_t, sin_t], axis=2)
    from_imag = jnp.concatenate([-sin_t, cos_t], axis=2)
    spectrum = jnp.einsum("dyn,dnk->dyk", part_real, from_real, precision=precision_mid)
    spectrum = spectrum + jnp.einsum("dyn,dnk->dyk", part_imag, from_imag, precision=precision_mid)
    return spectrum


def y_transform(real_part, imag_part):
    planes, length, width = real_part.shape
    outer = 1 << (length.bit_length() - 1) // 2
    inner = length // outer
    outer_index = jnp.arange(outer, dtype=jnp.int32)
    inner_index = jnp.arange(inner, dtype=jnp.int32)
    cos_one, sin_one = root_table(outer_index, outer_index, outer)
    cos_two, sin_two = root_table(inner_index, inner_index, inner)
    cos_mid, sin_mid = root_table(outer_index, inner_index, length)
    shaped_real = real_part.reshape(planes, outer, inner, width)
    shaped_imag = imag_part.reshape(planes, outer, inner, width)
    step_real, step_imag = complex_einsum(
        "zabc,ak->zkbc", shaped_real, shaped_imag, cos_one, sin_one
    )
    twist_cos = cos_mid[None, :, :, None]
    twist_sin = sin_mid[None, :, :, None]
    turned_real = step_real * twist_cos - step_imag * twist_sin
    turned_imag = step_real * twist_sin + step_imag * twist_cos
    final_real, final_imag = complex_einsum(
        "zkbc,bj->zjkc", turned_real, turned_imag, cos_two, sin_two
    )
    return (final_real.reshape(planes, length, width), final_imag.reshape(planes, length, width))


def y_kernel(norm_factor, cos_a_ref, sin_a_ref, twist_cos_ref, twist_sin_ref,
             cos_b_ref, sin_b_ref, row_scale_ref, row_rate_ref, col_scale_ref, col_shift_ref,
             col_mix_ref, spectrum_hbm, out_hbm, sum_ref,
             held, step_real, step_imag, staged, in_sems, out_sems):
    high, low, blocks, rows, both_width = spectrum_hbm.shape
    width = both_width // 2
    size_b = low * rows
    size_a = high * blocks
    half = width // 2
    loads = []
    for part in range(2):
        for index in range(size_b):
            copy = pltpu.make_async_copy(
                spectrum_hbm.at[:, index // rows, :, index % rows, pl.ds(part * width, width)],
                held.at[part, index],
                in_sems.at[part, index],
            )
            copy.start()
            loads.append(copy)

    def dot(left, right):
        return jnp.dot(left, right, precision=precision_mid, preferred_element_type=jnp.float32)

    both_a = jnp.concatenate([cos_a_ref[...], sin_a_ref[...]], axis=0)

    def first(index, carry):
        for part in range(2):
            pltpu.make_async_copy(
                spectrum_hbm.at[:, index // rows, :, index % rows, pl.ds(part * width, width)],
                held.at[part, index],
                in_sems.at[part, index],
            ).wait()
        part_real = held[0, index].reshape(size_a, width)
        part_imag = held[1, index].reshape(size_a, width)
        from_real = dot(both_a, part_real)
        from_imag = dot(both_a, part_imag)
        out_real = from_real[:size_a] - from_imag[size_a:]
        out_imag = from_imag[:size_a] + from_real[size_a:]
        rows_here = pl.ds(pl.multiple_of(index * size_a, size_a), size_a)
        twist_cos = twist_cos_ref[rows_here, :]
        twist_sin = twist_sin_ref[rows_here, :]
        turned_real = out_real * twist_cos - out_imag * twist_sin
        turned_imag = out_real * twist_sin + out_imag * twist_cos
        for side in range(2):
            lanes = slice(side * half, (side + 1) * half)
            step_real[side, rows_here, :] = turned_real[:, lanes]
            step_imag[side, rows_here, :] = turned_imag[:, lanes]
        return carry

    lax.fori_loop(0, size_b, first, 0)

    col_scale = col_scale_ref[...]
    col_shift = col_shift_ref[...]
    col_mix = col_mix_ref[...]
    both_b = jnp.concatenate([cos_b_ref[...], sin_b_ref[...]], axis=0)

    def second(index, total):
        picked = pl.ds(index, size_b, stride=size_a)
        rows = pl.ds(pl.multiple_of(index * size_b, size_b), size_b)
        row_scale = row_scale_ref[rows, :]
        row_rate = row_rate_ref[rows, :]
        for side in range(2):
            lanes = slice(side * half, (side + 1) * half)
            part_real = step_real[side, picked, :]
            part_imag = step_imag[side, picked, :]
            from_real = dot(both_b, part_real)
            from_imag = dot(both_b, part_imag)
            spec_real = from_real[:size_b] - from_imag[size_b:]
            spec_imag = from_imag[:size_b] + from_real[size_b:]
            scale = row_scale * col_scale[:, lanes]
            latent_u = spec_real * norm_factor * scale
            latent_v = spec_imag * norm_factor * scale
            log_scale = row_rate * jnp.tanh(latent_u + col_shift[:, lanes])
            latent_w = latent_v * jnp.exp(log_scale) + col_mix[:, lanes] * latent_u
            terms = (
                -0.5 * (latent_u * latent_u + latent_w * latent_w)
                - math.log(2.0 * math.pi)
                + log_scale
                + 2.0 * jnp.log(scale)
            )
            staged[0, index, :, lanes] = latent_u
            staged[1, index, :, lanes] = latent_w
            total = total + terms
        for part in range(2):
            pltpu.make_async_copy(
                staged.at[part, index], out_hbm.at[part, :, index, :], out_sems.at[part, index]
            ).start()
        return total

    total = lax.fori_loop(0, size_a, second, jnp.zeros((size_b, half), jnp.float32))
    sum_ref[...] = jnp.broadcast_to(jnp.sum(total), sum_ref.shape)

    def finish(index, carry):
        for part in range(2):
            pltpu.make_async_copy(
                staged.at[part, index], out_hbm.at[part, :, index, :], out_sems.at[part, index]
            ).wait()
        return carry

    lax.fori_loop(0, size_a, finish, 0)


def y_stage(spectrum, row_scale, col_scale, row_rate, col_shift, col_mix, norm_factor, devices, height):
    _, count, both_width = spectrum.shape
    width = both_width // 2
    length = devices * count
    size_b = 1 << (length.bit_length() - 1) // 2
    size_a = length // size_b
    blocks = length // height
    rows = height // devices
    low = size_b // rows
    high = devices // low
    index_a = jnp.arange(size_a, dtype=jnp.int32)
    index_b = jnp.arange(size_b, dtype=jnp.int32)
    order_a = (index_a % blocks) * high + index_a // blocks
    cos_a, sin_a = root_table(index_a, order_a, size_a)
    cos_b, sin_b = root_table(index_b, index_b, size_b)
    twist_cos, twist_sin = root_table(index_b, index_a, length)
    twist_cos = twist_cos.reshape(length, 1)
    twist_sin = twist_sin.reshape(length, 1)
    row_scale_t = row_scale.reshape(size_b, size_a).T.reshape(length, 1)
    row_rate_t = row_rate.reshape(size_b, size_a).T.reshape(length, 1)
    vmem = pl.BlockSpec(memory_space=pltpu.VMEM)
    anywhere = pl.BlockSpec(memory_space=pl.ANY)
    shaped = spectrum.reshape(high, low, blocks, rows, both_width)
    latent, sums = pl.pallas_call(
        functools.partial(y_kernel, norm_factor),
        out_shape=(
            jax.ShapeDtypeStruct((2, size_b, size_a, width), jnp.float32),
            jax.ShapeDtypeStruct((8, 128), jnp.float32),
        ),
        in_specs=[vmem] * 11 + [anywhere],
        out_specs=(anywhere, vmem),
        scratch_shapes=[
            pltpu.VMEM((2, size_b, high, blocks, width), jnp.float32),
            pltpu.VMEM((2, length, width // 2), jnp.float32),
            pltpu.VMEM((2, length, width // 2), jnp.float32),
            pltpu.VMEM((2, size_a, size_b, width), jnp.float32),
            pltpu.SemaphoreType.DMA((2, size_b)),
            pltpu.SemaphoreType.DMA((2, size_a)),
        ],
        compiler_params=pltpu.CompilerParams(vmem_limit_bytes=60 * 1024 * 1024),
    )(
        cos_a, sin_a, twist_cos, twist_sin, cos_b, sin_b,
        row_scale_t, row_rate_t, col_scale.reshape(1, width), col_shift.reshape(1, width),
        col_mix.reshape(1, width), shaped,
    )
    return latent.reshape(2, length, width), sums

MESH_IDS = pl.DeviceIdType.MESH


def total_kernel(value_ref, out_ref, slots_a, slots_b, send_a, recv_a, send_b, recv_b):
    count_x = lax.axis_size("gx")
    count_y = lax.axis_size("gy")
    me_x = lax.axis_index("gx")
    me_y = lax.axis_index("gy")
    barrier = pltpu.get_barrier_semaphore()
    for step in range(1, count_x):
        pl.semaphore_signal(
            barrier, inc=1, device_id=((me_x + step) % count_x, me_y), device_id_type=MESH_IDS
        )
    for step in range(1, count_y):
        pl.semaphore_signal(
            barrier, inc=1, device_id=(me_x, (me_y + step) % count_y), device_id_type=MESH_IDS
        )
    slots_a[0] = value_ref[...]
    pl.semaphore_wait(barrier, count_x - 1 + count_y - 1)
    sends = []
    for step in range(1, count_x):
        copy = pltpu.make_async_remote_copy(
            src_ref=value_ref,
            dst_ref=slots_a.at[step],
            send_sem=send_a.at[step],
            recv_sem=recv_a.at[step],
            device_id=((me_x + step) % count_x, me_y),
            device_id_type=MESH_IDS,
        )
        copy.start()
        sends.append(copy)
    for copy in sends:
        copy.wait_recv()
    group_sum = slots_a[(me_x - 0) % count_x]
    for source in range(1, count_x):
        group_sum = group_sum + slots_a[(me_x - source + count_x) % count_x]
    slots_b[0] = group_sum
    later = []
    for step in range(1, count_y):
        copy = pltpu.make_async_remote_copy(
            src_ref=slots_b.at[0],
            dst_ref=slots_b.at[step],
            send_sem=send_b.at[step],
            recv_sem=recv_b.at[step],
            device_id=(me_x, (me_y + step) % count_y),
            device_id_type=MESH_IDS,
        )
        copy.start()
        later.append(copy)
    for copy in later:
        copy.wait_recv()
    grand = slots_b[(me_y - 0) % count_y]
    for source in range(1, count_y):
        grand = grand + slots_b[(me_y - source + count_y) % count_y]
    out_ref[...] = grand
    for copy in sends:
        copy.wait_send()
    for copy in later:
        copy.wait_send()


def total_everywhere(tile):
    count_x = lax.axis_size("gx")
    count_y = lax.axis_size("gy")
    result = pl.pallas_call(
        total_kernel,
        out_shape=jax.ShapeDtypeStruct((8, 128), jnp.float32),
        in_specs=[pl.BlockSpec(memory_space=pltpu.VMEM)],
        out_specs=pl.BlockSpec(memory_space=pltpu.VMEM),
        scratch_shapes=[
            pltpu.VMEM((count_x, 8, 128), jnp.float32),
            pltpu.VMEM((count_y, 8, 128), jnp.float32),
            pltpu.SemaphoreType.DMA((count_x,)),
            pltpu.SemaphoreType.DMA((count_x,)),
            pltpu.SemaphoreType.DMA((count_y,)),
            pltpu.SemaphoreType.DMA((count_y,)),
        ],
        compiler_params=pltpu.CompilerParams(collective_id=0, has_side_effects=True),
    )(tile)
    return result[0, 0]


def per_device(field, row_scale, col_scale, row_rate, col_shift, col_mix):
    devices = lax.axis_size("gx")
    planes, height, width = field.shape
    rows = height // devices
    outgoing = field.reshape(planes * devices, rows, width)
    incoming = lax.all_to_all(outgoing, ("gy", "gx"), split_axis=0, concat_axis=0, tiled=True)
    incoming = incoming.reshape(planes, devices, rows, width)
    both = x_stage(incoming)
    both = lax.all_to_all(both, "gx", split_axis=0, concat_axis=0, tiled=True)
    length = both.shape[0] * both.shape[1]
    total_cols = both.shape[2] // 2 * devices
    norm_factor = 1.0 / math.sqrt(length * total_cols)
    latent, part_sum = y_stage(
        both, row_scale, col_scale, row_rate, col_shift, col_mix, norm_factor, devices, height
    )
    total_sum = total_everywhere(part_sum)
    mode_count = length * total_cols * lax.axis_size("gy")
    loglik = total_sum / mode_count
    return (latent[:, None], loglik)


def solution(mesh):
    return jax.shard_map(
        per_device,
        mesh=mesh,
        in_specs=(P(None, "gy", "gx"), P(), P("gx"), P(), P("gx"), P("gx")),
        out_specs=(P(None, "gy", None, "gx"), P()),
        check_vma=False,
    )
```

```python
import functools
import math

import jax
import jax.numpy as jnp
from jax import lax
from jax.experimental import pallas as pl
from jax.experimental.pallas import tpu as pltpu
from jax.sharding import PartitionSpec as P

precision_top = lax.Precision.HIGHEST
precision_mid = lax.Precision.HIGH


def reverse_bits(value, count):
    result = value * 0
    for place in range(count):
        result = result + (value >> place & 1) * (1 << count - 1 - place)
    return result


def root_table(row_index, freqs, length):
    phase = row_index[:, None] * freqs[None, :] % length
    angle = phase.astype(jnp.float32) * (-2.0 * math.pi / length)
    return (jnp.cos(angle), jnp.sin(angle))


def complex_einsum(form, real_part, imag_part, cos_part, sin_part, precision=precision_top):
    first = jnp.einsum(form, real_part, cos_part, precision=precision)
    second = jnp.einsum(form, real_part, sin_part, precision=precision)
    first = first - jnp.einsum(form, imag_part, sin_part, precision=precision)
    second = second + jnp.einsum(form, imag_part, cos_part, precision=precision)
    return (first, second)


def x_stage(pieces):
    blocks, devices, rows, width = pieces.shape
    length = devices * width
    levels = devices.bit_length() - 1
    group = jnp.arange(devices, dtype=jnp.int32)
    residue = reverse_bits(group, levels)
    slices = [pieces[:, g].reshape(blocks * rows, width) for g in range(devices)]
    real_slots = []
    imag_slots = []
    for slot in range(devices):
        turn = sum(((slot >> place) & 1) << (levels - 1 - place) for place in range(levels))
        real_terms = []
        imag_terms = []
        for g in range(devices):
            phase = g * turn % devices
            angle = -2.0 * math.pi * phase / devices
            cos_value = 0.0 if phase * 4 % devices == 0 and phase * 4 // devices % 2 == 1 else math.cos(angle)
            sin_value = 0.0 if phase * 2 % devices == 0 else math.sin(angle)
            if cos_value != 0.0:
                real_terms.append(slices[g] * cos_value)
            if sin_value != 0.0:
                imag_terms.append(slices[g] * sin_value)
        real_slots.append(sum(real_terms[1:], real_terms[0]))
        imag_slots.append(
            sum(imag_terms[1:], imag_terms[0]) if imag_terms else jnp.zeros_like(slices[0])
        )
    parts = jnp.stack(
        [jnp.concatenate([re, im], axis=1) for re, im in zip(real_slots, imag_slots)]
    )
    local_index = jnp.arange(width, dtype=jnp.int32)
    freqs = residue[:, None] + devices * local_index[None, :]
    phase = local_index[None, :, None] * freqs[:, None, :] % length
    angle = phase.astype(jnp.float32) * (-2.0 * math.pi / length)
    cos_t = jnp.cos(angle)
    sin_t = jnp.sin(angle)
    from_real = jnp.concatenate([cos_t, sin_t], axis=2)
    from_imag = jnp.concatenate([-sin_t, cos_t], axis=2)
    table = jnp.concatenate([from_real, from_imag], axis=1)
    spectrum = jnp.einsum("dyn,dnk->dyk", parts, table, precision=precision_mid)
    return spectrum


def y_transform(real_part, imag_part):
    planes, length, width = real_part.shape
    outer = 1 << (length.bit_length() - 1) // 2
    inner = length // outer
    outer_index = jnp.arange(outer, dtype=jnp.int32)
    inner_index = jnp.arange(inner, dtype=jnp.int32)
    cos_one, sin_one = root_table(outer_index, outer_index, outer)
    cos_two, sin_two = root_table(inner_index, inner_index, inner)
    cos_mid, sin_mid = root_table(outer_index, inner_index, length)
    shaped_real = real_part.reshape(planes, outer, inner, width)
    shaped_imag = imag_part.reshape(planes, outer, inner, width)
    step_real, step_imag = complex_einsum(
        "zabc,ak->zkbc", shaped_real, shaped_imag, cos_one, sin_one
    )
    twist_cos = cos_mid[None, :, :, None]
    twist_sin = sin_mid[None, :, :, None]
    turned_real = step_real * twist_cos - step_imag * twist_sin
    turned_imag = step_real * twist_sin + step_imag * twist_cos
    final_real, final_imag = complex_einsum(
        "zkbc,bj->zjkc", turned_real, turned_imag, cos_two, sin_two
    )
    return (final_real.reshape(planes, length, width), final_imag.reshape(planes, length, width))


def y_kernel(norm_factor, cos_a_ref, sin_a_ref, twist_cos_ref, twist_sin_ref,
             cos_b_ref, sin_b_ref, row_scale_ref, row_rate_ref, col_scale_ref, col_shift_ref,
             col_mix_ref, spectrum_hbm, out_hbm, sum_ref,
             held, step_real, step_imag, staged, in_sems, out_sems):
    high, low, blocks, rows, both_width = spectrum_hbm.shape
    width = both_width // 2
    size_b = low * rows
    size_a = high * blocks
    half = width // 2
    loads = []
    for part in range(2):
        for index in range(size_b):
            copy = pltpu.make_async_copy(
                spectrum_hbm.at[:, index // rows, :, index % rows, pl.ds(part * width, width)],
                held.at[part, index],
                in_sems.at[part, index],
            )
            copy.start()
            loads.append(copy)

    def dot(left, right):
        return jnp.dot(left, right, precision=precision_mid, preferred_element_type=jnp.float32)

    both_a = jnp.concatenate([cos_a_ref[...], sin_a_ref[...]], axis=0)

    def first(index, carry):
        for part in range(2):
            pltpu.make_async_copy(
                spectrum_hbm.at[:, index // rows, :, index % rows, pl.ds(part * width, width)],
                held.at[part, index],
                in_sems.at[part, index],
            ).wait()
        part_real = held[0, index].reshape(size_a, width)
        part_imag = held[1, index].reshape(size_a, width)
        from_real = dot(both_a, part_real)
        from_imag = dot(both_a, part_imag)
        out_real = from_real[:size_a] - from_imag[size_a:]
        out_imag = from_imag[:size_a] + from_real[size_a:]
        rows_here = pl.ds(pl.multiple_of(index * size_a, size_a), size_a)
        twist_cos = twist_cos_ref[rows_here, :]
        twist_sin = twist_sin_ref[rows_here, :]
        turned_real = out_real * twist_cos - out_imag * twist_sin
        turned_imag = out_real * twist_sin + out_imag * twist_cos
        for side in range(2):
            lanes = slice(side * half, (side + 1) * half)
            step_real[side, rows_here, :] = turned_real[:, lanes]
            step_imag[side, rows_here, :] = turned_imag[:, lanes]
        return carry

    lax.fori_loop(0, size_b, first, 0)

    col_scale = col_scale_ref[...]
    col_shift = col_shift_ref[...]
    col_mix = col_mix_ref[...]
    both_b = jnp.concatenate([cos_b_ref[...], sin_b_ref[...]], axis=0)

    def second(index, total):
        picked = pl.ds(index, size_b, stride=size_a)
        rows = pl.ds(pl.multiple_of(index * size_b, size_b), size_b)
        row_scale = row_scale_ref[rows, :]
        row_rate = row_rate_ref[rows, :]
        for side in range(2):
            lanes = slice(side * half, (side + 1) * half)
            part_real = step_real[side, picked, :]
            part_imag = step_imag[side, picked, :]
            from_real = dot(both_b, part_real)
            from_imag = dot(both_b, part_imag)
            spec_real = from_real[:size_b] - from_imag[size_b:]
            spec_imag = from_imag[:size_b] + from_real[size_b:]
            scale = row_scale * col_scale[:, lanes]
            latent_u = spec_real * norm_factor * scale
            latent_v = spec_imag * norm_factor * scale
            log_scale = row_rate * jnp.tanh(latent_u + col_shift[:, lanes])
            latent_w = latent_v * jnp.exp(log_scale) + col_mix[:, lanes] * latent_u
            terms = (
                -0.5 * (latent_u * latent_u + latent_w * latent_w)
                - math.log(2.0 * math.pi)
                + log_scale
                + 2.0 * jnp.log(scale)
            )
            staged[0, index, :, lanes] = latent_u
            staged[1, index, :, lanes] = latent_w
            total = total + terms
        for part in range(2):
            pltpu.make_async_copy(
                staged.at[part, index], out_hbm.at[part, :, index, :], out_sems.at[part, index]
            ).start()
        return total

    total = lax.fori_loop(0, size_a, second, jnp.zeros((size_b, half), jnp.float32))
    sum_ref[...] = jnp.broadcast_to(jnp.sum(total), sum_ref.shape)

    def finish(index, carry):
        for part in range(2):
            pltpu.make_async_copy(
                staged.at[part, index], out_hbm.at[part, :, index, :], out_sems.at[part, index]
            ).wait()
        return carry

    lax.fori_loop(0, size_a, finish, 0)


def y_stage(spectrum, row_scale, col_scale, row_rate, col_shift, col_mix, norm_factor, devices, height):
    _, count, both_width = spectrum.shape
    width = both_width // 2
    length = devices * count
    size_b = 1 << (length.bit_length() - 1) // 2
    size_a = length // size_b
    blocks = length // height
    rows = height // devices
    low = size_b // rows
    high = devices // low
    index_a = jnp.arange(size_a, dtype=jnp.int32)
    index_b = jnp.arange(size_b, dtype=jnp.int32)
    order_a = (index_a % blocks) * high + index_a // blocks
    cos_a, sin_a = root_table(index_a, order_a, size_a)
    cos_b, sin_b = root_table(index_b, index_b, size_b)
    twist_cos, twist_sin = root_table(index_b, index_a, length)
    twist_cos = twist_cos.reshape(length, 1)
    twist_sin = twist_sin.reshape(length, 1)
    row_scale_t = row_scale.reshape(size_b, size_a).T.reshape(length, 1)
    row_rate_t = row_rate.reshape(size_b, size_a).T.reshape(length, 1)
    vmem = pl.BlockSpec(memory_space=pltpu.VMEM)
    anywhere = pl.BlockSpec(memory_space=pl.ANY)
    shaped = spectrum.reshape(high, low, blocks, rows, both_width)
    latent, sums = pl.pallas_call(
        functools.partial(y_kernel, norm_factor),
        out_shape=(
            jax.ShapeDtypeStruct((2, size_b, size_a, width), jnp.float32),
            jax.ShapeDtypeStruct((8, 128), jnp.float32),
        ),
        in_specs=[vmem] * 11 + [anywhere],
        out_specs=(anywhere, vmem),
        scratch_shapes=[
            pltpu.VMEM((2, size_b, high, blocks, width), jnp.float32),
            pltpu.VMEM((2, length, width // 2), jnp.float32),
            pltpu.VMEM((2, length, width // 2), jnp.float32),
            pltpu.VMEM((2, size_a, size_b, width), jnp.float32),
            pltpu.SemaphoreType.DMA((2, size_b)),
            pltpu.SemaphoreType.DMA((2, size_a)),
        ],
        compiler_params=pltpu.CompilerParams(vmem_limit_bytes=60 * 1024 * 1024),
    )(
        cos_a, sin_a, twist_cos, twist_sin, cos_b, sin_b,
        row_scale_t, row_rate_t, col_scale.reshape(1, width), col_shift.reshape(1, width),
        col_mix.reshape(1, width), shaped,
    )
    return latent.reshape(2, length, width), sums

MESH_IDS = pl.DeviceIdType.MESH


def total_kernel(value_ref, out_ref, slots_a, slots_b, send_a, recv_a, send_b, recv_b):
    count_x = lax.axis_size("gx")
    count_y = lax.axis_size("gy")
    me_x = lax.axis_index("gx")
    me_y = lax.axis_index("gy")
    barrier = pltpu.get_barrier_semaphore()
    for step in range(1, count_x):
        pl.semaphore_signal(
            barrier, inc=1, device_id=((me_x + step) % count_x, me_y), device_id_type=MESH_IDS
        )
    for step in range(1, count_y):
        pl.semaphore_signal(
            barrier, inc=1, device_id=(me_x, (me_y + step) % count_y), device_id_type=MESH_IDS
        )
    slots_a[0] = value_ref[...]
    pl.semaphore_wait(barrier, count_x - 1 + count_y - 1)
    sends = []
    for step in range(1, count_x):
        copy = pltpu.make_async_remote_copy(
            src_ref=value_ref,
            dst_ref=slots_a.at[step],
            send_sem=send_a.at[step],
            recv_sem=recv_a.at[step],
            device_id=((me_x + step) % count_x, me_y),
            device_id_type=MESH_IDS,
        )
        copy.start()
        sends.append(copy)
    for copy in sends:
        copy.wait_recv()
    group_sum = slots_a[(me_x - 0) % count_x]
    for source in range(1, count_x):
        group_sum = group_sum + slots_a[(me_x - source + count_x) % count_x]
    slots_b[0] = group_sum
    later = []
    for step in range(1, count_y):
        copy = pltpu.make_async_remote_copy(
            src_ref=slots_b.at[0],
            dst_ref=slots_b.at[step],
            send_sem=send_b.at[step],
            recv_sem=recv_b.at[step],
            device_id=(me_x, (me_y + step) % count_y),
            device_id_type=MESH_IDS,
        )
        copy.start()
        later.append(copy)
    for copy in later:
        copy.wait_recv()
    grand = slots_b[(me_y - 0) % count_y]
    for source in range(1, count_y):
        grand = grand + slots_b[(me_y - source + count_y) % count_y]
    out_ref[...] = grand
    for copy in sends:
        copy.wait_send()
    for copy in later:
        copy.wait_send()


def total_everywhere(tile):
    count_x = lax.axis_size("gx")
    count_y = lax.axis_size("gy")
    result = pl.pallas_call(
        total_kernel,
        out_shape=jax.ShapeDtypeStruct((8, 128), jnp.float32),
        in_specs=[pl.BlockSpec(memory_space=pltpu.VMEM)],
        out_specs=pl.BlockSpec(memory_space=pltpu.VMEM),
        scratch_shapes=[
            pltpu.VMEM((count_x, 8, 128), jnp.float32),
            pltpu.VMEM((count_y, 8, 128), jnp.float32),
            pltpu.SemaphoreType.DMA((count_x,)),
            pltpu.SemaphoreType.DMA((count_x,)),
            pltpu.SemaphoreType.DMA((count_y,)),
            pltpu.SemaphoreType.DMA((count_y,)),
        ],
        compiler_params=pltpu.CompilerParams(collective_id=0, has_side_effects=True),
    )(tile)
    return result[0, 0]


def per_device(field, row_scale, col_scale, row_rate, col_shift, col_mix):
    devices = lax.axis_size("gx")
    planes, height, width = field.shape
    rows = height // devices
    outgoing = field.reshape(planes * devices, rows, width)
    incoming = lax.all_to_all(outgoing, ("gy", "gx"), split_axis=0, concat_axis=0, tiled=True)
    incoming = incoming.reshape(planes, devices, rows, width)
    both = x_stage(incoming)
    both = lax.all_to_all(both, "gx", split_axis=0, concat_axis=0, tiled=True)
    length = both.shape[0] * both.shape[1]
    total_cols = both.shape[2] // 2 * devices
    norm_factor = 1.0 / math.sqrt(length * total_cols)
    latent, part_sum = y_stage(
        both, row_scale, col_scale, row_rate, col_shift, col_mix, norm_factor, devices, height
    )
    total_sum = total_everywhere(part_sum)
    mode_count = length * total_cols * lax.axis_size("gy")
    loglik = total_sum / mode_count
    return (latent[:, None], loglik)


def solution(mesh):
    return jax.shard_map(
        per_device,
        mesh=mesh,
        in_specs=(P(None, "gy", "gx"), P(), P("gx"), P(), P("gx"), P("gx")),
        out_specs=(P(None, "gy", None, "gx"), P()),
        check_vma=False,
    )
```

```python
import functools
import math

import jax
import jax.numpy as jnp
from jax import lax
from jax.experimental import pallas as pl
from jax.experimental.pallas import tpu as pltpu
from jax.sharding import PartitionSpec as P

precision_top = lax.Precision.HIGHEST
precision_mid = lax.Precision.HIGH


def reverse_bits(value, count):
    result = value * 0
    for place in range(count):
        result = result + (value >> place & 1) * (1 << count - 1 - place)
    return result


def root_table(row_index, freqs, length):
    phase = row_index[:, None] * freqs[None, :] % length
    angle = phase.astype(jnp.float32) * (-2.0 * math.pi / length)
    return (jnp.cos(angle), jnp.sin(angle))


def complex_einsum(form, real_part, imag_part, cos_part, sin_part, precision=precision_top):
    first = jnp.einsum(form, real_part, cos_part, precision=precision)
    second = jnp.einsum(form, real_part, sin_part, precision=precision)
    first = first - jnp.einsum(form, imag_part, sin_part, precision=precision)
    second = second + jnp.einsum(form, imag_part, cos_part, precision=precision)
    return (first, second)


def x_stage(pieces):
    blocks, devices, rows, width = pieces.shape
    length = devices * width
    levels = devices.bit_length() - 1
    group = jnp.arange(devices, dtype=jnp.int32)
    residue = reverse_bits(group, levels)
    slices = [pieces[:, g].reshape(blocks * rows, width) for g in range(devices)]
    real_slots = []
    imag_slots = []
    for slot in range(devices):
        turn = sum(((slot >> place) & 1) << (levels - 1 - place) for place in range(levels))
        real_terms = []
        imag_terms = []
        for g in range(devices):
            phase = g * turn % devices
            angle = -2.0 * math.pi * phase / devices
            cos_value = 0.0 if phase * 4 % devices == 0 and phase * 4 // devices % 2 == 1 else math.cos(angle)
            sin_value = 0.0 if phase * 2 % devices == 0 else math.sin(angle)
            if cos_value != 0.0:
                real_terms.append(slices[g] * cos_value)
            if sin_value != 0.0:
                imag_terms.append(slices[g] * sin_value)
        real_slots.append(sum(real_terms[1:], real_terms[0]))
        imag_slots.append(
            sum(imag_terms[1:], imag_terms[0]) if imag_terms else jnp.zeros_like(slices[0])
        )
    parts = jnp.stack(
        [jnp.concatenate([re, im], axis=1) for re, im in zip(real_slots, imag_slots)]
    )
    local_index = jnp.arange(width, dtype=jnp.int32)
    freqs = residue[:, None] + devices * local_index[None, :]
    phase = local_index[None, :, None] * freqs[:, None, :] % length
    angle = phase.astype(jnp.float32) * (-2.0 * math.pi / length)
    cos_t = jnp.cos(angle)
    sin_t = jnp.sin(angle)
    from_real = jnp.concatenate([cos_t, sin_t], axis=2)
    from_imag = jnp.concatenate([-sin_t, cos_t], axis=2)
    table = jnp.concatenate([from_real, from_imag], axis=1)
    spectrum = jnp.einsum("dyn,dnk->dyk", parts, table, precision=precision_mid)
    return spectrum


def y_transform(real_part, imag_part):
    planes, length, width = real_part.shape
    outer = 1 << (length.bit_length() - 1) // 2
    inner = length // outer
    outer_index = jnp.arange(outer, dtype=jnp.int32)
    inner_index = jnp.arange(inner, dtype=jnp.int32)
    cos_one, sin_one = root_table(outer_index, outer_index, outer)
    cos_two, sin_two = root_table(inner_index, inner_index, inner)
    cos_mid, sin_mid = root_table(outer_index, inner_index, length)
    shaped_real = real_part.reshape(planes, outer, inner, width)
    shaped_imag = imag_part.reshape(planes, outer, inner, width)
    step_real, step_imag = complex_einsum(
        "zabc,ak->zkbc", shaped_real, shaped_imag, cos_one, sin_one
    )
    twist_cos = cos_mid[None, :, :, None]
    twist_sin = sin_mid[None, :, :, None]
    turned_real = step_real * twist_cos - step_imag * twist_sin
    turned_imag = step_real * twist_sin + step_imag * twist_cos
    final_real, final_imag = complex_einsum(
        "zkbc,bj->zjkc", turned_real, turned_imag, cos_two, sin_two
    )
    return (final_real.reshape(planes, length, width), final_imag.reshape(planes, length, width))


def y_kernel(norm_factor, cos_a_ref, sin_a_ref, twist_cos_ref, twist_sin_ref,
             cos_b_ref, sin_b_ref, row_scale_ref, row_rate_ref, col_scale_ref, col_shift_ref,
             col_mix_ref, spectrum_hbm, out_hbm, sum_ref,
             held, step_real, step_imag, staged, in_sems, out_sems):
    high, low, blocks, rows, both_width = spectrum_hbm.shape
    width = both_width // 2
    size_b = low * rows
    size_a = high * blocks
    half = width // 2
    loads = []
    for part in range(2):
        for index in range(size_b):
            copy = pltpu.make_async_copy(
                spectrum_hbm.at[:, index // rows, :, index % rows, pl.ds(part * width, width)],
                held.at[part, index],
                in_sems.at[part, index],
            )
            copy.start()
            loads.append(copy)

    def dot(left, right):
        return jnp.dot(left, right, precision=precision_mid, preferred_element_type=jnp.float32)

    cos_a = cos_a_ref[...]
    sin_a = sin_a_ref[...]
    both_a = jnp.concatenate(
        [jnp.concatenate([cos_a, -sin_a], axis=1), jnp.concatenate([sin_a, cos_a], axis=1)], axis=0
    )

    def first(index, carry):
        for part in range(2):
            pltpu.make_async_copy(
                spectrum_hbm.at[:, index // rows, :, index % rows, pl.ds(part * width, width)],
                held.at[part, index],
                in_sems.at[part, index],
            ).wait()
        part = jnp.concatenate(
            [held[0, index].reshape(size_a, width), held[1, index].reshape(size_a, width)], axis=0
        )
        result = dot(both_a, part)
        out_real = result[:size_a]
        out_imag = result[size_a:]
        rows_here = pl.ds(pl.multiple_of(index * size_a, size_a), size_a)
        twist_cos = twist_cos_ref[rows_here, :]
        twist_sin = twist_sin_ref[rows_here, :]
        turned_real = out_real * twist_cos - out_imag * twist_sin
        turned_imag = out_real * twist_sin + out_imag * twist_cos
        for side in range(2):
            lanes = slice(side * half, (side + 1) * half)
            step_real[side, rows_here, :] = turned_real[:, lanes]
            step_imag[side, rows_here, :] = turned_imag[:, lanes]
        return carry

    lax.fori_loop(0, size_b, first, 0)

    col_scale = col_scale_ref[...]
    col_shift = col_shift_ref[...]
    col_mix = col_mix_ref[...]
    cos_b = cos_b_ref[...]
    sin_b = sin_b_ref[...]
    both_b = jnp.concatenate(
        [jnp.concatenate([cos_b, -sin_b], axis=1), jnp.concatenate([sin_b, cos_b], axis=1)], axis=0
    )

    def second(index, total):
        picked = pl.ds(index, size_b, stride=size_a)
        rows = pl.ds(pl.multiple_of(index * size_b, size_b), size_b)
        row_scale = row_scale_ref[rows, :]
        row_rate = row_rate_ref[rows, :]
        for side in range(2):
            lanes = slice(side * half, (side + 1) * half)
            part = jnp.concatenate([step_real[side, picked, :], step_imag[side, picked, :]], axis=0)
            result = dot(both_b, part)
            spec_real = result[:size_b]
            spec_imag = result[size_b:]
            scale = row_scale * col_scale[:, lanes]
            latent_u = spec_real * norm_factor * scale
            latent_v = spec_imag * norm_factor * scale
            log_scale = row_rate * jnp.tanh(latent_u + col_shift[:, lanes])
            latent_w = latent_v * jnp.exp(log_scale) + col_mix[:, lanes] * latent_u
            terms = (
                -0.5 * (latent_u * latent_u + latent_w * latent_w)
                - math.log(2.0 * math.pi)
                + log_scale
                + 2.0 * jnp.log(scale)
            )
            staged[0, index, :, lanes] = latent_u
            staged[1, index, :, lanes] = latent_w
            total = total + terms
        for part in range(2):
            pltpu.make_async_copy(
                staged.at[part, index], out_hbm.at[part, :, index, :], out_sems.at[part, index]
            ).start()
        return total

    total = lax.fori_loop(0, size_a, second, jnp.zeros((size_b, half), jnp.float32))
    sum_ref[...] = jnp.broadcast_to(jnp.sum(total), sum_ref.shape)

    def finish(index, carry):
        for part in range(2):
            pltpu.make_async_copy(
                staged.at[part, index], out_hbm.at[part, :, index, :], out_sems.at[part, index]
            ).wait()
        return carry

    lax.fori_loop(0, size_a, finish, 0)


def y_stage(spectrum, row_scale, col_scale, row_rate, col_shift, col_mix, norm_factor, devices, height):
    _, count, both_width = spectrum.shape
    width = both_width // 2
    length = devices * count
    size_b = 1 << (length.bit_length() - 1) // 2
    size_a = length // size_b
    blocks = length // height
    rows = height // devices
    low = size_b // rows
    high = devices // low
    index_a = jnp.arange(size_a, dtype=jnp.int32)
    index_b = jnp.arange(size_b, dtype=jnp.int32)
    order_a = (index_a % blocks) * high + index_a // blocks
    cos_a, sin_a = root_table(index_a, order_a, size_a)
    cos_b, sin_b = root_table(index_b, index_b, size_b)
    twist_cos, twist_sin = root_table(index_b, index_a, length)
    twist_cos = twist_cos.reshape(length, 1)
    twist_sin = twist_sin.reshape(length, 1)
    row_scale_t = row_scale.reshape(size_b, size_a).T.reshape(length, 1)
    row_rate_t = row_rate.reshape(size_b, size_a).T.reshape(length, 1)
    vmem = pl.BlockSpec(memory_space=pltpu.VMEM)
    anywhere = pl.BlockSpec(memory_space=pl.ANY)
    shaped = spectrum.reshape(high, low, blocks, rows, both_width)
    latent, sums = pl.pallas_call(
        functools.partial(y_kernel, norm_factor),
        out_shape=(
            jax.ShapeDtypeStruct((2, size_b, size_a, width), jnp.float32),
            jax.ShapeDtypeStruct((8, 128), jnp.float32),
        ),
        in_specs=[vmem] * 11 + [anywhere],
        out_specs=(anywhere, vmem),
        scratch_shapes=[
            pltpu.VMEM((2, size_b, high, blocks, width), jnp.float32),
            pltpu.VMEM((2, length, width // 2), jnp.float32),
            pltpu.VMEM((2, length, width // 2), jnp.float32),
            pltpu.VMEM((2, size_a, size_b, width), jnp.float32),
            pltpu.SemaphoreType.DMA((2, size_b)),
            pltpu.SemaphoreType.DMA((2, size_a)),
        ],
        compiler_params=pltpu.CompilerParams(vmem_limit_bytes=60 * 1024 * 1024),
    )(
        cos_a, sin_a, twist_cos, twist_sin, cos_b, sin_b,
        row_scale_t, row_rate_t, col_scale.reshape(1, width), col_shift.reshape(1, width),
        col_mix.reshape(1, width), shaped,
    )
    return latent.reshape(2, length, width), sums

MESH_IDS = pl.DeviceIdType.MESH


def total_kernel(value_ref, out_ref, slots_a, slots_b, send_a, recv_a, send_b, recv_b):
    count_x = lax.axis_size("gx")
    count_y = lax.axis_size("gy")
    me_x = lax.axis_index("gx")
    me_y = lax.axis_index("gy")
    barrier = pltpu.get_barrier_semaphore()
    for step in range(1, count_x):
        pl.semaphore_signal(
            barrier, inc=1, device_id=((me_x + step) % count_x, me_y), device_id_type=MESH_IDS
        )
    for step in range(1, count_y):
        pl.semaphore_signal(
            barrier, inc=1, device_id=(me_x, (me_y + step) % count_y), device_id_type=MESH_IDS
        )
    slots_a[0] = value_ref[...]
    pl.semaphore_wait(barrier, count_x - 1 + count_y - 1)
    sends = []
    for step in range(1, count_x):
        copy = pltpu.make_async_remote_copy(
            src_ref=value_ref,
            dst_ref=slots_a.at[step],
            send_sem=send_a.at[step],
            recv_sem=recv_a.at[step],
            device_id=((me_x + step) % count_x, me_y),
            device_id_type=MESH_IDS,
        )
        copy.start()
        sends.append(copy)
    for copy in sends:
        copy.wait_recv()
    group_sum = slots_a[(me_x - 0) % count_x]
    for source in range(1, count_x):
        group_sum = group_sum + slots_a[(me_x - source + count_x) % count_x]
    slots_b[0] = group_sum
    later = []
    for step in range(1, count_y):
        copy = pltpu.make_async_remote_copy(
            src_ref=slots_b.at[0],
            dst_ref=slots_b.at[step],
            send_sem=send_b.at[step],
            recv_sem=recv_b.at[step],
            device_id=(me_x, (me_y + step) % count_y),
            device_id_type=MESH_IDS,
        )
        copy.start()
        later.append(copy)
    for copy in later:
        copy.wait_recv()
    grand = slots_b[(me_y - 0) % count_y]
    for source in range(1, count_y):
        grand = grand + slots_b[(me_y - source + count_y) % count_y]
    out_ref[...] = grand
    for copy in sends:
        copy.wait_send()
    for copy in later:
        copy.wait_send()


def total_everywhere(tile):
    count_x = lax.axis_size("gx")
    count_y = lax.axis_size("gy")
    result = pl.pallas_call(
        total_kernel,
        out_shape=jax.ShapeDtypeStruct((8, 128), jnp.float32),
        in_specs=[pl.BlockSpec(memory_space=pltpu.VMEM)],
        out_specs=pl.BlockSpec(memory_space=pltpu.VMEM),
        scratch_shapes=[
            pltpu.VMEM((count_x, 8, 128), jnp.float32),
            pltpu.VMEM((count_y, 8, 128), jnp.float32),
            pltpu.SemaphoreType.DMA((count_x,)),
            pltpu.SemaphoreType.DMA((count_x,)),
            pltpu.SemaphoreType.DMA((count_y,)),
            pltpu.SemaphoreType.DMA((count_y,)),
        ],
        compiler_params=pltpu.CompilerParams(collective_id=0, has_side_effects=True),
    )(tile)
    return result[0, 0]


def per_device(field, row_scale, col_scale, row_rate, col_shift, col_mix):
    devices = lax.axis_size("gx")
    planes, height, width = field.shape
    rows = height // devices
    outgoing = field.reshape(planes * devices, rows, width)
    incoming = lax.all_to_all(outgoing, ("gy", "gx"), split_axis=0, concat_axis=0, tiled=True)
    incoming = incoming.reshape(planes, devices, rows, width)
    both = x_stage(incoming)
    both = lax.all_to_all(both, "gx", split_axis=0, concat_axis=0, tiled=True)
    length = both.shape[0] * both.shape[1]
    total_cols = both.shape[2] // 2 * devices
    norm_factor = 1.0 / math.sqrt(length * total_cols)
    latent, part_sum = y_stage(
        both, row_scale, col_scale, row_rate, col_shift, col_mix, norm_factor, devices, height
    )
    total_sum = total_everywhere(part_sum)
    mode_count = length * total_cols * lax.axis_size("gy")
    loglik = total_sum / mode_count
    return (latent[:, None], loglik)


def solution(mesh):
    return jax.shard_map(
        per_device,
        mesh=mesh,
        in_specs=(P(None, "gy", "gx"), P(), P("gx"), P(), P("gx"), P("gx")),
        out_specs=(P(None, "gy", None, "gx"), P()),
        check_vma=False,
    )
```

```python
import functools
import math

import jax
import jax.numpy as jnp
from jax import lax
from jax.experimental import pallas as pl
from jax.experimental.pallas import tpu as pltpu
from jax.sharding import PartitionSpec as P

precision_top = lax.Precision.HIGHEST
precision_mid = lax.Precision.HIGH


def reverse_bits(value, count):
    result = value * 0
    for place in range(count):
        result = result + (value >> place & 1) * (1 << count - 1 - place)
    return result


def root_table(row_index, freqs, length):
    phase = row_index[:, None] * freqs[None, :] % length
    angle = phase.astype(jnp.float32) * (-2.0 * math.pi / length)
    return (jnp.cos(angle), jnp.sin(angle))


def complex_einsum(form, real_part, imag_part, cos_part, sin_part, precision=precision_top):
    first = jnp.einsum(form, real_part, cos_part, precision=precision)
    second = jnp.einsum(form, real_part, sin_part, precision=precision)
    first = first - jnp.einsum(form, imag_part, sin_part, precision=precision)
    second = second + jnp.einsum(form, imag_part, cos_part, precision=precision)
    return (first, second)


def x_stage(pieces):
    blocks, devices, rows, width = pieces.shape
    length = devices * width
    levels = devices.bit_length() - 1
    group = jnp.arange(devices, dtype=jnp.int32)
    residue = reverse_bits(group, levels)
    slices = [pieces[:, g].reshape(blocks * rows, width) for g in range(devices)]
    real_slots = []
    imag_slots = []
    for slot in range(devices):
        turn = sum(((slot >> place) & 1) << (levels - 1 - place) for place in range(levels))
        real_terms = []
        imag_terms = []
        for g in range(devices):
            phase = g * turn % devices
            angle = -2.0 * math.pi * phase / devices
            cos_value = 0.0 if phase * 4 % devices == 0 and phase * 4 // devices % 2 == 1 else math.cos(angle)
            sin_value = 0.0 if phase * 2 % devices == 0 else math.sin(angle)
            if cos_value != 0.0:
                real_terms.append(slices[g] * cos_value)
            if sin_value != 0.0:
                imag_terms.append(slices[g] * sin_value)
        real_slots.append(sum(real_terms[1:], real_terms[0]))
        imag_slots.append(
            sum(imag_terms[1:], imag_terms[0]) if imag_terms else jnp.zeros_like(slices[0])
        )
    parts = jnp.stack(
        [jnp.concatenate([re, im], axis=1) for re, im in zip(real_slots, imag_slots)]
    )
    local_index = jnp.arange(width, dtype=jnp.int32)
    freqs = residue[:, None] + devices * local_index[None, :]
    phase = local_index[None, :, None] * freqs[:, None, :] % length
    angle = phase.astype(jnp.float32) * (-2.0 * math.pi / length)
    cos_t = jnp.cos(angle)
    sin_t = jnp.sin(angle)
    from_real = jnp.concatenate([cos_t, sin_t], axis=2)
    from_imag = jnp.concatenate([-sin_t, cos_t], axis=2)
    table = jnp.concatenate([from_real, from_imag], axis=1)
    spectrum = jnp.einsum("dyn,dnk->dyk", parts, table, precision=precision_mid)
    return spectrum


def y_transform(real_part, imag_part):
    planes, length, width = real_part.shape
    outer = 1 << (length.bit_length() - 1) // 2
    inner = length // outer
    outer_index = jnp.arange(outer, dtype=jnp.int32)
    inner_index = jnp.arange(inner, dtype=jnp.int32)
    cos_one, sin_one = root_table(outer_index, outer_index, outer)
    cos_two, sin_two = root_table(inner_index, inner_index, inner)
    cos_mid, sin_mid = root_table(outer_index, inner_index, length)
    shaped_real = real_part.reshape(planes, outer, inner, width)
    shaped_imag = imag_part.reshape(planes, outer, inner, width)
    step_real, step_imag = complex_einsum(
        "zabc,ak->zkbc", shaped_real, shaped_imag, cos_one, sin_one
    )
    twist_cos = cos_mid[None, :, :, None]
    twist_sin = sin_mid[None, :, :, None]
    turned_real = step_real * twist_cos - step_imag * twist_sin
    turned_imag = step_real * twist_sin + step_imag * twist_cos
    final_real, final_imag = complex_einsum(
        "zkbc,bj->zjkc", turned_real, turned_imag, cos_two, sin_two
    )
    return (final_real.reshape(planes, length, width), final_imag.reshape(planes, length, width))


def y_kernel(norm_factor, cos_a_ref, sin_a_ref, table_b_ref, row_scale_ref, row_rate_ref, col_scale_ref, col_shift_ref,
             col_mix_ref, spectrum_hbm, out_hbm, sum_ref,
             held, step_real, step_imag, staged, in_sems, out_sems):
    high, low, blocks, rows, both_width = spectrum_hbm.shape
    width = both_width // 2
    size_b = low * rows
    size_a = high * blocks
    half = width // 2
    loads = []
    for part in range(2):
        for index in range(size_b):
            copy = pltpu.make_async_copy(
                spectrum_hbm.at[:, index // rows, :, index % rows, pl.ds(part * width, width)],
                held.at[part, index],
                in_sems.at[part, index],
            )
            copy.start()
            loads.append(copy)

    def dot(left, right):
        return jnp.dot(left, right, precision=precision_mid, preferred_element_type=jnp.float32)

    cos_a = cos_a_ref[...]
    sin_a = sin_a_ref[...]
    both_a = jnp.concatenate(
        [jnp.concatenate([cos_a, -sin_a], axis=1), jnp.concatenate([sin_a, cos_a], axis=1)], axis=0
    )

    def first(index, carry):
        for part in range(2):
            pltpu.make_async_copy(
                spectrum_hbm.at[:, index // rows, :, index % rows, pl.ds(part * width, width)],
                held.at[part, index],
                in_sems.at[part, index],
            ).wait()
        part = jnp.concatenate(
            [held[0, index].reshape(size_a, width), held[1, index].reshape(size_a, width)], axis=0
        )
        result = dot(both_a, part)
        turned_real = result[:size_a]
        turned_imag = result[size_a:]
        rows_here = pl.ds(pl.multiple_of(index * size_a, size_a), size_a)
        for side in range(2):
            lanes = slice(side * half, (side + 1) * half)
            step_real[side, rows_here, :] = turned_real[:, lanes]
            step_imag[side, rows_here, :] = turned_imag[:, lanes]
        return carry

    lax.fori_loop(0, size_b, first, 0)

    col_scale = col_scale_ref[...]
    col_shift = col_shift_ref[...]
    col_mix = col_mix_ref[...]

    def second(index, total):
        picked = pl.ds(index, size_b, stride=size_a)
        rows = pl.ds(pl.multiple_of(index * size_b, size_b), size_b)
        row_scale = row_scale_ref[rows, :]
        row_rate = row_rate_ref[rows, :]
        for side in range(2):
            lanes = slice(side * half, (side + 1) * half)
            part = jnp.concatenate([step_real[side, picked, :], step_imag[side, picked, :]], axis=0)
            result = dot(table_b_ref[index], part)
            spec_real = result[:size_b]
            spec_imag = result[size_b:]
            scale = row_scale * col_scale[:, lanes]
            latent_u = spec_real * norm_factor * scale
            latent_v = spec_imag * norm_factor * scale
            log_scale = row_rate * jnp.tanh(latent_u + col_shift[:, lanes])
            latent_w = latent_v * jnp.exp(log_scale) + col_mix[:, lanes] * latent_u
            terms = (
                -0.5 * (latent_u * latent_u + latent_w * latent_w)
                - math.log(2.0 * math.pi)
                + log_scale
                + 2.0 * jnp.log(scale)
            )
            staged[0, index, :, lanes] = latent_u
            staged[1, index, :, lanes] = latent_w
            total = total + terms
        for part in range(2):
            pltpu.make_async_copy(
                staged.at[part, index], out_hbm.at[part, :, index, :], out_sems.at[part, index]
            ).start()
        return total

    total = lax.fori_loop(0, size_a, second, jnp.zeros((size_b, half), jnp.float32))
    sum_ref[...] = jnp.broadcast_to(jnp.sum(total), sum_ref.shape)

    def finish(index, carry):
        for part in range(2):
            pltpu.make_async_copy(
                staged.at[part, index], out_hbm.at[part, :, index, :], out_sems.at[part, index]
            ).wait()
        return carry

    lax.fori_loop(0, size_a, finish, 0)


def y_stage(spectrum, row_scale, col_scale, row_rate, col_shift, col_mix, norm_factor, devices, height):
    _, count, both_width = spectrum.shape
    width = both_width // 2
    length = devices * count
    size_b = 1 << (length.bit_length() - 1) // 2
    size_a = length // size_b
    blocks = length // height
    rows = height // devices
    low = size_b // rows
    high = devices // low
    index_a = jnp.arange(size_a, dtype=jnp.int32)
    index_b = jnp.arange(size_b, dtype=jnp.int32)
    order_a = (index_a % blocks) * high + index_a // blocks
    cos_a, sin_a = root_table(index_a, order_a, size_a)
    out_rows = size_a * index_b[None, :, None] + index_a[:, None, None]
    phase = index_b[None, None, :] * out_rows % length
    angle = phase.astype(jnp.float32) * (-2.0 * math.pi / length)
    cos_b = jnp.cos(angle)
    sin_b = jnp.sin(angle)
    table_b = jnp.concatenate(
        [jnp.concatenate([cos_b, -sin_b], axis=2), jnp.concatenate([sin_b, cos_b], axis=2)], axis=1
    )
    row_scale_t = row_scale.reshape(size_b, size_a).T.reshape(length, 1)
    row_rate_t = row_rate.reshape(size_b, size_a).T.reshape(length, 1)
    vmem = pl.BlockSpec(memory_space=pltpu.VMEM)
    anywhere = pl.BlockSpec(memory_space=pl.ANY)
    shaped = spectrum.reshape(high, low, blocks, rows, both_width)
    latent, sums = pl.pallas_call(
        functools.partial(y_kernel, norm_factor),
        out_shape=(
            jax.ShapeDtypeStruct((2, size_b, size_a, width), jnp.float32),
            jax.ShapeDtypeStruct((8, 128), jnp.float32),
        ),
        in_specs=[vmem] * 8 + [anywhere],
        out_specs=(anywhere, vmem),
        scratch_shapes=[
            pltpu.VMEM((2, size_b, high, blocks, width), jnp.float32),
            pltpu.VMEM((2, length, width // 2), jnp.float32),
            pltpu.VMEM((2, length, width // 2), jnp.float32),
            pltpu.VMEM((2, size_a, size_b, width), jnp.float32),
            pltpu.SemaphoreType.DMA((2, size_b)),
            pltpu.SemaphoreType.DMA((2, size_a)),
        ],
        compiler_params=pltpu.CompilerParams(vmem_limit_bytes=60 * 1024 * 1024),
    )(
        cos_a, sin_a, table_b,
        row_scale_t, row_rate_t, col_scale.reshape(1, width), col_shift.reshape(1, width),
        col_mix.reshape(1, width), shaped,
    )
    return latent.reshape(2, length, width), sums

MESH_IDS = pl.DeviceIdType.MESH


def total_kernel(value_ref, out_ref, slots_a, slots_b, send_a, recv_a, send_b, recv_b):
    count_x = lax.axis_size("gx")
    count_y = lax.axis_size("gy")
    me_x = lax.axis_index("gx")
    me_y = lax.axis_index("gy")
    barrier = pltpu.get_barrier_semaphore()
    for step in range(1, count_x):
        pl.semaphore_signal(
            barrier, inc=1, device_id=((me_x + step) % count_x, me_y), device_id_type=MESH_IDS
        )
    for step in range(1, count_y):
        pl.semaphore_signal(
            barrier, inc=1, device_id=(me_x, (me_y + step) % count_y), device_id_type=MESH_IDS
        )
    slots_a[0] = value_ref[...]
    pl.semaphore_wait(barrier, count_x - 1 + count_y - 1)
    sends = []
    for step in range(1, count_x):
        copy = pltpu.make_async_remote_copy(
            src_ref=value_ref,
            dst_ref=slots_a.at[step],
            send_sem=send_a.at[step],
            recv_sem=recv_a.at[step],
            device_id=((me_x + step) % count_x, me_y),
            device_id_type=MESH_IDS,
        )
        copy.start()
        sends.append(copy)
    for copy in sends:
        copy.wait_recv()
    group_sum = slots_a[(me_x - 0) % count_x]
    for source in range(1, count_x):
        group_sum = group_sum + slots_a[(me_x - source + count_x) % count_x]
    slots_b[0] = group_sum
    later = []
    for step in range(1, count_y):
        copy = pltpu.make_async_remote_copy(
            src_ref=slots_b.at[0],
            dst_ref=slots_b.at[step],
            send_sem=send_b.at[step],
            recv_sem=recv_b.at[step],
            device_id=(me_x, (me_y + step) % count_y),
            device_id_type=MESH_IDS,
        )
        copy.start()
        later.append(copy)
    for copy in later:
        copy.wait_recv()
    grand = slots_b[(me_y - 0) % count_y]
    for source in range(1, count_y):
        grand = grand + slots_b[(me_y - source + count_y) % count_y]
    out_ref[...] = grand
    for copy in sends:
        copy.wait_send()
    for copy in later:
        copy.wait_send()


def total_everywhere(tile):
    count_x = lax.axis_size("gx")
    count_y = lax.axis_size("gy")
    result = pl.pallas_call(
        total_kernel,
        out_shape=jax.ShapeDtypeStruct((8, 128), jnp.float32),
        in_specs=[pl.BlockSpec(memory_space=pltpu.VMEM)],
        out_specs=pl.BlockSpec(memory_space=pltpu.VMEM),
        scratch_shapes=[
            pltpu.VMEM((count_x, 8, 128), jnp.float32),
            pltpu.VMEM((count_y, 8, 128), jnp.float32),
            pltpu.SemaphoreType.DMA((count_x,)),
            pltpu.SemaphoreType.DMA((count_x,)),
            pltpu.SemaphoreType.DMA((count_y,)),
            pltpu.SemaphoreType.DMA((count_y,)),
        ],
        compiler_params=pltpu.CompilerParams(collective_id=0, has_side_effects=True),
    )(tile)
    return result[0, 0]


def per_device(field, row_scale, col_scale, row_rate, col_shift, col_mix):
    devices = lax.axis_size("gx")
    planes, height, width = field.shape
    rows = height // devices
    outgoing = field.reshape(planes * devices, rows, width)
    incoming = lax.all_to_all(outgoing, ("gy", "gx"), split_axis=0, concat_axis=0, tiled=True)
    incoming = incoming.reshape(planes, devices, rows, width)
    both = x_stage(incoming)
    both = lax.all_to_all(both, "gx", split_axis=0, concat_axis=0, tiled=True)
    length = both.shape[0] * both.shape[1]
    total_cols = both.shape[2] // 2 * devices
    norm_factor = 1.0 / math.sqrt(length * total_cols)
    latent, part_sum = y_stage(
        both, row_scale, col_scale, row_rate, col_shift, col_mix, norm_factor, devices, height
    )
    total_sum = total_everywhere(part_sum)
    mode_count = length * total_cols * lax.axis_size("gy")
    loglik = total_sum / mode_count
    return (latent[:, None], loglik)


def solution(mesh):
    return jax.shard_map(
        per_device,
        mesh=mesh,
        in_specs=(P(None, "gy", "gx"), P(), P("gx"), P(), P("gx"), P("gx")),
        out_specs=(P(None, "gy", None, "gx"), P()),
        check_vma=False,
    )
```

```python
import functools
import math

import jax
import jax.numpy as jnp
from jax import lax
from jax.experimental import pallas as pl
from jax.experimental.pallas import tpu as pltpu
from jax.sharding import PartitionSpec as P

precision_top = lax.Precision.HIGHEST
precision_mid = lax.Precision.HIGH


def reverse_bits(value, count):
    result = value * 0
    for place in range(count):
        result = result + (value >> place & 1) * (1 << count - 1 - place)
    return result


def root_table(row_index, freqs, length):
    phase = row_index[:, None] * freqs[None, :] % length
    angle = phase.astype(jnp.float32) * (-2.0 * math.pi / length)
    return (jnp.cos(angle), jnp.sin(angle))


def complex_einsum(form, real_part, imag_part, cos_part, sin_part, precision=precision_top):
    first = jnp.einsum(form, real_part, cos_part, precision=precision)
    second = jnp.einsum(form, real_part, sin_part, precision=precision)
    first = first - jnp.einsum(form, imag_part, sin_part, precision=precision)
    second = second + jnp.einsum(form, imag_part, cos_part, precision=precision)
    return (first, second)


def x_stage(pieces):
    blocks, devices, rows, width = pieces.shape
    length = devices * width
    levels = devices.bit_length() - 1
    group = jnp.arange(devices, dtype=jnp.int32)
    residue = reverse_bits(group, levels)
    slices = [pieces[:, g].reshape(blocks * rows, width) for g in range(devices)]
    real_slots = []
    imag_slots = []
    for slot in range(devices):
        turn = sum(((slot >> place) & 1) << (levels - 1 - place) for place in range(levels))
        real_terms = []
        imag_terms = []
        for g in range(devices):
            phase = g * turn % devices
            angle = -2.0 * math.pi * phase / devices
            cos_value = 0.0 if phase * 4 % devices == 0 and phase * 4 // devices % 2 == 1 else math.cos(angle)
            sin_value = 0.0 if phase * 2 % devices == 0 else math.sin(angle)
            if cos_value != 0.0:
                real_terms.append(slices[g] * cos_value)
            if sin_value != 0.0:
                imag_terms.append(slices[g] * sin_value)
        real_slots.append(sum(real_terms[1:], real_terms[0]))
        imag_slots.append(
            sum(imag_terms[1:], imag_terms[0]) if imag_terms else jnp.zeros_like(slices[0])
        )
    parts = jnp.stack(
        [jnp.concatenate([re, im], axis=1) for re, im in zip(real_slots, imag_slots)]
    )
    local_index = jnp.arange(width, dtype=jnp.int32)
    freqs = residue[:, None] + devices * local_index[None, :]
    phase = local_index[None, :, None] * freqs[:, None, :] % length
    angle = phase.astype(jnp.float32) * (-2.0 * math.pi / length)
    cos_t = jnp.cos(angle)
    sin_t = jnp.sin(angle)
    from_real = jnp.concatenate([cos_t, sin_t], axis=2)
    from_imag = jnp.concatenate([-sin_t, cos_t], axis=2)
    table = jnp.concatenate([from_real, from_imag], axis=1)
    spectrum = jnp.einsum("dyn,dnk->dyk", parts, table, precision=precision_mid)
    return spectrum


def y_transform(real_part, imag_part):
    planes, length, width = real_part.shape
    outer = 1 << (length.bit_length() - 1) // 2
    inner = length // outer
    outer_index = jnp.arange(outer, dtype=jnp.int32)
    inner_index = jnp.arange(inner, dtype=jnp.int32)
    cos_one, sin_one = root_table(outer_index, outer_index, outer)
    cos_two, sin_two = root_table(inner_index, inner_index, inner)
    cos_mid, sin_mid = root_table(outer_index, inner_index, length)
    shaped_real = real_part.reshape(planes, outer, inner, width)
    shaped_imag = imag_part.reshape(planes, outer, inner, width)
    step_real, step_imag = complex_einsum(
        "zabc,ak->zkbc", shaped_real, shaped_imag, cos_one, sin_one
    )
    twist_cos = cos_mid[None, :, :, None]
    twist_sin = sin_mid[None, :, :, None]
    turned_real = step_real * twist_cos - step_imag * twist_sin
    turned_imag = step_real * twist_sin + step_imag * twist_cos
    final_real, final_imag = complex_einsum(
        "zkbc,bj->zjkc", turned_real, turned_imag, cos_two, sin_two
    )
    return (final_real.reshape(planes, length, width), final_imag.reshape(planes, length, width))


def y_kernel(norm_factor, cos_a_ref, sin_a_ref, table_b_ref, row_scale_ref, row_rate_ref, col_scale_ref, col_shift_ref,
             col_mix_ref, spectrum_hbm, out_hbm, sum_ref,
             held, step_a, turned, staged, in_sems, out_sems, turn_sems):
    high, low, blocks, rows, both_width = spectrum_hbm.shape
    width = both_width // 2
    size_b = low * rows
    size_a = high * blocks
    half = width // 2
    loads = []
    for part in range(2):
        for index in range(size_b):
            copy = pltpu.make_async_copy(
                spectrum_hbm.at[:, index // rows, :, index % rows, pl.ds(part * width, width)],
                held.at[part, index],
                in_sems.at[part, index],
            )
            copy.start()
            loads.append(copy)

    def dot(left, right):
        return jnp.dot(left, right, precision=precision_mid, preferred_element_type=jnp.float32)

    cos_a = cos_a_ref[...]
    sin_a = sin_a_ref[...]
    both_a = jnp.concatenate(
        [jnp.concatenate([cos_a, -sin_a], axis=1), jnp.concatenate([sin_a, cos_a], axis=1)], axis=0
    )

    def first(index, carry):
        for part in range(2):
            pltpu.make_async_copy(
                spectrum_hbm.at[:, index // rows, :, index % rows, pl.ds(part * width, width)],
                held.at[part, index],
                in_sems.at[part, index],
            ).wait()
        part = jnp.concatenate(
            [held[0, index].reshape(size_a, width), held[1, index].reshape(size_a, width)], axis=0
        )
        result = dot(both_a, part)
        step_a[0, index] = result[:size_a]
        step_a[1, index] = result[size_a:]
        for part in range(2):
            pltpu.make_async_copy(
                step_a.at[part, index], turned.at[part, :, index, :], turn_sems.at[part, index]
            ).start()
        return carry

    lax.fori_loop(0, size_b, first, 0)

    def settle(index, carry):
        for part in range(2):
            pltpu.make_async_copy(
                step_a.at[part, index], turned.at[part, :, index, :], turn_sems.at[part, index]
            ).wait()
        return carry

    lax.fori_loop(0, size_b, settle, 0)

    col_scale = col_scale_ref[...]
    col_shift = col_shift_ref[...]
    col_mix = col_mix_ref[...]

    def second(index, total):
        rows = pl.ds(pl.multiple_of(index * size_b, size_b), size_b)
        part = jnp.concatenate([turned[0, index], turned[1, index]], axis=0)
        result = dot(table_b_ref[index], part)
        spec_real = result[:size_b]
        spec_imag = result[size_b:]
        scale = row_scale_ref[rows, :] * col_scale
        latent_u = spec_real * norm_factor * scale
        latent_v = spec_imag * norm_factor * scale
        log_scale = row_rate_ref[rows, :] * jnp.tanh(latent_u + col_shift)
        latent_w = latent_v * jnp.exp(log_scale) + col_mix * latent_u
        terms = (
            -0.5 * (latent_u * latent_u + latent_w * latent_w)
            - math.log(2.0 * math.pi)
            + log_scale
            + 2.0 * jnp.log(scale)
        )
        staged[0, index] = latent_u
        staged[1, index] = latent_w
        for part in range(2):
            pltpu.make_async_copy(
                staged.at[part, index], out_hbm.at[part, :, index, :], out_sems.at[part, index]
            ).start()
        return total + terms

    total = lax.fori_loop(0, size_a, second, jnp.zeros((size_b, width), jnp.float32))
    sum_ref[...] = jnp.broadcast_to(jnp.sum(total), sum_ref.shape)

    def finish(index, carry):
        for part in range(2):
            pltpu.make_async_copy(
                staged.at[part, index], out_hbm.at[part, :, index, :], out_sems.at[part, index]
            ).wait()
        return carry

    lax.fori_loop(0, size_a, finish, 0)


def y_stage(spectrum, row_scale, col_scale, row_rate, col_shift, col_mix, norm_factor, devices, height):
    _, count, both_width = spectrum.shape
    width = both_width // 2
    length = devices * count
    size_b = 1 << (length.bit_length() - 1) // 2
    size_a = length // size_b
    blocks = length // height
    rows = height // devices
    low = size_b // rows
    high = devices // low
    index_a = jnp.arange(size_a, dtype=jnp.int32)
    index_b = jnp.arange(size_b, dtype=jnp.int32)
    order_a = (index_a % blocks) * high + index_a // blocks
    cos_a, sin_a = root_table(index_a, order_a, size_a)
    out_rows = size_a * index_b[None, :, None] + index_a[:, None, None]
    phase = index_b[None, None, :] * out_rows % length
    angle = phase.astype(jnp.float32) * (-2.0 * math.pi / length)
    cos_b = jnp.cos(angle)
    sin_b = jnp.sin(angle)
    table_b = jnp.concatenate(
        [jnp.concatenate([cos_b, -sin_b], axis=2), jnp.concatenate([sin_b, cos_b], axis=2)], axis=1
    )
    row_scale_t = row_scale.reshape(size_b, size_a).T.reshape(length, 1)
    row_rate_t = row_rate.reshape(size_b, size_a).T.reshape(length, 1)
    vmem = pl.BlockSpec(memory_space=pltpu.VMEM)
    anywhere = pl.BlockSpec(memory_space=pl.ANY)
    shaped = spectrum.reshape(high, low, blocks, rows, both_width)
    latent, sums = pl.pallas_call(
        functools.partial(y_kernel, norm_factor),
        out_shape=(
            jax.ShapeDtypeStruct((2, size_b, size_a, width), jnp.float32),
            jax.ShapeDtypeStruct((8, 128), jnp.float32),
        ),
        in_specs=[vmem] * 8 + [anywhere],
        out_specs=(anywhere, vmem),
        scratch_shapes=[
            pltpu.VMEM((2, size_b, high, blocks, width), jnp.float32),
            pltpu.VMEM((2, size_b, size_a, width), jnp.float32),
            pltpu.VMEM((2, size_a, size_b, width), jnp.float32),
            pltpu.VMEM((2, size_a, size_b, width), jnp.float32),
            pltpu.SemaphoreType.DMA((2, size_b)),
            pltpu.SemaphoreType.DMA((2, size_a)),
            pltpu.SemaphoreType.DMA((2, size_b)),
        ],
        compiler_params=pltpu.CompilerParams(vmem_limit_bytes=60 * 1024 * 1024),
    )(
        cos_a, sin_a, table_b,
        row_scale_t, row_rate_t, col_scale.reshape(1, width), col_shift.reshape(1, width),
        col_mix.reshape(1, width), shaped,
    )
    return latent.reshape(2, length, width), sums

MESH_IDS = pl.DeviceIdType.MESH


def total_kernel(value_ref, out_ref, slots_a, slots_b, send_a, recv_a, send_b, recv_b):
    count_x = lax.axis_size("gx")
    count_y = lax.axis_size("gy")
    me_x = lax.axis_index("gx")
    me_y = lax.axis_index("gy")
    barrier = pltpu.get_barrier_semaphore()
    for step in range(1, count_x):
        pl.semaphore_signal(
            barrier, inc=1, device_id=((me_x + step) % count_x, me_y), device_id_type=MESH_IDS
        )
    for step in range(1, count_y):
        pl.semaphore_signal(
            barrier, inc=1, device_id=(me_x, (me_y + step) % count_y), device_id_type=MESH_IDS
        )
    slots_a[0] = value_ref[...]
    pl.semaphore_wait(barrier, count_x - 1 + count_y - 1)
    sends = []
    for step in range(1, count_x):
        copy = pltpu.make_async_remote_copy(
            src_ref=value_ref,
            dst_ref=slots_a.at[step],
            send_sem=send_a.at[step],
            recv_sem=recv_a.at[step],
            device_id=((me_x + step) % count_x, me_y),
            device_id_type=MESH_IDS,
        )
        copy.start()
        sends.append(copy)
    for copy in sends:
        copy.wait_recv()
    group_sum = slots_a[(me_x - 0) % count_x]
    for source in range(1, count_x):
        group_sum = group_sum + slots_a[(me_x - source + count_x) % count_x]
    slots_b[0] = group_sum
    later = []
    for step in range(1, count_y):
        copy = pltpu.make_async_remote_copy(
            src_ref=slots_b.at[0],
            dst_ref=slots_b.at[step],
            send_sem=send_b.at[step],
            recv_sem=recv_b.at[step],
            device_id=(me_x, (me_y + step) % count_y),
            device_id_type=MESH_IDS,
        )
        copy.start()
        later.append(copy)
    for copy in later:
        copy.wait_recv()
    grand = slots_b[(me_y - 0) % count_y]
    for source in range(1, count_y):
        grand = grand + slots_b[(me_y - source + count_y) % count_y]
    out_ref[...] = grand
    for copy in sends:
        copy.wait_send()
    for copy in later:
        copy.wait_send()


def total_everywhere(tile):
    count_x = lax.axis_size("gx")
    count_y = lax.axis_size("gy")
    result = pl.pallas_call(
        total_kernel,
        out_shape=jax.ShapeDtypeStruct((8, 128), jnp.float32),
        in_specs=[pl.BlockSpec(memory_space=pltpu.VMEM)],
        out_specs=pl.BlockSpec(memory_space=pltpu.VMEM),
        scratch_shapes=[
            pltpu.VMEM((count_x, 8, 128), jnp.float32),
            pltpu.VMEM((count_y, 8, 128), jnp.float32),
            pltpu.SemaphoreType.DMA((count_x,)),
            pltpu.SemaphoreType.DMA((count_x,)),
            pltpu.SemaphoreType.DMA((count_y,)),
            pltpu.SemaphoreType.DMA((count_y,)),
        ],
        compiler_params=pltpu.CompilerParams(collective_id=0, has_side_effects=True),
    )(tile)
    return result[0, 0]


def per_device(field, row_scale, col_scale, row_rate, col_shift, col_mix):
    devices = lax.axis_size("gx")
    planes, height, width = field.shape
    rows = height // devices
    outgoing = field.reshape(planes * devices, rows, width)
    incoming = lax.all_to_all(outgoing, ("gy", "gx"), split_axis=0, concat_axis=0, tiled=True)
    incoming = incoming.reshape(planes, devices, rows, width)
    both = x_stage(incoming)
    both = lax.all_to_all(both, "gx", split_axis=0, concat_axis=0, tiled=True)
    length = both.shape[0] * both.shape[1]
    total_cols = both.shape[2] // 2 * devices
    norm_factor = 1.0 / math.sqrt(length * total_cols)
    latent, part_sum = y_stage(
        both, row_scale, col_scale, row_rate, col_shift, col_mix, norm_factor, devices, height
    )
    total_sum = total_everywhere(part_sum)
    mode_count = length * total_cols * lax.axis_size("gy")
    loglik = total_sum / mode_count
    return (latent[:, None], loglik)


def solution(mesh):
    return jax.shard_map(
        per_device,
        mesh=mesh,
        in_specs=(P(None, "gy", "gx"), P(), P("gx"), P(), P("gx"), P("gx")),
        out_specs=(P(None, "gy", None, "gx"), P()),
        check_vma=False,
    )
```

```python
import functools
import math

import jax
import jax.numpy as jnp
from jax import lax
from jax.experimental import pallas as pl
from jax.experimental.pallas import tpu as pltpu
from jax.sharding import PartitionSpec as P

precision_top = lax.Precision.HIGHEST
precision_mid = lax.Precision.HIGH


def reverse_bits(value, count):
    result = value * 0
    for place in range(count):
        result = result + (value >> place & 1) * (1 << count - 1 - place)
    return result


def root_table(row_index, freqs, length):
    phase = row_index[:, None] * freqs[None, :] % length
    angle = phase.astype(jnp.float32) * (-2.0 * math.pi / length)
    return (jnp.cos(angle), jnp.sin(angle))


def complex_einsum(form, real_part, imag_part, cos_part, sin_part, precision=precision_top):
    first = jnp.einsum(form, real_part, cos_part, precision=precision)
    second = jnp.einsum(form, real_part, sin_part, precision=precision)
    first = first - jnp.einsum(form, imag_part, sin_part, precision=precision)
    second = second + jnp.einsum(form, imag_part, cos_part, precision=precision)
    return (first, second)


def x_stage(pieces):
    blocks, devices, rows, width = pieces.shape
    length = devices * width
    levels = devices.bit_length() - 1
    group = jnp.arange(devices, dtype=jnp.int32)
    residue = reverse_bits(group, levels)
    slices = [pieces[:, g].reshape(blocks * rows, width) for g in range(devices)]
    real_slots = []
    imag_slots = []
    for slot in range(devices):
        turn = sum(((slot >> place) & 1) << (levels - 1 - place) for place in range(levels))
        real_terms = []
        imag_terms = []
        for g in range(devices):
            phase = g * turn % devices
            angle = -2.0 * math.pi * phase / devices
            cos_value = 0.0 if phase * 4 % devices == 0 and phase * 4 // devices % 2 == 1 else math.cos(angle)
            sin_value = 0.0 if phase * 2 % devices == 0 else math.sin(angle)
            if cos_value != 0.0:
                real_terms.append(slices[g] * cos_value)
            if sin_value != 0.0:
                imag_terms.append(slices[g] * sin_value)
        real_slots.append(sum(real_terms[1:], real_terms[0]))
        imag_slots.append(
            sum(imag_terms[1:], imag_terms[0]) if imag_terms else jnp.zeros_like(slices[0])
        )
    parts = jnp.stack(
        [jnp.concatenate([re, im], axis=1) for re, im in zip(real_slots, imag_slots)]
    )
    local_index = jnp.arange(width, dtype=jnp.int32)
    freqs = residue[:, None] + devices * local_index[None, :]
    phase = local_index[None, :, None] * freqs[:, None, :] % length
    angle = phase.astype(jnp.float32) * (-2.0 * math.pi / length)
    cos_t = jnp.cos(angle)
    sin_t = jnp.sin(angle)
    from_real = jnp.concatenate([cos_t, sin_t], axis=2)
    from_imag = jnp.concatenate([-sin_t, cos_t], axis=2)
    table = jnp.concatenate([from_real, from_imag], axis=1)
    spectrum = jnp.einsum("dyn,dnk->dyk", parts, table, precision=precision_mid)
    return spectrum


def y_transform(real_part, imag_part):
    planes, length, width = real_part.shape
    outer = 1 << (length.bit_length() - 1) // 2
    inner = length // outer
    outer_index = jnp.arange(outer, dtype=jnp.int32)
    inner_index = jnp.arange(inner, dtype=jnp.int32)
    cos_one, sin_one = root_table(outer_index, outer_index, outer)
    cos_two, sin_two = root_table(inner_index, inner_index, inner)
    cos_mid, sin_mid = root_table(outer_index, inner_index, length)
    shaped_real = real_part.reshape(planes, outer, inner, width)
    shaped_imag = imag_part.reshape(planes, outer, inner, width)
    step_real, step_imag = complex_einsum(
        "zabc,ak->zkbc", shaped_real, shaped_imag, cos_one, sin_one
    )
    twist_cos = cos_mid[None, :, :, None]
    twist_sin = sin_mid[None, :, :, None]
    turned_real = step_real * twist_cos - step_imag * twist_sin
    turned_imag = step_real * twist_sin + step_imag * twist_cos
    final_real, final_imag = complex_einsum(
        "zkbc,bj->zjkc", turned_real, turned_imag, cos_two, sin_two
    )
    return (final_real.reshape(planes, length, width), final_imag.reshape(planes, length, width))


def y_kernel(norm_factor, cos_a_ref, sin_a_ref, table_b_ref, row_scale_ref, row_rate_ref, col_scale_ref, col_shift_ref,
             col_mix_ref, spectrum_hbm, out_hbm, sum_ref,
             held, step_a, turned, staged, in_sems, out_sems, turn_sems):
    high, low, blocks, rows, both_width = spectrum_hbm.shape
    width = both_width // 2
    size_b = low * rows
    size_a = high * blocks
    half = width // 2
    loads = []
    for part in range(2):
        for index in range(size_b):
            copy = pltpu.make_async_copy(
                spectrum_hbm.at[:, index // rows, :, index % rows, pl.ds(part * width, width)],
                held.at[index, part],
                in_sems.at[part, index],
            )
            copy.start()
            loads.append(copy)

    def dot(left, right):
        return jnp.dot(left, right, precision=precision_mid, preferred_element_type=jnp.float32)

    cos_a = cos_a_ref[...]
    sin_a = sin_a_ref[...]
    both_a = jnp.concatenate(
        [jnp.concatenate([cos_a, -sin_a], axis=1), jnp.concatenate([sin_a, cos_a], axis=1)], axis=0
    )

    def first(index, carry):
        for part in range(2):
            pltpu.make_async_copy(
                spectrum_hbm.at[:, index // rows, :, index % rows, pl.ds(part * width, width)],
                held.at[index, part],
                in_sems.at[part, index],
            ).wait()
        result = dot(both_a, held[index].reshape(2 * size_a, width))
        step_a[0, index] = result[:size_a]
        step_a[1, index] = result[size_a:]
        for part in range(2):
            pltpu.make_async_copy(
                step_a.at[part, index], turned.at[:, part, index, :], turn_sems.at[part, index]
            ).start()
        return carry

    lax.fori_loop(0, size_b, first, 0)

    def settle(index, carry):
        for part in range(2):
            pltpu.make_async_copy(
                step_a.at[part, index], turned.at[:, part, index, :], turn_sems.at[part, index]
            ).wait()
        return carry

    lax.fori_loop(0, size_b, settle, 0)

    col_scale = col_scale_ref[...]
    col_shift = col_shift_ref[...]
    col_mix = col_mix_ref[...]

    def second(index, total):
        rows = pl.ds(pl.multiple_of(index * size_b, size_b), size_b)
        result = dot(table_b_ref[index], turned[index].reshape(2 * size_b, width))
        spec_real = result[:size_b]
        spec_imag = result[size_b:]
        scale = row_scale_ref[rows, :] * col_scale
        latent_u = spec_real * norm_factor * scale
        latent_v = spec_imag * norm_factor * scale
        log_scale = row_rate_ref[rows, :] * jnp.tanh(latent_u + col_shift)
        latent_w = latent_v * jnp.exp(log_scale) + col_mix * latent_u
        terms = (
            -0.5 * (latent_u * latent_u + latent_w * latent_w)
            - math.log(2.0 * math.pi)
            + log_scale
            + 2.0 * jnp.log(scale)
        )
        staged[0, index] = latent_u
        staged[1, index] = latent_w
        for part in range(2):
            pltpu.make_async_copy(
                staged.at[part, index], out_hbm.at[part, :, index, :], out_sems.at[part, index]
            ).start()
        return total + terms

    total = lax.fori_loop(0, size_a, second, jnp.zeros((size_b, width), jnp.float32))
    sum_ref[...] = jnp.broadcast_to(jnp.sum(total), sum_ref.shape)

    def finish(index, carry):
        for part in range(2):
            pltpu.make_async_copy(
                staged.at[part, index], out_hbm.at[part, :, index, :], out_sems.at[part, index]
            ).wait()
        return carry

    lax.fori_loop(0, size_a, finish, 0)


def y_stage(spectrum, row_scale, col_scale, row_rate, col_shift, col_mix, norm_factor, devices, height):
    _, count, both_width = spectrum.shape
    width = both_width // 2
    length = devices * count
    size_b = 1 << (length.bit_length() - 1) // 2
    size_a = length // size_b
    blocks = length // height
    rows = height // devices
    low = size_b // rows
    high = devices // low
    index_a = jnp.arange(size_a, dtype=jnp.int32)
    index_b = jnp.arange(size_b, dtype=jnp.int32)
    order_a = (index_a % blocks) * high + index_a // blocks
    cos_a, sin_a = root_table(index_a, order_a, size_a)
    out_rows = size_a * index_b[None, :, None] + index_a[:, None, None]
    phase = index_b[None, None, :] * out_rows % length
    angle = phase.astype(jnp.float32) * (-2.0 * math.pi / length)
    cos_b = jnp.cos(angle)
    sin_b = jnp.sin(angle)
    table_b = jnp.concatenate(
        [jnp.concatenate([cos_b, -sin_b], axis=2), jnp.concatenate([sin_b, cos_b], axis=2)], axis=1
    )
    row_scale_t = row_scale.reshape(size_b, size_a).T.reshape(length, 1)
    row_rate_t = row_rate.reshape(size_b, size_a).T.reshape(length, 1)
    vmem = pl.BlockSpec(memory_space=pltpu.VMEM)
    anywhere = pl.BlockSpec(memory_space=pl.ANY)
    shaped = spectrum.reshape(high, low, blocks, rows, both_width)
    latent, sums = pl.pallas_call(
        functools.partial(y_kernel, norm_factor),
        out_shape=(
            jax.ShapeDtypeStruct((2, size_b, size_a, width), jnp.float32),
            jax.ShapeDtypeStruct((8, 128), jnp.float32),
        ),
        in_specs=[vmem] * 8 + [anywhere],
        out_specs=(anywhere, vmem),
        scratch_shapes=[
            pltpu.VMEM((size_b, 2, high, blocks, width), jnp.float32),
            pltpu.VMEM((2, size_b, size_a, width), jnp.float32),
            pltpu.VMEM((size_a, 2, size_b, width), jnp.float32),
            pltpu.VMEM((2, size_a, size_b, width), jnp.float32),
            pltpu.SemaphoreType.DMA((2, size_b)),
            pltpu.SemaphoreType.DMA((2, size_a)),
            pltpu.SemaphoreType.DMA((2, size_b)),
        ],
        compiler_params=pltpu.CompilerParams(vmem_limit_bytes=60 * 1024 * 1024),
    )(
        cos_a, sin_a, table_b,
        row_scale_t, row_rate_t, col_scale.reshape(1, width), col_shift.reshape(1, width),
        col_mix.reshape(1, width), shaped,
    )
    return latent.reshape(2, length, width), sums

MESH_IDS = pl.DeviceIdType.MESH


def total_kernel(value_ref, out_ref, slots_a, slots_b, send_a, recv_a, send_b, recv_b):
    count_x = lax.axis_size("gx")
    count_y = lax.axis_size("gy")
    me_x = lax.axis_index("gx")
    me_y = lax.axis_index("gy")
    barrier = pltpu.get_barrier_semaphore()
    for step in range(1, count_x):
        pl.semaphore_signal(
            barrier, inc=1, device_id=((me_x + step) % count_x, me_y), device_id_type=MESH_IDS
        )
    for step in range(1, count_y):
        pl.semaphore_signal(
            barrier, inc=1, device_id=(me_x, (me_y + step) % count_y), device_id_type=MESH_IDS
        )
    slots_a[0] = value_ref[...]
    pl.semaphore_wait(barrier, count_x - 1 + count_y - 1)
    sends = []
    for step in range(1, count_x):
        copy = pltpu.make_async_remote_copy(
            src_ref=value_ref,
            dst_ref=slots_a.at[step],
            send_sem=send_a.at[step],
            recv_sem=recv_a.at[step],
            device_id=((me_x + step) % count_x, me_y),
            device_id_type=MESH_IDS,
        )
        copy.start()
        sends.append(copy)
    for copy in sends:
        copy.wait_recv()
    group_sum = slots_a[(me_x - 0) % count_x]
    for source in range(1, count_x):
        group_sum = group_sum + slots_a[(me_x - source + count_x) % count_x]
    slots_b[0] = group_sum
    later = []
    for step in range(1, count_y):
        copy = pltpu.make_async_remote_copy(
            src_ref=slots_b.at[0],
            dst_ref=slots_b.at[step],
            send_sem=send_b.at[step],
            recv_sem=recv_b.at[step],
            device_id=(me_x, (me_y + step) % count_y),
            device_id_type=MESH_IDS,
        )
        copy.start()
        later.append(copy)
    for copy in later:
        copy.wait_recv()
    grand = slots_b[(me_y - 0) % count_y]
    for source in range(1, count_y):
        grand = grand + slots_b[(me_y - source + count_y) % count_y]
    out_ref[...] = grand
    for copy in sends:
        copy.wait_send()
    for copy in later:
        copy.wait_send()


def total_everywhere(tile):
    count_x = lax.axis_size("gx")
    count_y = lax.axis_size("gy")
    result = pl.pallas_call(
        total_kernel,
        out_shape=jax.ShapeDtypeStruct((8, 128), jnp.float32),
        in_specs=[pl.BlockSpec(memory_space=pltpu.VMEM)],
        out_specs=pl.BlockSpec(memory_space=pltpu.VMEM),
        scratch_shapes=[
            pltpu.VMEM((count_x, 8, 128), jnp.float32),
            pltpu.VMEM((count_y, 8, 128), jnp.float32),
            pltpu.SemaphoreType.DMA((count_x,)),
            pltpu.SemaphoreType.DMA((count_x,)),
            pltpu.SemaphoreType.DMA((count_y,)),
            pltpu.SemaphoreType.DMA((count_y,)),
        ],
        compiler_params=pltpu.CompilerParams(collective_id=0, has_side_effects=True),
    )(tile)
    return result[0, 0]


def per_device(field, row_scale, col_scale, row_rate, col_shift, col_mix):
    devices = lax.axis_size("gx")
    planes, height, width = field.shape
    rows = height // devices
    outgoing = field.reshape(planes * devices, rows, width)
    incoming = lax.all_to_all(outgoing, ("gy", "gx"), split_axis=0, concat_axis=0, tiled=True)
    incoming = incoming.reshape(planes, devices, rows, width)
    both = x_stage(incoming)
    both = lax.all_to_all(both, "gx", split_axis=0, concat_axis=0, tiled=True)
    length = both.shape[0] * both.shape[1]
    total_cols = both.shape[2] // 2 * devices
    norm_factor = 1.0 / math.sqrt(length * total_cols)
    latent, part_sum = y_stage(
        both, row_scale, col_scale, row_rate, col_shift, col_mix, norm_factor, devices, height
    )
    total_sum = total_everywhere(part_sum)
    mode_count = length * total_cols * lax.axis_size("gy")
    loglik = total_sum / mode_count
    return (latent[:, None], loglik)


def solution(mesh):
    return jax.shard_map(
        per_device,
        mesh=mesh,
        in_specs=(P(None, "gy", "gx"), P(), P("gx"), P(), P("gx"), P("gx")),
        out_specs=(P(None, "gy", None, "gx"), P()),
        check_vma=False,
    )
```

```python
import functools
import math

import jax
import jax.numpy as jnp
from jax import lax
from jax.experimental import pallas as pl
from jax.experimental.pallas import tpu as pltpu
from jax.sharding import PartitionSpec as P

precision_top = lax.Precision.HIGHEST
precision_mid = lax.Precision.HIGH


def reverse_bits(value, count):
    result = value * 0
    for place in range(count):
        result = result + (value >> place & 1) * (1 << count - 1 - place)
    return result


def root_table(row_index, freqs, length):
    phase = row_index[:, None] * freqs[None, :] % length
    angle = phase.astype(jnp.float32) * (-2.0 * math.pi / length)
    return (jnp.cos(angle), jnp.sin(angle))


def complex_einsum(form, real_part, imag_part, cos_part, sin_part, precision=precision_top):
    first = jnp.einsum(form, real_part, cos_part, precision=precision)
    second = jnp.einsum(form, real_part, sin_part, precision=precision)
    first = first - jnp.einsum(form, imag_part, sin_part, precision=precision)
    second = second + jnp.einsum(form, imag_part, cos_part, precision=precision)
    return (first, second)


def x_stage(pieces):
    blocks, devices, rows, width = pieces.shape
    length = devices * width
    levels = devices.bit_length() - 1
    group = jnp.arange(devices, dtype=jnp.int32)
    residue = reverse_bits(group, levels)
    slices = [pieces[:, g].reshape(blocks * rows, width) for g in range(devices)]
    real_slots = []
    imag_slots = []
    for slot in range(devices):
        turn = sum(((slot >> place) & 1) << (levels - 1 - place) for place in range(levels))
        real_terms = []
        imag_terms = []
        for g in range(devices):
            phase = g * turn % devices
            angle = -2.0 * math.pi * phase / devices
            cos_value = 0.0 if phase * 4 % devices == 0 and phase * 4 // devices % 2 == 1 else math.cos(angle)
            sin_value = 0.0 if phase * 2 % devices == 0 else math.sin(angle)
            if cos_value != 0.0:
                real_terms.append(slices[g] * cos_value)
            if sin_value != 0.0:
                imag_terms.append(slices[g] * sin_value)
        real_slots.append(sum(real_terms[1:], real_terms[0]))
        imag_slots.append(
            sum(imag_terms[1:], imag_terms[0]) if imag_terms else jnp.zeros_like(slices[0])
        )
    parts = jnp.stack(
        [jnp.concatenate([re, im], axis=1) for re, im in zip(real_slots, imag_slots)]
    )
    local_index = jnp.arange(width, dtype=jnp.int32)
    freqs = residue[:, None] + devices * local_index[None, :]
    phase = local_index[None, :, None] * freqs[:, None, :] % length
    angle = phase.astype(jnp.float32) * (-2.0 * math.pi / length)
    cos_t = jnp.cos(angle)
    sin_t = jnp.sin(angle)
    from_real = jnp.concatenate([cos_t, sin_t], axis=2)
    from_imag = jnp.concatenate([-sin_t, cos_t], axis=2)
    table = jnp.concatenate([from_real, from_imag], axis=1)
    spectrum = jnp.einsum("dyn,dnk->dyk", parts, table, precision=precision_mid)
    return spectrum


def y_transform(real_part, imag_part):
    planes, length, width = real_part.shape
    outer = 1 << (length.bit_length() - 1) // 2
    inner = length // outer
    outer_index = jnp.arange(outer, dtype=jnp.int32)
    inner_index = jnp.arange(inner, dtype=jnp.int32)
    cos_one, sin_one = root_table(outer_index, outer_index, outer)
    cos_two, sin_two = root_table(inner_index, inner_index, inner)
    cos_mid, sin_mid = root_table(outer_index, inner_index, length)
    shaped_real = real_part.reshape(planes, outer, inner, width)
    shaped_imag = imag_part.reshape(planes, outer, inner, width)
    step_real, step_imag = complex_einsum(
        "zabc,ak->zkbc", shaped_real, shaped_imag, cos_one, sin_one
    )
    twist_cos = cos_mid[None, :, :, None]
    twist_sin = sin_mid[None, :, :, None]
    turned_real = step_real * twist_cos - step_imag * twist_sin
    turned_imag = step_real * twist_sin + step_imag * twist_cos
    final_real, final_imag = complex_einsum(
        "zkbc,bj->zjkc", turned_real, turned_imag, cos_two, sin_two
    )
    return (final_real.reshape(planes, length, width), final_imag.reshape(planes, length, width))


def y_kernel(norm_factor, cos_a_ref, sin_a_ref, table_b_ref, row_scale_ref, row_rate_ref, row_log_ref,
             col_scale_ref, col_log_ref, col_shift_ref,
             col_mix_ref, spectrum_hbm, out_hbm, sum_ref,
             held, step_a, turned, staged, in_sems, out_sems, turn_sems):
    high, low, blocks, rows, both_width = spectrum_hbm.shape
    width = both_width // 2
    size_b = low * rows
    size_a = high * blocks
    half = width // 2
    loads = []
    for part in range(2):
        for index in range(size_b):
            copy = pltpu.make_async_copy(
                spectrum_hbm.at[:, index // rows, :, index % rows, pl.ds(part * width, width)],
                held.at[index, part],
                in_sems.at[part, index],
            )
            copy.start()
            loads.append(copy)

    def dot(left, right):
        return jnp.dot(left, right, precision=precision_mid, preferred_element_type=jnp.float32)

    cos_a = cos_a_ref[...]
    sin_a = sin_a_ref[...]
    both_a = jnp.concatenate(
        [jnp.concatenate([cos_a, -sin_a], axis=1), jnp.concatenate([sin_a, cos_a], axis=1)], axis=0
    )

    def first(index, carry):
        for part in range(2):
            pltpu.make_async_copy(
                spectrum_hbm.at[:, index // rows, :, index % rows, pl.ds(part * width, width)],
                held.at[index, part],
                in_sems.at[part, index],
            ).wait()
        result = dot(both_a, held[index].reshape(2 * size_a, width))
        step_a[0, index] = result[:size_a]
        step_a[1, index] = result[size_a:]
        for part in range(2):
            pltpu.make_async_copy(
                step_a.at[part, index], turned.at[:, part, index, :], turn_sems.at[part, index]
            ).start()
        return carry

    lax.fori_loop(0, size_b, first, 0)

    def settle(index, carry):
        for part in range(2):
            pltpu.make_async_copy(
                step_a.at[part, index], turned.at[:, part, index, :], turn_sems.at[part, index]
            ).wait()
        return carry

    lax.fori_loop(0, size_b, settle, 0)

    col_scale = col_scale_ref[...]
    col_log = col_log_ref[...]
    col_shift = col_shift_ref[...]
    col_mix = col_mix_ref[...]

    def second(index, total):
        rows = pl.ds(pl.multiple_of(index * size_b, size_b), size_b)
        result = dot(table_b_ref[index], turned[index].reshape(2 * size_b, width))
        spec_real = result[:size_b]
        spec_imag = result[size_b:]
        scale = row_scale_ref[rows, :] * col_scale
        latent_u = spec_real * norm_factor * scale
        latent_v = spec_imag * norm_factor * scale
        log_scale = row_rate_ref[rows, :] * jnp.tanh(latent_u + col_shift)
        latent_w = latent_v * jnp.exp(log_scale) + col_mix * latent_u
        terms = (
            -0.5 * (latent_u * latent_u + latent_w * latent_w)
            - math.log(2.0 * math.pi)
            + log_scale
            + 2.0 * (row_log_ref[rows, :] + col_log)
        )
        staged[0, index] = latent_u
        staged[1, index] = latent_w
        for part in range(2):
            pltpu.make_async_copy(
                staged.at[part, index], out_hbm.at[part, :, index, :], out_sems.at[part, index]
            ).start()
        return total + terms

    total = lax.fori_loop(0, size_a, second, jnp.zeros((size_b, width), jnp.float32))
    sum_ref[...] = jnp.broadcast_to(jnp.sum(total), sum_ref.shape)

    def finish(index, carry):
        for part in range(2):
            pltpu.make_async_copy(
                staged.at[part, index], out_hbm.at[part, :, index, :], out_sems.at[part, index]
            ).wait()
        return carry

    lax.fori_loop(0, size_a, finish, 0)


def y_stage(spectrum, row_scale, col_scale, row_rate, col_shift, col_mix, norm_factor, devices, height):
    _, count, both_width = spectrum.shape
    width = both_width // 2
    length = devices * count
    size_b = 1 << (length.bit_length() - 1) // 2
    size_a = length // size_b
    blocks = length // height
    rows = height // devices
    low = size_b // rows
    high = devices // low
    index_a = jnp.arange(size_a, dtype=jnp.int32)
    index_b = jnp.arange(size_b, dtype=jnp.int32)
    order_a = (index_a % blocks) * high + index_a // blocks
    cos_a, sin_a = root_table(index_a, order_a, size_a)
    out_rows = size_a * index_b[None, :, None] + index_a[:, None, None]
    phase = index_b[None, None, :] * out_rows % length
    angle = phase.astype(jnp.float32) * (-2.0 * math.pi / length)
    cos_b = jnp.cos(angle)
    sin_b = jnp.sin(angle)
    table_b = jnp.concatenate(
        [jnp.concatenate([cos_b, -sin_b], axis=2), jnp.concatenate([sin_b, cos_b], axis=2)], axis=1
    )
    row_scale_t = row_scale.reshape(size_b, size_a).T.reshape(length, 1)
    row_rate_t = row_rate.reshape(size_b, size_a).T.reshape(length, 1)
    vmem = pl.BlockSpec(memory_space=pltpu.VMEM)
    anywhere = pl.BlockSpec(memory_space=pl.ANY)
    shaped = spectrum.reshape(high, low, blocks, rows, both_width)
    latent, sums = pl.pallas_call(
        functools.partial(y_kernel, norm_factor),
        out_shape=(
            jax.ShapeDtypeStruct((2, size_b, size_a, width), jnp.float32),
            jax.ShapeDtypeStruct((8, 128), jnp.float32),
        ),
        in_specs=[vmem] * 10 + [anywhere],
        out_specs=(anywhere, vmem),
        scratch_shapes=[
            pltpu.VMEM((size_b, 2, high, blocks, width), jnp.float32),
            pltpu.VMEM((2, size_b, size_a, width), jnp.float32),
            pltpu.VMEM((size_a, 2, size_b, width), jnp.float32),
            pltpu.VMEM((2, size_a, size_b, width), jnp.float32),
            pltpu.SemaphoreType.DMA((2, size_b)),
            pltpu.SemaphoreType.DMA((2, size_a)),
            pltpu.SemaphoreType.DMA((2, size_b)),
        ],
        compiler_params=pltpu.CompilerParams(vmem_limit_bytes=60 * 1024 * 1024),
    )(
        cos_a, sin_a, table_b,
        row_scale_t, row_rate_t, jnp.log(row_scale_t), col_scale.reshape(1, width),
        jnp.log(col_scale).reshape(1, width), col_shift.reshape(1, width),
        col_mix.reshape(1, width), shaped,
    )
    return latent.reshape(2, length, width), sums

MESH_IDS = pl.DeviceIdType.MESH


def total_kernel(value_ref, out_ref, slots_a, slots_b, send_a, recv_a, send_b, recv_b):
    count_x = lax.axis_size("gx")
    count_y = lax.axis_size("gy")
    me_x = lax.axis_index("gx")
    me_y = lax.axis_index("gy")
    barrier = pltpu.get_barrier_semaphore()
    for step in range(1, count_x):
        pl.semaphore_signal(
            barrier, inc=1, device_id=((me_x + step) % count_x, me_y), device_id_type=MESH_IDS
        )
    for step in range(1, count_y):
        pl.semaphore_signal(
            barrier, inc=1, device_id=(me_x, (me_y + step) % count_y), device_id_type=MESH_IDS
        )
    slots_a[0] = value_ref[...]
    pl.semaphore_wait(barrier, count_x - 1 + count_y - 1)
    sends = []
    for step in range(1, count_x):
        copy = pltpu.make_async_remote_copy(
            src_ref=value_ref,
            dst_ref=slots_a.at[step],
            send_sem=send_a.at[step],
            recv_sem=recv_a.at[step],
            device_id=((me_x + step) % count_x, me_y),
            device_id_type=MESH_IDS,
        )
        copy.start()
        sends.append(copy)
    for copy in sends:
        copy.wait_recv()
    group_sum = slots_a[(me_x - 0) % count_x]
    for source in range(1, count_x):
        group_sum = group_sum + slots_a[(me_x - source + count_x) % count_x]
    slots_b[0] = group_sum
    later = []
    for step in range(1, count_y):
        copy = pltpu.make_async_remote_copy(
            src_ref=slots_b.at[0],
            dst_ref=slots_b.at[step],
            send_sem=send_b.at[step],
            recv_sem=recv_b.at[step],
            device_id=(me_x, (me_y + step) % count_y),
            device_id_type=MESH_IDS,
        )
        copy.start()
        later.append(copy)
    for copy in later:
        copy.wait_recv()
    grand = slots_b[(me_y - 0) % count_y]
    for source in range(1, count_y):
        grand = grand + slots_b[(me_y - source + count_y) % count_y]
    out_ref[...] = grand
    for copy in sends:
        copy.wait_send()
    for copy in later:
        copy.wait_send()


def total_everywhere(tile):
    count_x = lax.axis_size("gx")
    count_y = lax.axis_size("gy")
    result = pl.pallas_call(
        total_kernel,
        out_shape=jax.ShapeDtypeStruct((8, 128), jnp.float32),
        in_specs=[pl.BlockSpec(memory_space=pltpu.VMEM)],
        out_specs=pl.BlockSpec(memory_space=pltpu.VMEM),
        scratch_shapes=[
            pltpu.VMEM((count_x, 8, 128), jnp.float32),
            pltpu.VMEM((count_y, 8, 128), jnp.float32),
            pltpu.SemaphoreType.DMA((count_x,)),
            pltpu.SemaphoreType.DMA((count_x,)),
            pltpu.SemaphoreType.DMA((count_y,)),
            pltpu.SemaphoreType.DMA((count_y,)),
        ],
        compiler_params=pltpu.CompilerParams(collective_id=0, has_side_effects=True),
    )(tile)
    return result[0, 0]


def per_device(field, row_scale, col_scale, row_rate, col_shift, col_mix):
    devices = lax.axis_size("gx")
    planes, height, width = field.shape
    rows = height // devices
    outgoing = field.reshape(planes * devices, rows, width)
    incoming = lax.all_to_all(outgoing, ("gy", "gx"), split_axis=0, concat_axis=0, tiled=True)
    incoming = incoming.reshape(planes, devices, rows, width)
    both = x_stage(incoming)
    both = lax.all_to_all(both, "gx", split_axis=0, concat_axis=0, tiled=True)
    length = both.shape[0] * both.shape[1]
    total_cols = both.shape[2] // 2 * devices
    norm_factor = 1.0 / math.sqrt(length * total_cols)
    latent, part_sum = y_stage(
        both, row_scale, col_scale, row_rate, col_shift, col_mix, norm_factor, devices, height
    )
    total_sum = total_everywhere(part_sum)
    mode_count = length * total_cols * lax.axis_size("gy")
    loglik = total_sum / mode_count
    return (latent[:, None], loglik)


def solution(mesh):
    return jax.shard_map(
        per_device,
        mesh=mesh,
        in_specs=(P(None, "gy", "gx"), P(), P("gx"), P(), P("gx"), P("gx")),
        out_specs=(P(None, "gy", None, "gx"), P()),
        check_vma=False,
    )
```
